128 devices in a mesh: img: 4 (over y_lo, core), tile: 32 (over x, y_hi, z).
Axes of the slice: x: 4, y: 4 (y_hi: 2, y_lo: 2; y = y_hi * 2 + y_lo), z: 4, core: 2. Of those that a mesh axis runs over, the one named last changes fastest.
Arguments:
- tiles: bfloat16 [32768, 1152], P(('img', 'tile')), may hold values from -6 to 6
- tile_image: int32 [128], P(('img', 'tile')), may hold values from 0 to 1
- guide: bfloat16 [8, 512, 1152], P('img', 'tile'), may hold values from -160 to 160
- gain: float32 [1152], replicated, may hold values from 0.5 to 1.5
- w_query: bfloat16 [1152, 1152], replicated, may hold values from -0.1875 to 0.1875
- w_key: bfloat16 [1152, 1152], replicated, may hold values from -0.1875 to 0.1875
- w_value: bfloat16 [1152, 1152], replicated, may hold values from -0.1875 to 0.1875
- w_out: bfloat16 [1152, 1152], replicated, may hold values from -0.1875 to 0.1875
- grad_out: bfloat16 [32768, 1152], P(('img', 'tile')), may hold values from -24 to 24
Outputs:
- grad_tiles: bfloat16 [32768, 1152], P(('img', 'tile'))
- grad_guide: bfloat16 [8, 512, 1152], P('img', 'tile')
- grad_weights: float32 [4, 1152, 1152], P(None, ('img', 'tile'))
- grad_gain: float32 [1152], replicated
The draws below stay inside these ranges and needn't reach their ends.
Inputs may be any that keep to these rules, and one draw needn't show every extreme that they name: `tile_image`: image of each tile within its own img group of 2 images.
All inputs are finite; a program needn't handle non-finite values.
Results may differ from the reference program's by a relative error of at most 0.034.
The reference program's roundings to bfloat16 on the way count: a program that leaves them out, or rounds other values in their place, can miss the bound.
Values may be sent and summed in bfloat16 or wider, within the bound.
No kernel may reach another device: no remote copies, remote signals or barrier semaphores. Data moves between devices by JAX's collectives and lax.ppermute only.
A program may use at most 128 MiB of HBM per device.

```python
import jax
import jax.numpy as jnp
from jax import lax

D = 1152
HEADS = 16
TILE = 256
IMG_GRP = 2
G = 512
TILES = 128
TOKENS = 32768
IMAGES = 8
N_IMG = 4


def draw_guide(key, part):
    base_key = jax.random.fold_in(key, 11)
    values = jax.random.normal(base_key, (IMAGES, G, D), jnp.float32)
    return jnp.clip(values, -160.0, 160.0).astype(jnp.bfloat16)


def touch_ends(result, stream_key, smallest, top_value):
    spot = [jax.random.randint(jax.random.fold_in(stream_key, axis), (), 0, length) for axis, length in enumerate(result.shape)]
    widest = result.shape.index(max(result.shape))
    next_to = spot[:widest] + [(spot[widest] + 1) % result.shape[widest]] + spot[widest + 1:]
    return result.at[tuple(spot)].set(smallest).at[tuple(next_to)].set(top_value)


def strengthened(result, rng, source, target, shards_of, factor):
    owner, partner = [(jnp.arange(result.shape[axis_at]) // (result.shape[axis_at] // shards_of)).reshape([-1 if axis == axis_at else 1 for axis in range(result.ndim)]) for axis_at in (source, target)]
    chosen = jax.random.permutation(rng, shards_of)[partner]
    strong = (owner == chosen) | (owner == (partner + shards_of // 2) % shards_of)
    return jnp.where(strong, factor * result, result)


def levels(key, shape, shards, least, top_value):
    level, own = 1.0, jax.random.fold_in(key, 6)
    for axis_at, blocks in shards:
        draws = jnp.exp(jax.random.uniform(jax.random.fold_in(own, axis_at), (blocks,), jnp.float32, least / len(shards), top_value / len(shards)))
        level = level * jnp.repeat(draws, shape[axis_at] // blocks).reshape([-1 if axis == axis_at else 1 for axis in range(len(shape))])
    return level


def gaussian(rng, extent, deviation, limit, pieces=(), held_as=jnp.bfloat16):
    level = levels(rng, extent, pieces, -0.22, 0.18) if pieces else 1.0
    values = jax.random.normal(rng, extent, jnp.float32) * deviation * level
    return jnp.minimum(jnp.maximum(values, -limit), limit).astype(held_as)


def gaussian_with(stream_key, dims, deviation, reach, cuts, heavy, kind=jnp.bfloat16):
    result = deviation * jax.random.normal(stream_key, dims, jnp.float32)
    if cuts:
        result = result * levels(stream_key, dims, cuts, -0.22, 0.18)
    return jnp.clip(strengthened(result, jax.random.fold_in(stream_key, 3), *heavy), -reach, reach).astype(kind)


def setup_inputs(seed: int = 0) -> dict:
    key_list = jax.random.split(jax.random.key(seed), 10)
    return {
        "tiles": gaussian(key_list[0], (TOKENS, D), 1.0, 6.0, ((0, 128),)),
        "tile_image": touch_ends(jax.random.randint(key_list[1], (TILES,), 0, IMG_GRP), jax.random.fold_in(key_list[1], 1), 0, IMG_GRP - 1).astype(jnp.int32),
        "guide": draw_guide(jax.random.fold_in(key_list[9], 71), 0),
        "gain": jnp.clip(1.0 + 0.1 * jax.random.normal(key_list[3], (D,), jnp.float32), 0.5, 1.5),
        "w_query": gaussian(key_list[4], (D, D), D ** -0.5, 0.1875),
        "w_key": gaussian(key_list[5], (D, D), D ** -0.5, 0.1875),
        "w_value": gaussian(key_list[6], (D, D), D ** -0.5, 0.1875),
        "w_out": gaussian(key_list[7], (D, D), D ** -0.5, 0.1875),
        "grad_out": gaussian_with(key_list[8], (TOKENS, D), 1.0, 24.0, ((0, 128),), (0, 1, 128, 5.5)),
    }


def tile_pass(q_tile, k_img, v_img, d_tile):
    head_size = D // HEADS
    scale = head_size ** (-0.5)
    qh = q_tile.reshape(TILE, HEADS, head_size).astype(jnp.float32)
    kh = k_img.reshape(G, HEADS, head_size).astype(jnp.float32)
    vh = v_img.reshape(G, HEADS, head_size).astype(jnp.float32)
    dh = d_tile.reshape(TILE, HEADS, head_size).astype(jnp.float32)
    scores = jnp.einsum('qhd,khd->hqk', qh, kh) * scale
    top = lax.optimization_barrier(jnp.max(scores, axis=-1, keepdims=True))
    expo = jnp.exp(scores - top)
    probs = expo / lax.optimization_barrier(jnp.sum(expo, axis=-1, keepdims=True))
    pb = probs.astype(jnp.bfloat16)
    outv = jnp.einsum('hqk,khd->qhd', pb.astype(jnp.float32), vh).astype(jnp.bfloat16)
    dprob = jnp.einsum('qhd,khd->hqk', dh, vh)
    delta = lax.optimization_barrier(jnp.sum(probs * dprob, axis=-1, keepdims=True))
    dscore = (probs * (dprob - delta) * scale).astype(jnp.bfloat16).astype(jnp.float32)
    dq = jnp.einsum('hqk,khd->qhd', dscore, kh).astype(jnp.bfloat16)
    dk = jnp.einsum('hqk,qhd->khd', dscore, qh).reshape(G, D)
    dv = jnp.einsum('hqk,qhd->khd', pb.astype(jnp.float32), dh).reshape(G, D)
    return (outv.reshape(TILE, D), dq.reshape(TILE, D), dk, dv)

def reference(tiles, tile_image, guide, gain, w_query, w_key, w_value, w_out, grad_out):
    xf = tiles.astype(jnp.float32)
    rstd = lax.rsqrt(lax.optimization_barrier(jnp.mean(xf * xf, axis=-1, keepdims=True)) + 1e-06)
    normed = xf * rstd
    hidden = (normed * gain).astype(jnp.bfloat16)
    query = jnp.dot(hidden, w_query, preferred_element_type=jnp.float32).astype(jnp.bfloat16)
    flat = guide.reshape(IMAGES * G, D)
    keys = jnp.dot(flat, w_key, preferred_element_type=jnp.float32).astype(jnp.bfloat16).reshape(IMAGES, G, D)
    values = jnp.dot(flat, w_value, preferred_element_type=jnp.float32).astype(jnp.bfloat16).reshape(IMAGES, G, D)
    dout = jnp.dot(grad_out, w_out.T, preferred_element_type=jnp.float32).astype(jnp.bfloat16)
    group = (jnp.arange(TILES, dtype=jnp.int32) // (TILES // N_IMG)).astype(jnp.int32)
    owner = (group * IMG_GRP + tile_image).astype(jnp.int32)

    def step(carry, item):
        dk_acc, dv_acc = carry
        q_tile, d_tile, image = item
        k_img = lax.dynamic_index_in_dim(keys, image, 0, keepdims=False)
        v_img = lax.dynamic_index_in_dim(values, image, 0, keepdims=False)
        outv, dq, dk, dv = tile_pass(q_tile, k_img, v_img, d_tile)
        old_k = lax.dynamic_index_in_dim(dk_acc, image, 0, keepdims=False)
        old_v = lax.dynamic_index_in_dim(dv_acc, image, 0, keepdims=False)
        dk_acc = lax.dynamic_update_index_in_dim(dk_acc, old_k + dk, image, 0)
        dv_acc = lax.dynamic_update_index_in_dim(dv_acc, old_v + dv, image, 0)
        return ((dk_acc, dv_acc), (outv, dq))
    start = (jnp.zeros((IMAGES, G, D), jnp.float32), jnp.zeros((IMAGES, G, D), jnp.float32))
    (dk_all, dv_all), (outs, dqs) = lax.scan(step, start, (query.reshape(TILES, TILE, D), dout.reshape(TILES, TILE, D), owner))
    outv = outs.reshape(TOKENS, D)
    dq = dqs.reshape(TOKENS, D)
    dkb = dk_all.astype(jnp.bfloat16).reshape(IMAGES * G, D)
    dvb = dv_all.astype(jnp.bfloat16).reshape(IMAGES * G, D)
    grad_guide = (jnp.dot(dkb, w_key.T, preferred_element_type=jnp.float32) + jnp.dot(dvb, w_value.T, preferred_element_type=jnp.float32)).astype(jnp.bfloat16).reshape(IMAGES, G, D)
    grad_weights = jnp.stack([jnp.dot(hidden.T, dq, preferred_element_type=jnp.float32), jnp.dot(flat.T, dkb, preferred_element_type=jnp.float32), jnp.dot(flat.T, dvb, preferred_element_type=jnp.float32), jnp.dot(outv.T, grad_out, preferred_element_type=jnp.float32)])
    dh = jnp.dot(dq, w_query.T, preferred_element_type=jnp.float32)
    grad_gain = lax.optimization_barrier(jnp.sum(dh * normed, axis=0))
    dn = dh * gain
    grad_tiles = (rstd * (dn - normed * lax.optimization_barrier(jnp.mean(dn * normed, axis=-1, keepdims=True)))).astype(jnp.bfloat16)
    return (grad_tiles, grad_guide, grad_weights, grad_gain)
```

```python
import jax
import jax.numpy as jnp
from jax import lax
from jax.experimental import pallas as pl
from jax.experimental.pallas import tpu as pltpu
from jax.sharding import Mesh, PartitionSpec as P

HEADS = 16
HD = 72
HP = 128
D = 1152
G = 512
F32 = jnp.float32
BF16 = jnp.bfloat16
TILE_AXES = ("x", "yh", "z")
CHIP_AXES = ("yl", "x", "yh", "z")
SWAP = [(0, 1), (1, 0)]


def dot(a, b, ca, cb):
    return lax.dot_general(a, b, (((ca,), (cb,)), ((), ())), preferred_element_type=F32)


def spread_heads_kernel(q_ref, d_ref, qo_ref, do_ref):
    for src, dst in ((q_ref, qo_ref), (d_ref, do_ref)):
        dst[...] = jnp.zeros_like(dst)
        for h in range(HEADS):
            dst[:, h * HP : h * HP + HD] = src[:, h * HD : (h + 1) * HD]


def spread_heads(q, d):
    rows = q.shape[0]
    return pl.pallas_call(
        spread_heads_kernel,
        out_shape=[jax.ShapeDtypeStruct((rows, HEADS * HP), BF16)] * 2,
        name="spread_heads",
    )(q, d)


def spread_weights_kernel(k_ref, v_ref, o_ref):
    o_ref[...] = jnp.zeros_like(o_ref)
    for h in range(HEADS):
        o_ref[:, 2 * h * HP : 2 * h * HP + HD] = k_ref[:, h * HD : (h + 1) * HD]
        o_ref[:, (2 * h + 1) * HP : (2 * h + 1) * HP + HD] = v_ref[:, h * HD : (h + 1) * HD]


def spread_weights(w_key, w_value):
    step = 384
    return pl.pallas_call(
        spread_weights_kernel,
        grid=(D // step,),
        in_specs=[pl.BlockSpec((step, D), lambda i: (i, 0))] * 2,
        out_specs=pl.BlockSpec((step, 2 * HEADS * HP), lambda i: (i, 0)),
        out_shape=jax.ShapeDtypeStruct((D, 2 * HEADS * HP), BF16),
        name="spread_weights",
    )(w_key, w_value)


def attention_kernel(img_ref, g_ref, w_ref, q_ref, d_ref, pay_ref, o_ref, dq_ref, o_scr, dq_scr):
    h = pl.program_id(0)
    scale = HD ** (-0.5)
    guide = g_ref[...].reshape(G, D)
    kv = dot(guide, w_ref[...], 1, 0).astype(BF16)
    k, v = kv[:, :HP], kv[:, HP:]
    q, d = q_ref[...], d_ref[...]
    scores = dot(q, k, 1, 1) * scale
    top = jnp.max(scores, axis=-1, keepdims=True)
    expo = jnp.exp(scores - top)
    probs = expo / jnp.sum(expo, axis=-1, keepdims=True)
    pb = probs.astype(BF16)
    o_scr[h] = dot(pb, v, 1, 0).astype(BF16)
    dprob = dot(d, v, 1, 1)
    delta = jnp.sum(probs * dprob, axis=-1, keepdims=True)
    ds = (probs * (dprob - delta) * scale).astype(BF16)
    dq_scr[h] = dot(ds, k, 1, 0).astype(BF16)
    dk = dot(q, ds, 0, 0)
    dv = dot(d, pb, 0, 0)
    flag = jnp.full((4, G), img_ref[0], jnp.int32).astype(F32)
    for i in range(2):
        for j, part in enumerate((dk, dv)):
            rows = jnp.concatenate([part[36 * i : 36 * i + 36], flag], axis=0)
            pay_ref[i, j] = rows.astype(BF16)

    @pl.when(h == HEADS - 1)
    def _():
        for n in range(HEADS):
            o_ref[:, n * HD : (n + 1) * HD] = o_scr[n][:, :HD]
            dq_ref[:, n * HD : (n + 1) * HD] = dq_scr[n][:, :HD]


def attention(img, whole, w_kv, q, d):
    t = q.shape[0]
    grid_spec = pltpu.PrefetchScalarGridSpec(
        num_scalar_prefetch=1,
        grid=(HEADS,),
        in_specs=[
            pl.BlockSpec((32, pl.Squeezed(), 16, D), lambda h, i: (0, i[0], 0, 0)),
            pl.BlockSpec((D, 2 * HP), lambda h, i: (0, h)),
            pl.BlockSpec((t, HP), lambda h, i: (0, h)),
            pl.BlockSpec((t, HP), lambda h, i: (0, h)),
        ],
        out_specs=[
            pl.BlockSpec((2, 2, 40, G), lambda h, i: (h, 0, 0, 0)),
            pl.BlockSpec((t, D), lambda h, i: (0, 0)),
            pl.BlockSpec((t, D), lambda h, i: (0, 0)),
        ],
        scratch_shapes=[pltpu.VMEM((HEADS, t, HP), BF16), pltpu.VMEM((HEADS, t, HP), BF16)],
    )
    return pl.pallas_call(
        attention_kernel,
        grid_spec=grid_spec,
        out_shape=[
            jax.ShapeDtypeStruct((32, 2, 40, G), BF16),
            jax.ShapeDtypeStruct((t, D), BF16),
            jax.ShapeDtypeStruct((t, D), BF16),
        ],
        name="attention",
    )(img, whole, w_kv, q, d)


def pieces(x, n):
    out = []
    for _ in range(n):
        p = lax.reduce_precision(x, 8, 7)
        out.append(p.astype(BF16))
        x = x - p
    return out


def selection(c):
    j = lax.broadcasted_iota(jnp.int32, (D, 576), 1)
    feature = lax.broadcasted_iota(jnp.int32, (D, 576), 0)
    main = j < 512
    dest = jnp.where(main, j // 8, j - 512)
    row = jnp.where(main, j % 8, 8)
    want = (dest // 32) * 576 + c * 288 + (dest % 32) * 9 + row
    return (feature == want).astype(BF16)


def on_device(tiles, tile_image, guide, gain, w_query, w_key, w_value, w_out, grad_out):
    core = lax.axis_index("c")
    yl = lax.axis_index("yl")
    whole = lax.all_to_all(
        jnp.broadcast_to(guide, (32, *guide.shape)), TILE_AXES, 0, 0, tiled=True
    )
    xf = tiles.astype(F32)
    rstd = lax.rsqrt(jnp.mean(xf * xf, axis=-1, keepdims=True) + 1e-06)
    normed = xf * rstd
    hidden = (normed * gain).astype(BF16)
    query = dot(hidden, w_query, 1, 0).astype(BF16)
    dout = dot(grad_out, w_out, 1, 1).astype(BF16)
    q_wide, d_wide = spread_heads(query, dout)
    w_kv = spread_weights(w_key, w_value)
    pick_mine, pick_theirs = selection(core), selection(1 - core)
    hid_mine = dot(hidden, pick_mine, 1, 0).astype(BF16)
    hid_theirs = dot(hidden, pick_theirs, 1, 0).astype(BF16)
    hid_got = lax.ppermute(hid_theirs, "c", SWAP)
    grad_got = lax.ppermute(grad_out, "c", SWAP)

    pay, outv, dq = attention(tile_image, whole, w_kv, q_wide, d_wide)

    dh = dot(dq, w_query, 1, 1)
    gain_part = jnp.sum(dh * normed, axis=0)
    dn = dh * gain
    grad_tiles = (rstd * (dn - normed * jnp.mean(dn * normed, axis=-1, keepdims=True))).astype(BF16)
    gain_rows = jnp.concatenate([p.reshape(32, 36) for p in pieces(gain_part, 3)], axis=1)
    pay = lax.dynamic_update_slice(pay, gain_rows.reshape(32, 1, 1, 108), (0, 0, 37, 0))
    got = lax.all_to_all(pay, TILE_AXES, 0, 0, tiled=True)

    out_mine = dot(outv, pick_mine, 1, 0).astype(BF16)
    out_theirs = dot(outv, pick_theirs, 1, 0).astype(BF16)
    dq_got = lax.ppermute(dq, "c", SWAP)
    out_got = lax.ppermute(out_theirs, "c", SWAP)
    gq = (dot(hid_mine, dq, 0, 0) + dot(hid_got, dq_got, 0, 0)).astype(BF16)
    go = (dot(out_mine, grad_out, 0, 0) + dot(out_got, grad_got, 0, 0)).astype(BF16)

    flags = got[:, :1, 36:37, :1]
    terms = got[:, :, :36].astype(F32)
    dkv = jnp.stack(
        [jnp.sum(jnp.where(flags == m, terms, 0.0), axis=0) for m in (0, 1)]
    ).astype(BF16)
    gain_mine = jnp.sum(got[:, 0, 37, :108].astype(F32), axis=0).reshape(3, 36).sum(0)
    by_image = whole.transpose(1, 0, 2, 3).reshape(2 * G, D)
    gkv = dot(by_image, dkv.transpose(1, 2, 0, 3).reshape(72, 2 * G), 0, 1)
    gkv = gkv.reshape(2, 2, 288, 72)
    kv_mine = lax.dynamic_index_in_dim(gkv, core, 1, keepdims=False)
    kv_theirs = lax.dynamic_index_in_dim(gkv, 1 - core, 1, keepdims=False)
    kv_sum = (kv_mine + lax.ppermute(kv_theirs, "c", SWAP)).reshape(64, 648)
    gain_mine = gain_mine + lax.ppermute(gain_mine, "c", SWAP)
    tokens = dkv.reshape(144, 32, 16).transpose(1, 0, 2).reshape(1, 32, 2304)
    tokens = jnp.broadcast_to(tokens, (2, 32, 2304)).reshape(64, 2304)
    gains = jnp.broadcast_to(jnp.concatenate(pieces(gain_mine, 3))[None], (64, 108))
    misc = jnp.concatenate(
        [gq[512:], go[512:], *pieces(kv_sum, 2), tokens, gains, jnp.zeros((64, 3204), BF16)],
        axis=1,
    )
    send = jnp.concatenate(
        [gq[:512].reshape(64, 8, D), go[:512].reshape(64, 8, D), misc.reshape(64, 8, D)], axis=1
    )
    recv = lax.all_to_all(send, CHIP_AXES, 0, 0, tiled=True)
    main = jnp.sum(recv[:, :16].astype(F32), axis=0).reshape(2, 8, D)
    rest = recv[:, 16:].reshape(64, 9216)
    ninth = jnp.sum(rest[:, :2304].astype(F32), axis=0).reshape(2, 1, D)
    g_qo = jnp.concatenate([main, ninth], axis=1)
    kv = rest[:, 2304:3600].reshape(2, 32, 2, 9, 2, 36).astype(F32).sum((0, 2))
    g_kv = kv.transpose(2, 1, 0, 3).reshape(2, 9, D)
    grad_weights = jnp.concatenate([g_qo[:1], g_kv, g_qo[1:]], axis=0)
    near = lax.dynamic_index_in_dim(rest.reshape(2, 32, 9216), yl, 0, keepdims=False)
    tok = near[:, 3600:5904].reshape(32, 2, 2, 36, 16)
    tok = tok.transpose(2, 1, 4, 0, 3).reshape(2, 32, D)
    grad_guide = (
        (dot(tok[0], w_key, 1, 1) + dot(tok[1], w_value, 1, 1)).astype(BF16).reshape(guide.shape)
    )
    far = rest.reshape(2, 32, 9216)[:, :, 5904:6012].astype(F32)
    grad_gain = far.reshape(2, 32, 3, 36).sum((0, 2)).reshape(D)
    return (grad_tiles, grad_guide, grad_weights, grad_gain)


def solution(mesh):
    fine = Mesh(mesh.devices.reshape(2, 2, 4, 2, 4), ("yl", "c", "x", "yh", "z"))
    every = ("yl", "c", "x", "yh", "z")
    return jax.shard_map(
        on_device,
        mesh=fine,
        in_specs=(
            P(every, None),
            P(every),
            P(("yl", "c"), TILE_AXES, None),
            P(),
            P(),
            P(),
            P(),
            P(),
            P(every, None),
        ),
        out_specs=(
            P(every, None),
            P(("yl", "c"), TILE_AXES, None),
            P(None, every, None),
            P(),
        ),
        check_vma=False,
    )
```

```python
import jax
import jax.numpy as jnp
from jax import lax
from jax.experimental import pallas as pl
from jax.experimental.pallas import tpu as pltpu
from jax.sharding import Mesh, PartitionSpec as P

HEADS = 16
HD = 72
HP = 128
D = 1152
G = 512
F32 = jnp.float32
BF16 = jnp.bfloat16
TILE_AXES = ("x", "yh", "z")
CHIP_AXES = ("yl", "x", "yh", "z")
SWAP = [(0, 1), (1, 0)]
PER_STEP = 2


def dot(a, b, ca, cb):
    return lax.dot_general(a, b, (((ca,), (cb,)), ((), ())), preferred_element_type=F32)


def spread_heads_kernel(q_ref, d_ref, qo_ref, do_ref):
    for src, dst in ((q_ref, qo_ref), (d_ref, do_ref)):
        dst[...] = jnp.zeros_like(dst)
        for h in range(HEADS):
            dst[:, h * HP : h * HP + HD] = src[:, h * HD : (h + 1) * HD]


def spread_heads(q, d):
    rows = q.shape[0]
    return pl.pallas_call(
        spread_heads_kernel,
        out_shape=[jax.ShapeDtypeStruct((rows, HEADS * HP), BF16)] * 2,
        name="spread_heads",
    )(q, d)


def spread_weights_kernel(k_ref, v_ref, o_ref):
    o_ref[...] = jnp.zeros_like(o_ref)
    for h in range(HEADS):
        o_ref[:, 2 * h * HP : 2 * h * HP + HD] = k_ref[:, h * HD : (h + 1) * HD]
        o_ref[:, (2 * h + 1) * HP : (2 * h + 1) * HP + HD] = v_ref[:, h * HD : (h + 1) * HD]


def spread_weights(w_key, w_value):
    step = 384
    return pl.pallas_call(
        spread_weights_kernel,
        grid=(D // step,),
        in_specs=[pl.BlockSpec((step, D), lambda i: (i, 0))] * 2,
        out_specs=pl.BlockSpec((step, 2 * HEADS * HP), lambda i: (i, 0)),
        out_shape=jax.ShapeDtypeStruct((D, 2 * HEADS * HP), BF16),
        name="spread_weights",
    )(w_key, w_value)


def attention_kernel(img_ref, g_ref, w_ref, q_ref, d_ref, pay_ref, o_ref, dq_ref, o_scr, dq_scr):
    step = pl.program_id(0)
    scale = HD ** (-0.5)
    guide = g_ref[...].reshape(G, D)
    kv_all = dot(guide, w_ref[...], 1, 0).astype(BF16)
    flag = jnp.full((4, G), img_ref[0], jnp.int32).astype(F32)
    for n in range(PER_STEP):
        k = kv_all[:, 2 * n * HP : (2 * n + 1) * HP]
        v = kv_all[:, (2 * n + 1) * HP : (2 * n + 2) * HP]
        q, d = q_ref[:, n * HP : (n + 1) * HP], d_ref[:, n * HP : (n + 1) * HP]
        scores = dot(q, k, 1, 1) * scale
        dprob = dot(d, v, 1, 1)
        top = jnp.max(scores, axis=-1, keepdims=True)
        expo = jnp.exp(scores - top)
        probs = expo * (1.0 / jnp.sum(expo, axis=-1, keepdims=True))
        pb = probs.astype(BF16)
        weighted = probs * dprob
        delta = jnp.sum(weighted, axis=-1, keepdims=True)
        ds = ((weighted - probs * delta) * scale).astype(BF16)
        o_scr[step * PER_STEP + n] = dot(pb, v, 1, 0).astype(BF16)
        dq_scr[step * PER_STEP + n] = dot(ds, k, 1, 0).astype(BF16)
        dk = dot(q, ds, 0, 0)
        dv = dot(d, pb, 0, 0)
        for i in range(2):
            for j, part in enumerate((dk, dv)):
                rows = jnp.concatenate([part[36 * i : 36 * i + 36], flag], axis=0)
                pay_ref[2 * n + i, j] = rows.astype(BF16)

    @pl.when(step == HEADS // PER_STEP - 1)
    def _():
        for n in range(HEADS):
            o_ref[:, n * HD : (n + 1) * HD] = o_scr[n][:, :HD]
            dq_ref[:, n * HD : (n + 1) * HD] = dq_scr[n][:, :HD]


def attention(img, whole, w_kv, q, d):
    t = q.shape[0]
    grid_spec = pltpu.PrefetchScalarGridSpec(
        num_scalar_prefetch=1,
        grid=(HEADS // PER_STEP,),
        in_specs=[
            pl.BlockSpec((32, pl.Squeezed(), 16, D), lambda h, i: (0, i[0], 0, 0)),
            pl.BlockSpec((D, 2 * PER_STEP * HP), lambda h, i: (0, h)),
            pl.BlockSpec((t, PER_STEP * HP), lambda h, i: (0, h)),
            pl.BlockSpec((t, PER_STEP * HP), lambda h, i: (0, h)),
        ],
        out_specs=[
            pl.BlockSpec((2 * PER_STEP, 2, 40, G), lambda h, i: (h, 0, 0, 0)),
            pl.BlockSpec((t, D), lambda h, i: (0, 0)),
            pl.BlockSpec((t, D), lambda h, i: (0, 0)),
        ],
        scratch_shapes=[pltpu.VMEM((HEADS, t, HP), BF16), pltpu.VMEM((HEADS, t, HP), BF16)],
    )
    return pl.pallas_call(
        attention_kernel,
        grid_spec=grid_spec,
        out_shape=[
            jax.ShapeDtypeStruct((32, 2, 40, G), BF16),
            jax.ShapeDtypeStruct((t, D), BF16),
            jax.ShapeDtypeStruct((t, D), BF16),
        ],
        name="attention",
    )(img, whole, w_kv, q, d)


RING_AXES = ("x", ("yl", "yh"), "z")
ROWS = 640
THIRD = D // 3


def ring_send(block, axis, distance):
    at = (0, 2, 1, 3) if isinstance(axis, tuple) else (0, 1, 2, 3)
    return lax.ppermute(block, axis, [(at[i], at[(i + distance) % 4]) for i in range(4)])


def wanted_rows(position, core):
    j = jnp.arange(ROWS, dtype=jnp.int32)
    distance = (j // 160, (j % 160) // 40, (j % 40) // 10)
    r = j % 10
    out = []
    for colour in range(3):
        dest = [None] * 3
        for i in range(3):
            axis = (colour + i) % 3
            dest[axis] = (position[axis] + distance[i]) % 4
        x, y, z = dest
        feature = (y % 2) * 576 + core * 288 + (x * 8 + (y // 2) * 4 + z) * 9 + r
        out.append(jnp.where(r < 9, feature, -1))
    return jnp.stack(out)[:, :, None]


def one_hot(want):
    return (want == lax.broadcasted_iota(jnp.int32, (ROWS, D), 1)).astype(BF16)


def weight_parts_kernel(want_ref, hid_ref, o_ref, o2_ref, dq_ref, dq2_ref, g_ref, g2_ref, *outs):
    o = jnp.concatenate([o_ref[...], o2_ref[...]], axis=0)
    dq = jnp.concatenate([dq_ref[...], dq2_ref[...]], axis=0)
    g = jnp.concatenate([g_ref[...], g2_ref[...]], axis=0)
    for n in range(3):
        lanes = slice(n * THIRD, (n + 1) * THIRD)
        o_rows = dot(one_hot(want_ref[n]), o, 1, 1).astype(BF16)
        parts = (dot(hid_ref[n], dq[:, lanes], 1, 0), dot(o_rows, g[:, lanes], 1, 0))
        for m, part in enumerate(parts):
            for i in range(4):
                out = outs[4 * n + i]
                out[:, m * THIRD : (m + 1) * THIRD] = part[160 * i : 160 * i + 160].astype(out.dtype)


def weight_parts(*args):
    shapes = []
    for _ in range(3):
        shapes.append(jax.ShapeDtypeStruct((160, 2 * THIRD), F32))
        shapes += [jax.ShapeDtypeStruct((160, 2 * THIRD), BF16)] * 3
    return pl.pallas_call(weight_parts_kernel, out_shape=shapes, name="weight_parts")(*args)


def sum_split_kernel(*refs):
    rows = refs[12].shape[0]
    for n in range(3):
        total = refs[4 * n][...]
        for i in range(1, 4):
            total = total + refs[4 * n + i][...].astype(F32)
        for i in range(4):
            refs[12 + 4 * n + i][...] = total[rows * i : rows * i + rows]


def sum_split(blocks, rows):
    shape = jax.ShapeDtypeStruct((rows, 2 * THIRD), F32)
    return pl.pallas_call(sum_split_kernel, out_shape=[shape] * 12, name="sum_split")(*blocks)


def exchange(blocks, stage):
    out = []
    for n in range(3):
        axis = RING_AXES[(n + stage) % 3]
        out.append(blocks[4 * n])
        out += [ring_send(blocks[4 * n + i], axis, i) for i in (1, 2, 3)]
    return out


def reduce_weights(parts):
    parts = sum_split(exchange(parts, 0), 40)
    parts = sum_split(exchange(parts, 1), 10)
    parts = exchange(parts, 2)
    sums = [sum(parts[4 * n : 4 * n + 4])[:9].reshape(9, 2, THIRD) for n in range(3)]
    return jnp.concatenate(sums, axis=2).transpose(1, 0, 2)


def pieces(x, n):
    out = []
    for _ in range(n):
        p = lax.reduce_precision(x, 8, 7)
        out.append(p.astype(BF16))
        x = x - p
    return out


def all_sum(x):
    x = x + lax.ppermute(x, "c", SWAP)
    for axes in RING_AXES:
        one, two, three = (ring_send(x, axes, n) for n in (1, 2, 3))
        x = (x + two) + (one + three)
    return x


def on_device(tiles, tile_image, guide, gain, w_query, w_key, w_value, w_out, grad_out):
    core = lax.axis_index("c")
    yl = lax.axis_index("yl")
    whole = lax.all_to_all(
        jnp.broadcast_to(guide, (32, *guide.shape)), TILE_AXES, 0, 0, tiled=True
    )
    xf = tiles.astype(F32)
    rstd = lax.rsqrt(jnp.mean(xf * xf, axis=-1, keepdims=True) + 1e-06)
    normed = xf * rstd
    hidden = (normed * gain).astype(BF16)
    query = dot(hidden, w_query, 1, 0).astype(BF16)
    dout = dot(grad_out, w_out, 1, 1).astype(BF16)
    q_wide, d_wide = spread_heads(query, dout)
    w_kv = spread_weights(w_key, w_value)
    position = (lax.axis_index("x"), 2 * lax.axis_index("yh") + yl, lax.axis_index("z"))
    want = wanted_rows(position, core)
    hid_both = jnp.concatenate([hidden, lax.ppermute(hidden, "c", SWAP)], axis=0)
    hid_rows = jnp.stack([dot(one_hot(want[n]), hid_both, 1, 1).astype(BF16) for n in range(3)])
    grad_got = lax.ppermute(grad_out, "c", SWAP)

    pay, outv, dq = attention(tile_image, whole, w_kv, q_wide, d_wide)

    got = lax.all_to_all(pay, TILE_AXES, 0, 0, tiled=True)

    dq_got = lax.ppermute(dq, "c", SWAP)
    out_got = lax.ppermute(outv, "c", SWAP)
    parts = weight_parts(want, hid_rows, outv, out_got, dq, dq_got, grad_out, grad_got)
    g_qo = reduce_weights(parts)

    dh = dot(dq, w_query, 1, 1)
    grad_gain = all_sum(jnp.sum(dh * normed, axis=0))
    dn = dh * gain
    grad_tiles = (rstd * (dn - normed * jnp.mean(dn * normed, axis=-1, keepdims=True))).astype(BF16)

    flags = got[:, :1, 36:37, :1]
    terms = got[:, :, :36].astype(F32)
    dkv = jnp.stack(
        [jnp.sum(jnp.where(flags == m, terms, 0.0), axis=0) for m in (0, 1)]
    ).astype(BF16)
    by_image = whole.transpose(1, 0, 2, 3).reshape(2 * G, D)
    gkv = dot(by_image, dkv.transpose(1, 2, 0, 3).reshape(72, 2 * G), 0, 1)
    gkv = gkv.reshape(2, 2, 288, 72)
    kv_mine = lax.dynamic_index_in_dim(gkv, core, 1, keepdims=False)
    kv_theirs = lax.dynamic_index_in_dim(gkv, 1 - core, 1, keepdims=False)
    kv_sum = (kv_mine + lax.ppermute(kv_theirs, "c", SWAP)).reshape(64, 648)
    tokens = dkv.reshape(144, 32, 16).transpose(1, 0, 2).reshape(1, 32, 2304)
    tokens = jnp.broadcast_to(tokens, (2, 32, 2304)).reshape(64, 2304)
    misc = jnp.concatenate([*pieces(kv_sum, 2), tokens, jnp.zeros((64, 496), BF16)], axis=1)
    rest = lax.all_to_all(misc.reshape(64, 8, 512), CHIP_AXES, 0, 0, tiled=True).reshape(64, 4096)
    kv = rest[:, :1296].reshape(2, 32, 2, 9, 2, 36).astype(F32).sum((0, 2))
    g_kv = kv.transpose(2, 1, 0, 3).reshape(2, 9, D)
    near = lax.dynamic_index_in_dim(rest.reshape(2, 32, 4096), yl, 0, keepdims=False)
    tok = near[:, 1296:3600].reshape(32, 2, 2, 36, 16)
    tok = tok.transpose(2, 1, 4, 0, 3).reshape(2, 32, D)
    grad_guide = (
        (dot(tok[0], w_key, 1, 1) + dot(tok[1], w_value, 1, 1)).astype(BF16).reshape(guide.shape)
    )
    grad_weights = jnp.concatenate([g_qo[:1], g_kv, g_qo[1:]], axis=0)
    return (grad_tiles, grad_guide, grad_weights, grad_gain)


def solution(mesh):
    fine = Mesh(mesh.devices.reshape(2, 2, 4, 2, 4), ("yl", "c", "x", "yh", "z"))
    every = ("yl", "c", "x", "yh", "z")
    return jax.shard_map(
        on_device,
        mesh=fine,
        in_specs=(
            P(every, None),
            P(every),
            P(("yl", "c"), TILE_AXES, None),
            P(),
            P(),
            P(),
            P(),
            P(),
            P(every, None),
        ),
        out_specs=(
            P(every, None),
            P(("yl", "c"), TILE_AXES, None),
            P(None, every, None),
            P(),
        ),
        check_vma=False,
    )
```

```python
import jax
import jax.numpy as jnp
from jax import lax
from jax.experimental import pallas as pl
from jax.experimental.pallas import tpu as pltpu
from jax.sharding import Mesh, PartitionSpec as P

HEADS = 16
HD = 72
HP = 128
D = 1152
G = 512
F32 = jnp.float32
BF16 = jnp.bfloat16
TILE_AXES = ("x", "yh", "z")
CHIP_AXES = ("yl", "x", "yh", "z")
SWAP = [(0, 1), (1, 0)]
PER_STEP = 2


def dot(a, b, ca, cb):
    return lax.dot_general(a, b, (((ca,), (cb,)), ((), ())), preferred_element_type=F32)


def spread_heads_kernel(q_ref, d_ref, qo_ref, do_ref):
    for src, dst in ((q_ref, qo_ref), (d_ref, do_ref)):
        dst[...] = jnp.zeros_like(dst)
        for h in range(HEADS):
            dst[:, h * HP : h * HP + HD] = src[:, h * HD : (h + 1) * HD]


def spread_heads(q, d):
    rows = q.shape[0]
    return pl.pallas_call(
        spread_heads_kernel,
        out_shape=[jax.ShapeDtypeStruct((rows, HEADS * HP), BF16)] * 2,
        name="spread_heads",
    )(q, d)


def spread_weights_kernel(k_ref, v_ref, o_ref):
    o_ref[...] = jnp.zeros_like(o_ref)
    for h in range(HEADS):
        o_ref[:, 2 * h * HP : 2 * h * HP + HD] = k_ref[:, h * HD : (h + 1) * HD]
        o_ref[:, (2 * h + 1) * HP : (2 * h + 1) * HP + HD] = v_ref[:, h * HD : (h + 1) * HD]


def spread_weights(w_key, w_value):
    step = 128
    return pl.pallas_call(
        spread_weights_kernel,
        grid=(D // step,),
        in_specs=[pl.BlockSpec((step, D), lambda i: (i, 0))] * 2,
        out_specs=pl.BlockSpec((step, 2 * HEADS * HP), lambda i: (i, 0)),
        out_shape=jax.ShapeDtypeStruct((D, 2 * HEADS * HP), BF16),
        name="spread_weights",
    )(w_key, w_value)


def attention_kernel(img_ref, g_ref, w_ref, q_ref, d_ref, pay_ref, o_ref, dq_ref, o_scr, dq_scr):
    step = pl.program_id(0)
    scale = HD ** (-0.5)
    guide = g_ref[...].reshape(G, D)
    kv_all = dot(guide, w_ref[...], 1, 0).astype(BF16)
    flag = jnp.full((4, G), img_ref[0], jnp.int32).astype(F32)
    for n in range(PER_STEP):
        k = kv_all[:, 2 * n * HP : (2 * n + 1) * HP]
        v = kv_all[:, (2 * n + 1) * HP : (2 * n + 2) * HP]
        q, d = q_ref[:, n * HP : (n + 1) * HP], d_ref[:, n * HP : (n + 1) * HP]
        scores = dot(q, k, 1, 1) * scale
        dprob = dot(d, v, 1, 1)
        top = jnp.max(scores, axis=-1, keepdims=True)
        expo = jnp.exp(scores - top)
        probs = expo * (1.0 / jnp.sum(expo, axis=-1, keepdims=True))
        pb = probs.astype(BF16)
        weighted = probs * dprob
        delta = jnp.sum(weighted, axis=-1, keepdims=True)
        ds = ((weighted - probs * delta) * scale).astype(BF16)
        o_scr[step * PER_STEP + n] = dot(pb, v, 1, 0).astype(BF16)
        dq_scr[step * PER_STEP + n] = dot(ds, k, 1, 0).astype(BF16)
        dk = dot(q, ds, 0, 0)
        dv = dot(d, pb, 0, 0)
        for i in range(2):
            for j, part in enumerate((dk, dv)):
                rows = jnp.concatenate([part[36 * i : 36 * i + 36], flag], axis=0)
                pay_ref[2 * n + i, j] = rows.astype(BF16)

    @pl.when(step == HEADS // PER_STEP - 1)
    def _():
        for n in range(HEADS):
            o_ref[:, n * HD : (n + 1) * HD] = o_scr[n][:, :HD]
            dq_ref[:, n * HD : (n + 1) * HD] = dq_scr[n][:, :HD]


def attention(img, whole, w_kv, q, d):
    t = q.shape[0]
    grid_spec = pltpu.PrefetchScalarGridSpec(
        num_scalar_prefetch=1,
        grid=(HEADS // PER_STEP,),
        in_specs=[
            pl.BlockSpec((32, pl.Squeezed(), 16, D), lambda h, i: (0, i[0], 0, 0)),
            pl.BlockSpec((D, 2 * PER_STEP * HP), lambda h, i: (0, h)),
            pl.BlockSpec((t, PER_STEP * HP), lambda h, i: (0, h)),
            pl.BlockSpec((t, PER_STEP * HP), lambda h, i: (0, h)),
        ],
        out_specs=[
            pl.BlockSpec((2 * PER_STEP, 2, 40, G), lambda h, i: (h, 0, 0, 0)),
            pl.BlockSpec((t, D), lambda h, i: (0, 0)),
            pl.BlockSpec((t, D), lambda h, i: (0, 0)),
        ],
        scratch_shapes=[pltpu.VMEM((HEADS, t, HP), BF16), pltpu.VMEM((HEADS, t, HP), BF16)],
    )
    return pl.pallas_call(
        attention_kernel,
        grid_spec=grid_spec,
        out_shape=[
            jax.ShapeDtypeStruct((32, 2, 40, G), BF16),
            jax.ShapeDtypeStruct((t, D), BF16),
            jax.ShapeDtypeStruct((t, D), BF16),
        ],
        name="attention",
    )(img, whole, w_kv, q, d)


RING_AXES = ("x", ("yl", "yh"), "z")
ROWS = 576


def ring_send(block, axis, distance):
    at = (0, 2, 1, 3) if isinstance(axis, tuple) else (0, 1, 2, 3)
    return lax.ppermute(block, axis, [(at[i], at[(i + distance) % 4]) for i in range(4)])


def eight_and_one(rows):
    return jnp.where(rows < 512, rows // 8 * 9 + rows % 8, (rows - 512) * 9 + 8)


def wanted_rows(core):
    row = eight_and_one(jnp.arange(ROWS, dtype=jnp.int32))
    return (row // 288 * 576 + core * 288 + row % 288)[:, None]


def one_hot(want, width):
    return (want == lax.broadcasted_iota(jnp.int32, (want.shape[0], width), 1)).astype(BF16)


def weight_parts_kernel(
    want_ref, hid_ref, o_ref, o2_ref, dq_ref, dq2_ref, g_ref, g2_ref, send_ref, ninth_ref
):
    o = jnp.concatenate([o_ref[...], o2_ref[...]], axis=0)
    dq = jnp.concatenate([dq_ref[...], dq2_ref[...]], axis=0)
    g = jnp.concatenate([g_ref[...], g2_ref[...]], axis=0)
    o_rows = dot(one_hot(want_ref[...], D), o, 1, 1).astype(BF16)
    parts = (dot(hid_ref[...], dq, 1, 0), dot(o_rows, g, 1, 0))
    for m, part in enumerate(parts):
        send_ref[:, m] = part[:512].reshape(64, 8, D).astype(BF16)
        ninth_ref[:, m * D : (m + 1) * D] = part[512:]


def weight_parts(*args):
    vmem = pl.BlockSpec(memory_space=pltpu.VMEM)
    return pl.pallas_call(
        weight_parts_kernel,
        grid=(1,),
        in_specs=[vmem] * 8,
        out_specs=[
            pl.BlockSpec((64, 2, 8, D), lambda i: (0, 0, 0, 0)),
            pl.BlockSpec((64, 2 * D), lambda i: (0, 0)),
        ],
        out_shape=[
            jax.ShapeDtypeStruct((64, 3, 8, D), BF16),
            jax.ShapeDtypeStruct((64, 2 * D), F32),
        ],
        name="weight_parts",
    )(*args)


def image_sums_kernel(core_ref, got_ref, g_ref, mine_ref, theirs_ref, tok_ref, scr):
    def add(s, sums):
        terms = got_ref[s].astype(F32)
        first = terms[:, 36:37, :] == 0.0
        zero = jnp.zeros_like(terms)
        return sums[0] + jnp.where(first, terms, zero), sums[1] + jnp.where(first, zero, terms)

    zero = jnp.zeros((2, 40, G), F32)
    sums = lax.fori_loop(0, 32, add, (zero, zero))
    rounded = [x.reshape(80, G).astype(BF16) for x in sums]
    prod = dot(rounded[0], g_ref[:, 0].reshape(G, D), 1, 0)
    prod = prod + dot(rounded[1], g_ref[:, 1].reshape(G, D), 1, 0)
    scr[...] = jnp.concatenate([prod, jnp.zeros((48, D), F32)], axis=0).T
    core = core_ref[0]
    for n in range(2):
        for out, c in ((mine_ref, core), (theirs_ref, 1 - core)):
            start = pl.multiple_of(n * 576 + c * 288, 32)
            out[n * 288 : n * 288 + 288] = scr[pl.ds(start, 288), :]
    both = jnp.concatenate([x.astype(F32) for x in rounded] + [jnp.zeros((96, G), F32)], axis=0)
    tok_ref[...] = both.T


def image_sums(core, got, whole):
    vmem = pl.BlockSpec(memory_space=pltpu.VMEM)
    return pl.pallas_call(
        image_sums_kernel,
        in_specs=[pl.BlockSpec(memory_space=pltpu.SMEM), vmem, vmem],
        out_specs=[vmem] * 3,
        out_shape=[
            jax.ShapeDtypeStruct((ROWS, 128), F32),
            jax.ShapeDtypeStruct((ROWS, 128), F32),
            jax.ShapeDtypeStruct((G, 256), F32),
        ],
        scratch_shapes=[pltpu.VMEM((D, 128), F32)],
        name="image_sums",
    )(core, got, whole)


SLOTS = [(r, 256) for r in range(1, 8)] + [(r, 384) for r in range(1, 8)]
SLOTS += [(r, 1024) for r in range(4)]


def fill_rest_kernel(send_ref, mine_ref, got_ref, tok_ref, ninth_ref, out_ref, scr):
    scr[...] = jnp.zeros_like(scr)
    total = mine_ref[...] + got_ref[...]
    high = total.astype(BF16)
    low = (total - high.astype(F32)).astype(BF16)
    want = eight_and_one(lax.broadcasted_iota(jnp.int32, (ROWS, ROWS), 0))
    order = (want == lax.broadcasted_iota(jnp.int32, (ROWS, ROWS), 1)).astype(BF16)
    moved = dot(order, jnp.concatenate([high, low], axis=1), 1, 0)
    scr[:, :, :256] = moved[:512].reshape(64, 8, 256)
    scr[:, 0, 256:512] = moved[512:]
    tok = tok_ref[...].reshape(32, 16, 256)
    for n in range(2):
        scr[32 * n : 32 * n + 32, :, 512:768] = tok[:, :8]
        scr[32 * n : 32 * n + 32, :, 768:1024] = tok[:, 8:]
    for b, (row, lane) in enumerate(SLOTS):
        scr[:, row, lane : lane + 128] = ninth_ref[:, 128 * b : 128 * b + 128]
    out_ref[:, 0] = scr[...].astype(BF16)


def fill_rest(send, mine, got, tok, ninth):
    vmem = pl.BlockSpec(memory_space=pltpu.VMEM)
    return pl.pallas_call(
        fill_rest_kernel,
        grid=(1,),
        in_specs=[pl.BlockSpec(memory_space=pl.ANY)] + [vmem] * 4,
        out_specs=pl.BlockSpec((64, 1, 8, D), lambda i: (0, 2, 0, 0)),
        out_shape=jax.ShapeDtypeStruct((64, 3, 8, D), BF16),
        scratch_shapes=[pltpu.VMEM((64, 8, D), F32)],
        input_output_aliases={0: 0},
        name="fill_rest",
    )(send, mine, got, tok, ninth)


def finish_kernel(yl_ref, recv_ref, wk_ref, wv_ref, gw_ref, gg_ref, scr):
    def add(j, sums):
        return tuple(s + recv_ref[j, n].astype(F32) for n, s in enumerate(sums))

    sums = lax.fori_loop(0, 64, add, tuple(jnp.zeros((8, D), F32) for _ in range(3)))
    gw_ref[0, :8] = sums[0]
    gw_ref[3, :8] = sums[1]
    for b, (row, lane) in enumerate(SLOTS):
        at = 128 * (b % 9)
        gw_ref[3 * (b // 9), 8:9, at : at + 128] = sums[2][row : row + 1, lane : lane + 128]
    base = yl_ref[0] * 32
    for t in range(32):
        cols = slice(36 * t, 36 * t + 36)
        x = recv_ref[t, 2, :, :512].astype(F32) + recv_ref[32 + t, 2, :, :512].astype(F32)
        eight = x[:, :128] + x[:, 128:256]
        one = x[:1, 256:384] + x[:1, 384:512]
        for n in range(2):
            gw_ref[1 + n, :8, cols] = eight[:, 40 * n : 40 * n + 36]
            gw_ref[1 + n, 8:9, cols] = one[:, 40 * n : 40 * n + 36]
        near = recv_ref[base + t, 2, :, 512:1024].astype(F32)
        for half in range(2):
            for m in range(2):
                for n in range(2):
                    lane = 256 * half + 80 * m + 40 * n
                    row = 16 * m + 8 * half
                    scr[n, row : row + 8, cols] = near[:, lane : lane + 36]
    grad = dot(scr[0].astype(BF16), wk_ref[...], 1, 1) + dot(scr[1].astype(BF16), wv_ref[...], 1, 1)
    gg_ref[...] = grad.astype(BF16)


def finish(yl, recv, w_key, w_value):
    vmem = pl.BlockSpec(memory_space=pltpu.VMEM)
    return pl.pallas_call(
        finish_kernel,
        in_specs=[pl.BlockSpec(memory_space=pltpu.SMEM), vmem, vmem, vmem],
        out_specs=[vmem] * 2,
        out_shape=[jax.ShapeDtypeStruct((4, 9, D), F32), jax.ShapeDtypeStruct((32, D), BF16)],
        scratch_shapes=[pltpu.VMEM((2, 32, D), F32)],
        name="finish",
    )(yl, recv, w_key, w_value)


def all_sum(x):
    x = x + lax.ppermute(x, "c", SWAP)
    for axes in RING_AXES:
        one, two, three = (ring_send(x, axes, n) for n in (1, 2, 3))
        x = (x + two) + (one + three)
    return x


def on_device(tiles, tile_image, guide, gain, w_query, w_key, w_value, w_out, grad_out):
    core = lax.axis_index("c")
    yl = lax.axis_index("yl")
    whole = lax.all_to_all(
        jnp.broadcast_to(guide, (32, *guide.shape)), TILE_AXES, 0, 0, tiled=True
    )
    xf = tiles.astype(F32)
    rstd = lax.rsqrt(jnp.mean(xf * xf, axis=-1, keepdims=True) + 1e-06)
    normed = xf * rstd
    hidden = (normed * gain).astype(BF16)
    query = dot(hidden, w_query, 1, 0).astype(BF16)
    dout = dot(grad_out, w_out, 1, 1).astype(BF16)
    q_wide, d_wide = spread_heads(query, dout)
    w_kv = spread_weights(w_key, w_value)
    want = wanted_rows(core)
    hid_both = jnp.concatenate([hidden, lax.ppermute(hidden, "c", SWAP)], axis=0)
    hid_rows = dot(one_hot(want, D), hid_both, 1, 1).astype(BF16)
    grad_got = lax.ppermute(grad_out, "c", SWAP)
    q_wide, hid_rows = lax.optimization_barrier((q_wide, hid_rows))

    pay, outv, dq = attention(tile_image, whole, w_kv, q_wide, d_wide)
    got = lax.all_to_all(pay, TILE_AXES, 0, 0, tiled=True)

    dq_got = lax.ppermute(dq, "c", SWAP)
    out_got = lax.ppermute(outv, "c", SWAP)
    send, ninth = weight_parts(want, hid_rows, outv, out_got, dq, dq_got, grad_out, grad_got)
    dh = dot(dq, w_query, 1, 1)
    gain_part = jnp.sum(dh * normed, axis=0)
    dn = dh * gain
    grad_tiles = (rstd * (dn - normed * jnp.mean(dn * normed, axis=-1, keepdims=True))).astype(BF16)

    got, ninth, gain_part = lax.optimization_barrier((got, ninth, gain_part))
    mine, theirs, tok = image_sums(core[None], got, whole)
    send = fill_rest(send, mine, lax.ppermute(theirs, "c", SWAP), tok, ninth)
    send, gain_part = lax.optimization_barrier((send, gain_part))
    recv = lax.all_to_all(send, CHIP_AXES, 0, 0, tiled=True)
    grad_gain = all_sum(gain_part)
    grad_weights, grad_guide = finish(yl[None], recv, w_key, w_value)
    return (grad_tiles, grad_guide.reshape(guide.shape), grad_weights, grad_gain)


def solution(mesh):
    fine = Mesh(mesh.devices.reshape(2, 2, 4, 2, 4), ("yl", "c", "x", "yh", "z"))
    every = ("yl", "c", "x", "yh", "z")
    return jax.shard_map(
        on_device,
        mesh=fine,
        in_specs=(
            P(every, None),
            P(every),
            P(("yl", "c"), TILE_AXES, None),
            P(),
            P(),
            P(),
            P(),
            P(),
            P(every, None),
        ),
        out_specs=(
            P(every, None),
            P(("yl", "c"), TILE_AXES, None),
            P(None, every, None),
            P(),
        ),
        check_vma=False,
    )
```

```python
import jax
import jax.numpy as jnp
from jax import lax
from jax.experimental import pallas as pl
from jax.experimental.pallas import tpu as pltpu
from jax.sharding import Mesh, PartitionSpec as P

HEADS = 16
HD = 72
HP = 128
D = 1152
G = 512
F32 = jnp.float32
BF16 = jnp.bfloat16
TILE_AXES = ("x", "yh", "z")
CHIP_AXES = ("yl", "x", "yh", "z")
SWAP = [(0, 1), (1, 0)]
PER_STEP = 4


def dot(a, b, ca, cb):
    return lax.dot_general(a, b, (((ca,), (cb,)), ((), ())), preferred_element_type=F32)


def spread_heads_kernel(q_ref, d_ref, qo_ref, do_ref):
    for src, dst in ((q_ref, qo_ref), (d_ref, do_ref)):
        dst[...] = jnp.zeros_like(dst)
        for h in range(HEADS):
            dst[:, h * HP : h * HP + HD] = src[:, h * HD : (h + 1) * HD]


def spread_heads(q, d):
    rows = q.shape[0]
    return pl.pallas_call(
        spread_heads_kernel,
        out_shape=[jax.ShapeDtypeStruct((rows, HEADS * HP), BF16)] * 2,
        name="spread_heads",
    )(q, d)


def spread_weights_kernel(k_ref, v_ref, o_ref):
    o_ref[...] = jnp.zeros_like(o_ref)
    for h in range(HEADS):
        o_ref[:, 2 * h * HP : 2 * h * HP + HD] = k_ref[:, h * HD : (h + 1) * HD]
        o_ref[:, (2 * h + 1) * HP : (2 * h + 1) * HP + HD] = v_ref[:, h * HD : (h + 1) * HD]


def spread_weights(w_key, w_value):
    step = 384
    return pl.pallas_call(
        spread_weights_kernel,
        grid=(D // step,),
        in_specs=[pl.BlockSpec((step, D), lambda i: (i, 0))] * 2,
        out_specs=pl.BlockSpec((step, 2 * HEADS * HP), lambda i: (i, 0)),
        out_shape=jax.ShapeDtypeStruct((D, 2 * HEADS * HP), BF16),
        name="spread_weights",
    )(w_key, w_value)


def attention_kernel(img_ref, g_ref, w_ref, q_ref, d_ref, pay_ref, o_ref, dq_ref, o_scr, dq_scr):
    step = pl.program_id(0)
    scale = HD ** (-0.5)
    guide = g_ref[...].reshape(G, D)
    kv_all = dot(guide, w_ref[...], 1, 0).astype(BF16)
    flag = jnp.full((4, G), img_ref[0], jnp.int32).astype(F32)
    for n in range(PER_STEP):
        k = kv_all[:, 2 * n * HP : (2 * n + 1) * HP]
        v = kv_all[:, (2 * n + 1) * HP : (2 * n + 2) * HP]
        q, d = q_ref[:, n * HP : (n + 1) * HP], d_ref[:, n * HP : (n + 1) * HP]
        scores = dot(q, k, 1, 1) * scale
        dprob = dot(d, v, 1, 1)
        top = jnp.max(scores, axis=-1, keepdims=True)
        expo = jnp.exp(scores - top)
        probs = expo * (1.0 / jnp.sum(expo, axis=-1, keepdims=True))
        pb = probs.astype(BF16)
        weighted = probs * dprob
        delta = jnp.sum(weighted, axis=-1, keepdims=True)
        ds = ((weighted - probs * delta) * scale).astype(BF16)
        o_scr[step * PER_STEP + n] = dot(pb, v, 1, 0).astype(BF16)
        dq_scr[step * PER_STEP + n] = dot(ds, k, 1, 0).astype(BF16)
        dk = dot(q, ds, 0, 0)
        dv = dot(d, pb, 0, 0)
        for i in range(2):
            for j, part in enumerate((dk, dv)):
                rows = jnp.concatenate([part[36 * i : 36 * i + 36], flag], axis=0)
                pay_ref[2 * n + i, j] = rows.astype(BF16)

    @pl.when(step == HEADS // PER_STEP - 1)
    def _():
        for n in range(HEADS):
            o_ref[:, n * HD : (n + 1) * HD] = o_scr[n][:, :HD]
            dq_ref[:, n * HD : (n + 1) * HD] = dq_scr[n][:, :HD]


def attention(img, whole, w_kv, q, d):
    t = q.shape[0]
    grid_spec = pltpu.PrefetchScalarGridSpec(
        num_scalar_prefetch=1,
        grid=(HEADS // PER_STEP,),
        in_specs=[
            pl.BlockSpec((32, pl.Squeezed(), 16, D), lambda h, i: (0, i[0], 0, 0)),
            pl.BlockSpec((D, 2 * PER_STEP * HP), lambda h, i: (0, h)),
            pl.BlockSpec((t, PER_STEP * HP), lambda h, i: (0, h)),
            pl.BlockSpec((t, PER_STEP * HP), lambda h, i: (0, h)),
        ],
        out_specs=[
            pl.BlockSpec((2 * PER_STEP, 2, 40, G), lambda h, i: (h, 0, 0, 0)),
            pl.BlockSpec((t, D), lambda h, i: (0, 0)),
            pl.BlockSpec((t, D), lambda h, i: (0, 0)),
        ],
        scratch_shapes=[pltpu.VMEM((HEADS, t, HP), BF16), pltpu.VMEM((HEADS, t, HP), BF16)],
    )
    return pl.pallas_call(
        attention_kernel,
        grid_spec=grid_spec,
        out_shape=[
            jax.ShapeDtypeStruct((32, 2, 40, G), BF16),
            jax.ShapeDtypeStruct((t, D), BF16),
            jax.ShapeDtypeStruct((t, D), BF16),
        ],
        name="attention",
    )(img, whole, w_kv, q, d)


ROWS = 576


def eight_and_one(rows):
    return jnp.where(rows < 512, rows // 8 * 9 + rows % 8, (rows - 512) * 9 + 8)


def wanted_rows(core):
    row = eight_and_one(jnp.arange(ROWS, dtype=jnp.int32))
    return (row // 288 * 576 + core * 288 + row % 288)[:, None]


def one_hot(want, width):
    return (want == lax.broadcasted_iota(jnp.int32, (want.shape[0], width), 1)).astype(BF16)


def weight_parts_kernel(
    want_ref, hid_ref, o_ref, o2_ref, dq_ref, dq2_ref, g_ref, g2_ref, send_ref, ninth_ref
):
    o = jnp.concatenate([o_ref[...], o2_ref[...]], axis=0)
    dq = jnp.concatenate([dq_ref[...], dq2_ref[...]], axis=0)
    g = jnp.concatenate([g_ref[...], g2_ref[...]], axis=0)
    o_rows = dot(one_hot(want_ref[...], D), o, 1, 1).astype(BF16)
    parts = (dot(hid_ref[...], dq, 1, 0), dot(o_rows, g, 1, 0))
    for m, part in enumerate(parts):
        send_ref[:, m] = part[:512].reshape(64, 8, D).astype(BF16)
        ninth_ref[:, m * D : (m + 1) * D] = part[512:]


def weight_parts(*args):
    vmem = pl.BlockSpec(memory_space=pltpu.VMEM)
    return pl.pallas_call(
        weight_parts_kernel,
        grid=(1,),
        in_specs=[vmem] * 8,
        out_specs=[
            pl.BlockSpec((64, 2, 8, D), lambda i: (0, 0, 0, 0)),
            pl.BlockSpec((64, 2 * D), lambda i: (0, 0)),
        ],
        out_shape=[
            jax.ShapeDtypeStruct((64, 3, 8, D), BF16),
            jax.ShapeDtypeStruct((64, 2 * D), F32),
        ],
        name="weight_parts",
    )(*args)


def image_sums_kernel(core_ref, got_ref, g_ref, mine_ref, theirs_ref, tok_ref, scr):
    def add(s, sums):
        terms = got_ref[s].astype(F32)
        first = terms[:, 36:37, :] == 0.0
        zero = jnp.zeros_like(terms)
        return sums[0] + jnp.where(first, terms, zero), sums[1] + jnp.where(first, zero, terms)

    zero = jnp.zeros((2, 40, G), F32)
    sums = lax.fori_loop(0, 32, add, (zero, zero))
    rounded = [x.reshape(80, G).astype(BF16) for x in sums]
    prod = dot(rounded[0], g_ref[:, 0].reshape(G, D), 1, 0)
    prod = prod + dot(rounded[1], g_ref[:, 1].reshape(G, D), 1, 0)
    scr[...] = jnp.concatenate([prod, jnp.zeros((48, D), F32)], axis=0).T
    core = core_ref[0]
    for n in range(2):
        for out, c in ((mine_ref, core), (theirs_ref, 1 - core)):
            start = pl.multiple_of(n * 576 + c * 288, 32)
            out[n * 288 : n * 288 + 288] = scr[pl.ds(start, 288), :]
    both = jnp.concatenate([x.astype(F32) for x in rounded] + [jnp.zeros((96, G), F32)], axis=0)
    tok_ref[...] = both.T


def image_sums(core, got, whole):
    vmem = pl.BlockSpec(memory_space=pltpu.VMEM)
    return pl.pallas_call(
        image_sums_kernel,
        in_specs=[pl.BlockSpec(memory_space=pltpu.SMEM), vmem, vmem],
        out_specs=[vmem] * 3,
        out_shape=[
            jax.ShapeDtypeStruct((ROWS, 128), F32),
            jax.ShapeDtypeStruct((ROWS, 128), F32),
            jax.ShapeDtypeStruct((G, 256), F32),
        ],
        scratch_shapes=[pltpu.VMEM((D, 128), F32)],
        name="image_sums",
    )(core, got, whole)


SLOTS = [(row, lane) for lane in range(512, D, 128) for row in range(8)]


def fill_rest_kernel(send_ref, mine_ref, got_ref, tok_ref, ninth_ref, gain_ref, out_ref, scr):
    scr[:, :, 384:512] = jnp.zeros((64, 8, 128), F32)
    total = mine_ref[...] + got_ref[...]
    high = total.astype(BF16)
    low = (total - high.astype(F32)).astype(BF16)
    want = eight_and_one(lax.broadcasted_iota(jnp.int32, (ROWS, ROWS), 0))
    order = (want == lax.broadcasted_iota(jnp.int32, (ROWS, ROWS), 1)).astype(BF16)
    moved = [dot(order, x, 1, 0) for x in (high, low)]
    tok = tok_ref[...].reshape(32, 16, 256)
    for n in range(2):
        scr[:, :, 80 * n : 80 * n + 80] = moved[n][:512].reshape(64, 8, 128)[:, :, :80]
        for half in range(2):
            lanes = slice(160 * half + 160, 160 * half + 320)
            scr[32 * n : 32 * n + 32, :, lanes] = tok[:, 8 * half : 8 * half + 8, :160]
    gain = gain_ref[...]
    gain_high = gain.astype(BF16).astype(F32)
    gains = jnp.concatenate([gain_high, gain - gain_high], axis=1)
    for b, (row, lane) in enumerate(SLOTS):
        if b < 18:
            block = ninth_ref[:, 128 * b : 128 * b + 128]
        elif b < 20:
            block = moved[b - 18][512:]
        elif b < 38:
            block = jnp.broadcast_to(gains[:, 128 * (b - 20) : 128 * (b - 20) + 128], (64, 128))
        else:
            block = jnp.zeros((64, 128), F32)
        scr[:, row, lane : lane + 128] = block
    out_ref[:, 0] = scr[...].astype(BF16)


def fill_rest(send, mine, got, tok, ninth, gain):
    vmem = pl.BlockSpec(memory_space=pltpu.VMEM)
    return pl.pallas_call(
        fill_rest_kernel,
        grid=(1,),
        in_specs=[pl.BlockSpec(memory_space=pl.ANY)] + [vmem] * 5,
        out_specs=pl.BlockSpec((64, 1, 8, D), lambda i: (0, 2, 0, 0)),
        out_shape=jax.ShapeDtypeStruct((64, 3, 8, D), BF16),
        scratch_shapes=[pltpu.VMEM((64, 8, D), F32)],
        input_output_aliases={0: 0},
        name="fill_rest",
    )(send, mine, got, tok, ninth, gain)


def finish_kernel(yl_ref, recv_ref, wk_hbm, wv_hbm, gw_ref, gg_ref, gain_ref, scr, wk, wv, sems):
    copies = [
        pltpu.make_async_copy(wk_hbm, wk, sems.at[0]),
        pltpu.make_async_copy(wv_hbm, wv, sems.at[1]),
    ]
    for copy in copies:
        copy.start()

    def add(j, sums):
        return tuple(s + recv_ref[j, n].astype(F32) for n, s in enumerate(sums))

    sums = lax.fori_loop(0, 64, add, tuple(jnp.zeros((8, D), F32) for _ in range(3)))
    gw_ref[0, :8] = sums[0]
    gw_ref[3, :8] = sums[1]

    def slot(b):
        row, lane = SLOTS[b]
        return sums[2][row : row + 1, lane : lane + 128]

    for b in range(18):
        at = 128 * (b % 9)
        gw_ref[3 * (b // 9), 8:9, at : at + 128] = slot(b)
    for b in range(9):
        gain_ref[:, 128 * b : 128 * b + 128] = slot(20 + b) + slot(29 + b)
    base = yl_ref[0] * 32
    nines = [SLOTS[18], SLOTS[19]]
    for t in range(32):
        cols = slice(36 * t, 36 * t + 36)
        x = recv_ref[t, 2, :, :256].astype(F32) + recv_ref[32 + t, 2, :, :256].astype(F32)
        eight = x[:, :80] + x[:, 80:160]
        one = jnp.zeros((1, 128), F32)
        for row, lane in nines:
            for j in (t, 32 + t):
                one = one + recv_ref[j, 2, :, lane : lane + 128].astype(F32)[row : row + 1]
        for n in range(2):
            gw_ref[1 + n, :8, cols] = eight[:, 40 * n : 40 * n + 36]
            gw_ref[1 + n, 8:9, cols] = one[:, 40 * n : 40 * n + 36]
        near = recv_ref[base + t, 2, :, 128:512].astype(F32)
        for half in range(2):
            for m in range(2):
                for n in range(2):
                    lane = 32 + 160 * half + 80 * m + 40 * n
                    row = 16 * m + 8 * half
                    scr[n, row : row + 8, cols] = near[:, lane : lane + 36]
    for copy in copies:
        copy.wait()
    grad = dot(scr[0].astype(BF16), wk[...], 1, 1) + dot(scr[1].astype(BF16), wv[...], 1, 1)
    gg_ref[...] = grad.astype(BF16)


def finish(yl, recv, w_key, w_value):
    vmem = pl.BlockSpec(memory_space=pltpu.VMEM)
    hbm = pl.BlockSpec(memory_space=pl.ANY)
    return pl.pallas_call(
        finish_kernel,
        in_specs=[pl.BlockSpec(memory_space=pltpu.SMEM), vmem, hbm, hbm],
        out_specs=[vmem] * 3,
        out_shape=[
            jax.ShapeDtypeStruct((4, 9, D), F32),
            jax.ShapeDtypeStruct((32, D), BF16),
            jax.ShapeDtypeStruct((1, D), F32),
        ],
        scratch_shapes=[
            pltpu.VMEM((2, 32, D), F32),
            pltpu.VMEM((D, D), BF16),
            pltpu.VMEM((D, D), BF16),
            pltpu.SemaphoreType.DMA((2,)),
        ],
        name="finish",
    )(yl, recv, w_key, w_value)


def on_device(tiles, tile_image, guide, gain, w_query, w_key, w_value, w_out, grad_out):
    core = lax.axis_index("c")
    yl = lax.axis_index("yl")
    whole = lax.all_to_all(
        jnp.broadcast_to(guide, (32, *guide.shape)), TILE_AXES, 0, 0, tiled=True
    )
    xf = tiles.astype(F32)
    rstd = lax.rsqrt(jnp.mean(xf * xf, axis=-1, keepdims=True) + 1e-06)
    normed = xf * rstd
    hidden = (normed * gain).astype(BF16)
    query = dot(hidden, w_query, 1, 0).astype(BF16)
    dout = dot(grad_out, w_out, 1, 1).astype(BF16)
    q_wide, d_wide = spread_heads(query, dout)
    w_kv = spread_weights(w_key, w_value)
    want = wanted_rows(core)
    hid_both = jnp.concatenate([hidden, lax.ppermute(hidden, "c", SWAP)], axis=0)
    hid_rows = dot(one_hot(want, D), hid_both, 1, 1).astype(BF16)
    grad_got = lax.ppermute(grad_out, "c", SWAP)
    q_wide, hid_rows = lax.optimization_barrier((q_wide, hid_rows))

    pay, outv, dq = attention(tile_image, whole, w_kv, q_wide, d_wide)
    got = lax.all_to_all(pay, TILE_AXES, 0, 0, tiled=True)

    dq_got = lax.ppermute(dq, "c", SWAP)
    out_got = lax.ppermute(outv, "c", SWAP)
    send, ninth = weight_parts(want, hid_rows, outv, out_got, dq, dq_got, grad_out, grad_got)
    dh = dot(dq, w_query, 1, 1)
    gain_part = jnp.sum(dh * normed, axis=0, keepdims=True)
    gain_part = gain_part + lax.ppermute(gain_part, "c", SWAP)
    dn = dh * gain
    grad_tiles = (rstd * (dn - normed * jnp.mean(dn * normed, axis=-1, keepdims=True))).astype(BF16)

    got, ninth, gain_part = lax.optimization_barrier((got, ninth, gain_part))
    mine, theirs, tok = image_sums(core[None], got, whole)
    send = fill_rest(send, mine, lax.ppermute(theirs, "c", SWAP), tok, ninth, gain_part)
    recv = lax.all_to_all(send, CHIP_AXES, 0, 0, tiled=True)
    grad_weights, grad_guide, grad_gain = finish(yl[None], recv, w_key, w_value)
    return (grad_tiles, grad_guide.reshape(guide.shape), grad_weights, grad_gain.reshape(D))


def solution(mesh):
    fine = Mesh(mesh.devices.reshape(2, 2, 4, 2, 4), ("yl", "c", "x", "yh", "z"))
    every = ("yl", "c", "x", "yh", "z")
    return jax.shard_map(
        on_device,
        mesh=fine,
        in_specs=(
            P(every, None),
            P(every),
            P(("yl", "c"), TILE_AXES, None),
            P(),
            P(),
            P(),
            P(),
            P(),
            P(every, None),
        ),
        out_specs=(
            P(every, None),
            P(("yl", "c"), TILE_AXES, None),
            P(None, every, None),
            P(),
        ),
        check_vma=False,
    )
```

```python
import jax
import jax.numpy as jnp
from jax import lax
from jax.experimental import pallas as pl
from jax.experimental.pallas import tpu as pltpu
from jax.sharding import Mesh, PartitionSpec as P

HEADS = 16
HD = 72
D = 1152
G = 512
F32 = jnp.float32
BF16 = jnp.bfloat16
TILE_AXES = ("x", "yh", "z")
CHIP_AXES = ("yl", "x", "yh", "z")
SWAP = [(0, 1), (1, 0)]


def dot(a, b, ca, cb):
    return lax.dot_general(a, b, (((ca,), (cb,)), ((), ())), preferred_element_type=F32)


def attention_kernel(
    img_ref, g_hbm, wk_hbm, wv_hbm, q_ref, d_ref, pay_hbm, o_ref, dq_ref,
    guide, wk, wv, k_scr, v_scr, pay, sems, out_sems,
):
    loads = [
        pltpu.make_async_copy(g_hbm.at[:, img_ref[0]], guide, sems.at[0]),
        pltpu.make_async_copy(wk_hbm, wk, sems.at[1]),
        pltpu.make_async_copy(wv_hbm, wv, sems.at[2]),
    ]
    for copy in loads:
        copy.start()
    loads[0].wait()
    tokens = guide[...].reshape(G, D)
    loads[1].wait()
    k_scr[...] = dot(tokens, wk[...], 1, 0).astype(BF16)
    loads[2].wait()
    v_scr[...] = dot(tokens, wv[...], 1, 0).astype(BF16)
    scale = HD ** (-0.5)
    flag = jnp.full((4, G), img_ref[0], jnp.int32).astype(F32)
    stores = []
    for h in range(HEADS):
        cols = slice(h * HD, (h + 1) * HD)
        q, d, k, v = q_ref[:, cols], d_ref[:, cols], k_scr[:, cols], v_scr[:, cols]
        scores = dot(q, k, 1, 1) * scale
        dprob = dot(d, v, 1, 1)
        top = jnp.max(scores, axis=-1, keepdims=True)
        expo = jnp.exp(scores - top)
        probs = expo * (1.0 / jnp.sum(expo, axis=-1, keepdims=True))
        pb = probs.astype(BF16)
        weighted = probs * dprob
        delta = jnp.sum(weighted, axis=-1, keepdims=True)
        ds = ((weighted - probs * delta) * scale).astype(BF16)
        o_ref[:, cols] = dot(pb, v, 1, 0).astype(BF16)
        dq_ref[:, cols] = dot(ds, k, 1, 0).astype(BF16)
        for j, part in enumerate((dot(q, ds, 0, 0), dot(d, pb, 0, 0))):
            for i in range(2):
                rows = jnp.concatenate([part[36 * i : 36 * i + 36], flag], axis=0)
                pay[2 * h + i, j] = rows.astype(BF16)
        two = pl.ds(2 * h, 2)
        stores.append(pltpu.make_async_copy(pay.at[two], pay_hbm.at[two], out_sems.at[h]))
        stores[-1].start()
    for copy in stores:
        copy.wait()


def attention(img, whole, w_key, w_value, q, d):
    t = q.shape[0]
    vmem = pl.BlockSpec(memory_space=pltpu.VMEM)
    hbm = pl.BlockSpec(memory_space=pl.ANY)
    return pl.pallas_call(
        attention_kernel,
        in_specs=[pl.BlockSpec(memory_space=pltpu.SMEM), hbm, hbm, hbm, vmem, vmem],
        out_specs=[hbm, vmem, vmem],
        out_shape=[
            jax.ShapeDtypeStruct((32, 2, 40, G), BF16),
            jax.ShapeDtypeStruct((t, D), BF16),
            jax.ShapeDtypeStruct((t, D), BF16),
        ],
        scratch_shapes=[
            pltpu.VMEM((32, 16, D), BF16),
            pltpu.VMEM((D, D), BF16),
            pltpu.VMEM((D, D), BF16),
            pltpu.VMEM((G, D), BF16),
            pltpu.VMEM((G, D), BF16),
            pltpu.VMEM((32, 2, 40, G), BF16),
            pltpu.SemaphoreType.DMA((3,)),
            pltpu.SemaphoreType.DMA((HEADS,)),
        ],
        name="attention",
    )(img, whole, w_key, w_value, q, d)


ROWS = 576


def eight_and_one(rows):
    return jnp.where(rows < 512, rows // 8 * 9 + rows % 8, (rows - 512) * 9 + 8)


def wanted_rows(core):
    row = eight_and_one(jnp.arange(ROWS, dtype=jnp.int32))
    return (row // 288 * 576 + core * 288 + row % 288)[:, None]


def one_hot(want, width):
    return (want == lax.broadcasted_iota(jnp.int32, (want.shape[0], width), 1)).astype(BF16)


def weight_parts_kernel(
    want_ref, hid_ref, o_ref, o2_ref, dq_ref, dq2_ref, g_ref, g2_ref, send_ref, ninth_ref
):
    o = jnp.concatenate([o_ref[...], o2_ref[...]], axis=0)
    dq = jnp.concatenate([dq_ref[...], dq2_ref[...]], axis=0)
    g = jnp.concatenate([g_ref[...], g2_ref[...]], axis=0)
    o_rows = dot(one_hot(want_ref[...], D), o, 1, 1).astype(BF16)
    parts = (dot(hid_ref[...], dq, 1, 0), dot(o_rows, g, 1, 0))
    for m, part in enumerate(parts):
        send_ref[:, m] = part[:512].reshape(64, 8, D).astype(BF16)
        ninth_ref[:, m * D : (m + 1) * D] = part[512:]


def weight_parts(*args):
    vmem = pl.BlockSpec(memory_space=pltpu.VMEM)
    return pl.pallas_call(
        weight_parts_kernel,
        grid=(1,),
        in_specs=[vmem] * 8,
        out_specs=[
            pl.BlockSpec((64, 2, 8, D), lambda i: (0, 0, 0, 0)),
            pl.BlockSpec((64, 2 * D), lambda i: (0, 0)),
        ],
        out_shape=[
            jax.ShapeDtypeStruct((64, 3, 8, D), BF16),
            jax.ShapeDtypeStruct((64, 2 * D), F32),
        ],
        name="weight_parts",
    )(*args)


def image_sums_kernel(core_ref, got_ref, g_ref, mine_ref, theirs_ref, tok_ref, scr):
    def add(s, sums):
        terms = got_ref[s].astype(F32)
        first = terms[:, 36:37, :] == 0.0
        zero = jnp.zeros_like(terms)
        return sums[0] + jnp.where(first, terms, zero), sums[1] + jnp.where(first, zero, terms)

    zero = jnp.zeros((2, 40, G), F32)
    sums = lax.fori_loop(0, 32, add, (zero, zero))
    rounded = [x.reshape(80, G).astype(BF16) for x in sums]
    prod = dot(rounded[0], g_ref[:, 0].reshape(G, D), 1, 0)
    prod = prod + dot(rounded[1], g_ref[:, 1].reshape(G, D), 1, 0)
    scr[...] = jnp.concatenate([prod, jnp.zeros((48, D), F32)], axis=0).T
    core = core_ref[0]
    for n in range(2):
        for out, c in ((mine_ref, core), (theirs_ref, 1 - core)):
            start = pl.multiple_of(n * 576 + c * 288, 32)
            out[n * 288 : n * 288 + 288] = scr[pl.ds(start, 288), :]
    both = jnp.concatenate([x.astype(F32) for x in rounded] + [jnp.zeros((96, G), F32)], axis=0)
    tok_ref[...] = both.T


def image_sums(core, got, whole):
    vmem = pl.BlockSpec(memory_space=pltpu.VMEM)
    return pl.pallas_call(
        image_sums_kernel,
        in_specs=[pl.BlockSpec(memory_space=pltpu.SMEM), vmem, vmem],
        out_specs=[vmem] * 3,
        out_shape=[
            jax.ShapeDtypeStruct((ROWS, 128), F32),
            jax.ShapeDtypeStruct((ROWS, 128), F32),
            jax.ShapeDtypeStruct((G, 256), F32),
        ],
        scratch_shapes=[pltpu.VMEM((D, 128), F32)],
        name="image_sums",
    )(core, got, whole)


SLOTS = [(row, lane) for lane in range(512, D, 128) for row in range(8)]


def fill_rest_kernel(send_ref, mine_ref, got_ref, tok_ref, ninth_ref, gain_ref, out_ref, scr):
    scr[:, :, 384:512] = jnp.zeros((64, 8, 128), F32)
    total = mine_ref[...] + got_ref[...]
    high = total.astype(BF16)
    low = (total - high.astype(F32)).astype(BF16)
    want = eight_and_one(lax.broadcasted_iota(jnp.int32, (ROWS, ROWS), 0))
    order = (want == lax.broadcasted_iota(jnp.int32, (ROWS, ROWS), 1)).astype(BF16)
    moved = [dot(order, x, 1, 0) for x in (high, low)]
    tok = tok_ref[...].reshape(32, 16, 256)
    for n in range(2):
        scr[:, :, 80 * n : 80 * n + 80] = moved[n][:512].reshape(64, 8, 128)[:, :, :80]
        for half in range(2):
            lanes = slice(160 * half + 160, 160 * half + 320)
            scr[32 * n : 32 * n + 32, :, lanes] = tok[:, 8 * half : 8 * half + 8, :160]
    gain = gain_ref[...]
    gain_high = gain.astype(BF16).astype(F32)
    gains = jnp.concatenate([gain_high, gain - gain_high], axis=1)
    for b, (row, lane) in enumerate(SLOTS):
        if b < 18:
            block = ninth_ref[:, 128 * b : 128 * b + 128]
        elif b < 20:
            block = moved[b - 18][512:]
        elif b < 38:
            block = jnp.broadcast_to(gains[:, 128 * (b - 20) : 128 * (b - 20) + 128], (64, 128))
        else:
            block = jnp.zeros((64, 128), F32)
        scr[:, row, lane : lane + 128] = block
    out_ref[:, 0] = scr[...].astype(BF16)


def fill_rest(send, mine, got, tok, ninth, gain):
    vmem = pl.BlockSpec(memory_space=pltpu.VMEM)
    return pl.pallas_call(
        fill_rest_kernel,
        grid=(1,),
        in_specs=[pl.BlockSpec(memory_space=pl.ANY)] + [vmem] * 5,
        out_specs=pl.BlockSpec((64, 1, 8, D), lambda i: (0, 2, 0, 0)),
        out_shape=jax.ShapeDtypeStruct((64, 3, 8, D), BF16),
        scratch_shapes=[pltpu.VMEM((64, 8, D), F32)],
        input_output_aliases={0: 0},
        name="fill_rest",
    )(send, mine, got, tok, ninth, gain)


def finish_kernel(yl_ref, recv_ref, wk_hbm, wv_hbm, gw_ref, gg_ref, gain_ref, scr, wk, wv, sems):
    copies = [
        pltpu.make_async_copy(wk_hbm, wk, sems.at[0]),
        pltpu.make_async_copy(wv_hbm, wv, sems.at[1]),
    ]
    for copy in copies:
        copy.start()

    def add(j, sums):
        return tuple(s + recv_ref[j, n].astype(F32) for n, s in enumerate(sums))

    sums = lax.fori_loop(0, 64, add, tuple(jnp.zeros((8, D), F32) for _ in range(3)))
    gw_ref[:8, 0] = sums[0]
    gw_ref[:8, 3] = sums[1]

    def slot(b):
        row, lane = SLOTS[b]
        return sums[2][row : row + 1, lane : lane + 128]

    for b in range(18):
        at = 128 * (b % 9)
        gw_ref[8:9, 3 * (b // 9), at : at + 128] = slot(b)
    for b in range(9):
        gain_ref[b : b + 1] = slot(20 + b) + slot(29 + b)
    base = yl_ref[0] * 32
    nines = [SLOTS[18], SLOTS[19]]
    for t in range(32):
        cols = slice(36 * t, 36 * t + 36)
        x = recv_ref[t, 2, :, :256].astype(F32) + recv_ref[32 + t, 2, :, :256].astype(F32)
        eight = x[:, :80] + x[:, 80:160]
        one = jnp.zeros((1, 128), F32)
        for row, lane in nines:
            for j in (t, 32 + t):
                one = one + recv_ref[j, 2, :, lane : lane + 128].astype(F32)[row : row + 1]
        for n in range(2):
            gw_ref[:8, 1 + n, cols] = eight[:, 40 * n : 40 * n + 36]
            gw_ref[8:9, 1 + n, cols] = one[:, 40 * n : 40 * n + 36]
        near = recv_ref[base + t, 2, :, 128:512].astype(F32)
        for half in range(2):
            for m in range(2):
                for n in range(2):
                    lane = 32 + 160 * half + 80 * m + 40 * n
                    row = 16 * m + 8 * half
                    scr[n, row : row + 8, cols] = near[:, lane : lane + 36]
    for copy in copies:
        copy.wait()
    grad = dot(scr[0].astype(BF16), wk[...], 1, 1) + dot(scr[1].astype(BF16), wv[...], 1, 1)
    gg_ref[...] = grad.astype(BF16)


def finish(yl, recv, w_key, w_value):
    vmem = pl.BlockSpec(memory_space=pltpu.VMEM)
    hbm = pl.BlockSpec(memory_space=pl.ANY)
    return pl.pallas_call(
        finish_kernel,
        in_specs=[pl.BlockSpec(memory_space=pltpu.SMEM), vmem, hbm, hbm],
        out_specs=[vmem] * 3,
        out_shape=[
            jax.ShapeDtypeStruct((9, 4, D), F32),
            jax.ShapeDtypeStruct((32, D), BF16),
            jax.ShapeDtypeStruct((9, 128), F32),
        ],
        scratch_shapes=[
            pltpu.VMEM((2, 32, D), F32),
            pltpu.VMEM((D, D), BF16),
            pltpu.VMEM((D, D), BF16),
            pltpu.SemaphoreType.DMA((2,)),
        ],
        name="finish",
    )(yl, recv, w_key, w_value)


def on_device(tiles, tile_image, guide, gain, w_query, w_key, w_value, w_out, grad_out):
    core = lax.axis_index("c")
    yl = lax.axis_index("yl")
    whole = lax.all_to_all(
        jnp.broadcast_to(guide, (32, *guide.shape)), TILE_AXES, 0, 0, tiled=True
    )
    xf = tiles.astype(F32)
    rstd = lax.rsqrt(jnp.mean(xf * xf, axis=-1, keepdims=True) + 1e-06)
    normed = xf * rstd
    hidden = (normed * gain).astype(BF16)
    query = dot(hidden, w_query, 1, 0).astype(BF16)
    dout = dot(grad_out, w_out, 1, 1).astype(BF16)
    want = wanted_rows(core)
    hid_both = jnp.concatenate([hidden, lax.ppermute(hidden, "c", SWAP)], axis=0)
    hid_rows = dot(one_hot(want, D), hid_both, 1, 1).astype(BF16)
    grad_got = lax.ppermute(grad_out, "c", SWAP)
    query, hid_rows = lax.optimization_barrier((query, hid_rows))

    pay, outv, dq = attention(tile_image, whole, w_key, w_value, query, dout)
    got = lax.all_to_all(pay, TILE_AXES, 0, 0, tiled=True)

    dq_got = lax.ppermute(dq, "c", SWAP)
    out_got = lax.ppermute(outv, "c", SWAP)
    send, ninth = weight_parts(want, hid_rows, outv, out_got, dq, dq_got, grad_out, grad_got)
    dh = dot(dq, w_query, 1, 1)
    gain_part = jnp.sum(dh * normed, axis=0, keepdims=True)
    gain_part = gain_part + lax.ppermute(gain_part, "c", SWAP)
    dn = dh * gain
    grad_tiles = (rstd * (dn - normed * jnp.mean(dn * normed, axis=-1, keepdims=True))).astype(BF16)

    got, ninth, gain_part = lax.optimization_barrier((got, ninth, gain_part))
    mine, theirs, tok = image_sums(core[None], got, whole)
    send = fill_rest(send, mine, lax.ppermute(theirs, "c", SWAP), tok, ninth, gain_part)
    recv = lax.all_to_all(send, CHIP_AXES, 0, 0, tiled=True)
    grad_weights, grad_guide, grad_gain = finish(yl[None], recv, w_key, w_value)
    grad_weights = grad_weights.transpose(1, 0, 2)
    return (grad_tiles, grad_guide.reshape(guide.shape), grad_weights, grad_gain.reshape(D))


def solution(mesh):
    fine = Mesh(mesh.devices.reshape(2, 2, 4, 2, 4), ("yl", "c", "x", "yh", "z"))
    every = ("yl", "c", "x", "yh", "z")
    return jax.shard_map(
        on_device,
        mesh=fine,
        in_specs=(
            P(every, None),
            P(every),
            P(("yl", "c"), TILE_AXES, None),
            P(),
            P(),
            P(),
            P(),
            P(),
            P(every, None),
        ),
        out_specs=(
            P(every, None),
            P(("yl", "c"), TILE_AXES, None),
            P(None, every, None),
            P(),
        ),
        check_vma=False,
    )
```

```python
import jax
import jax.numpy as jnp
from jax import lax
from jax.experimental import pallas as pl
from jax.experimental.pallas import tpu as pltpu
from jax.sharding import Mesh, PartitionSpec as P

HEADS = 16
HD = 72
D = 1152
G = 512
F32 = jnp.float32
BF16 = jnp.bfloat16
TILE_AXES = ("x", "yh", "z")
CHIP_AXES = ("yl", "x", "yh", "z")
SWAP = [(0, 1), (1, 0)]


def dot(a, b, ca, cb):
    return lax.dot_general(a, b, (((ca,), (cb,)), ((), ())), preferred_element_type=F32)


def ring_send(block, axis, distance):
    return lax.ppermute(block, axis, [(i, (i + distance) % 4) for i in range(4)])


def ring_gather(block, axis):
    half = block.shape[0] // 2
    before = ring_send(block, axis, 1)
    after = ring_send(block, axis, 3)
    first = ring_send(before[:half], axis, 1)
    second = ring_send(after[half:], axis, 3)
    return [block, after, first, second, before]


def gather_guide(guide):
    other = lax.ppermute(guide, "yh", SWAP)
    near = [ring_gather(jnp.stack([guide[m], other[m]]), "xz"[m]) for m in (0, 1)]
    near = [jnp.concatenate(blocks).reshape(4, 2, 16, D) for blocks in near]
    return [ring_gather(near[m], "zx"[m]) for m in (0, 1)]


def guide_pieces(m, blocks, pos_ref):
    x, yh, z = pos_ref[0], pos_ref[1], pos_ref[2]
    places = ((0, 0, 4), (1, 0, 4), (2, 0, 2), (2, 2, 2), (3, 0, 4))
    for block, (two, start, count) in zip(blocks, places):
        for i in range(count):
            one = start + i
            dx, dz = (one, two) if m == 0 else (two, one)
            for dy in range(2):
                place = ((x + dx) & 3) * 8 + ((yh + dy) & 1) * 4 + ((z + dz) & 3)
                yield block.at[i, dy], place


def whole_guide_kernel(pos_ref, *refs):
    out, sems = refs[10], refs[11]
    copies = []
    for m in range(2):
        for i, (source, place) in enumerate(guide_pieces(m, refs[5 * m : 5 * m + 5], pos_ref)):
            copies.append(pltpu.make_async_copy(source, out.at[place, m], sems.at[32 * m + i]))
            copies[-1].start()
    for copy in copies:
        copy.wait()


def whole_guide(pos, blocks):
    hbm = pl.BlockSpec(memory_space=pl.ANY)
    return pl.pallas_call(
        whole_guide_kernel,
        in_specs=[pl.BlockSpec(memory_space=pltpu.SMEM)] + [hbm] * 10,
        out_specs=hbm,
        out_shape=jax.ShapeDtypeStruct((32, 2, 16, D), BF16),
        scratch_shapes=[pltpu.SemaphoreType.DMA((64,))],
        name="whole_guide",
    )(pos, *blocks)


def attention_kernel(img_ref, pos_ref, *refs):
    blocks, refs = refs[:10], refs[10:]
    wk_hbm, wv_hbm, q_ref, d_ref, pay_hbm, o_ref, dq_ref = refs[:7]
    guide, wk, wv, k_scr, v_scr, pay, sems, guide_sems, out_sems = refs[7:]
    loads = [
        pltpu.make_async_copy(wk_hbm, wk, sems.at[0]),
        pltpu.make_async_copy(wv_hbm, wv, sems.at[1]),
    ]
    for m in range(2):

        @pl.when(img_ref[0] == m)
        def _(m=m):
            pieces = guide_pieces(m, blocks[5 * m : 5 * m + 5], pos_ref)
            copies = [
                pltpu.make_async_copy(source, guide.at[place], guide_sems.at[i])
                for i, (source, place) in enumerate(pieces)
            ]
            for copy in copies:
                copy.start()
            for copy in loads:
                copy.start()
            for copy in copies:
                copy.wait()

    tokens = guide[...].reshape(G, D)
    loads[0].wait()
    k_scr[...] = dot(tokens, wk[...], 1, 0).astype(BF16)
    loads[1].wait()
    v_scr[...] = dot(tokens, wv[...], 1, 0).astype(BF16)
    scale = HD ** (-0.5)
    flag = jnp.full((4, G), img_ref[0], jnp.int32).astype(F32)
    stores = []
    for h in range(HEADS):
        cols = slice(h * HD, (h + 1) * HD)
        q, d, k, v = q_ref[:, cols], d_ref[:, cols], k_scr[:, cols], v_scr[:, cols]
        scores = dot(q, k, 1, 1) * scale
        dprob = dot(d, v, 1, 1)
        top = jnp.max(scores, axis=-1, keepdims=True)
        expo = jnp.exp(scores - top)
        probs = expo * (1.0 / jnp.sum(expo, axis=-1, keepdims=True))
        pb = probs.astype(BF16)
        weighted = probs * dprob
        delta = jnp.sum(weighted, axis=-1, keepdims=True)
        ds = ((weighted - probs * delta) * scale).astype(BF16)
        o_ref[:, cols] = dot(pb, v, 1, 0).astype(BF16)
        dq_ref[:, cols] = dot(ds, k, 1, 0).astype(BF16)
        for j, part in enumerate((dot(q, ds, 0, 0), dot(d, pb, 0, 0))):
            for i in range(2):
                rows = jnp.concatenate([part[36 * i : 36 * i + 36], flag], axis=0)
                pay[2 * h + i, j] = rows.astype(BF16)
        two = pl.ds(2 * h, 2)
        stores.append(pltpu.make_async_copy(pay.at[two], pay_hbm.at[two], out_sems.at[h]))
        stores[-1].start()
    for copy in stores:
        copy.wait()


def attention(img, pos, blocks, w_key, w_value, q, d):
    t = q.shape[0]
    vmem = pl.BlockSpec(memory_space=pltpu.VMEM)
    hbm = pl.BlockSpec(memory_space=pl.ANY)
    return pl.pallas_call(
        attention_kernel,
        in_specs=[pl.BlockSpec(memory_space=pltpu.SMEM)] * 2 + [hbm] * 12 + [vmem] * 2,
        out_specs=[hbm, vmem, vmem],
        out_shape=[
            jax.ShapeDtypeStruct((32, 2, 40, G), BF16),
            jax.ShapeDtypeStruct((t, D), BF16),
            jax.ShapeDtypeStruct((t, D), BF16),
        ],
        scratch_shapes=[
            pltpu.VMEM((32, 16, D), BF16),
            pltpu.VMEM((D, D), BF16),
            pltpu.VMEM((D, D), BF16),
            pltpu.VMEM((G, D), BF16),
            pltpu.VMEM((G, D), BF16),
            pltpu.VMEM((32, 2, 40, G), BF16),
            pltpu.SemaphoreType.DMA((2,)),
            pltpu.SemaphoreType.DMA((32,)),
            pltpu.SemaphoreType.DMA((HEADS,)),
        ],
        name="attention",
    )(img, pos, *blocks, w_key, w_value, q, d)


ROWS = 576


def eight_and_one(rows):
    return jnp.where(rows < 512, rows // 8 * 9 + rows % 8, (rows - 512) * 9 + 8)


def wanted_rows(core):
    row = eight_and_one(jnp.arange(ROWS, dtype=jnp.int32))
    return (row // 288 * 576 + core * 288 + row % 288)[:, None]


def one_hot(want, width):
    return (want == lax.broadcasted_iota(jnp.int32, (want.shape[0], width), 1)).astype(BF16)


def weight_parts_kernel(
    want_ref, hid_ref, o_ref, o2_ref, dq_ref, dq2_ref, g_ref, g2_ref, send_ref, ninth_ref
):
    o = jnp.concatenate([o_ref[...], o2_ref[...]], axis=0)
    dq = jnp.concatenate([dq_ref[...], dq2_ref[...]], axis=0)
    g = jnp.concatenate([g_ref[...], g2_ref[...]], axis=0)
    o_rows = dot(one_hot(want_ref[...], D), o, 1, 1).astype(BF16)
    parts = (dot(hid_ref[...], dq, 1, 0), dot(o_rows, g, 1, 0))
    for m, part in enumerate(parts):
        send_ref[:, m] = part[:512].reshape(64, 8, D).astype(BF16)
        ninth_ref[:, m * D : (m + 1) * D] = part[512:]


def weight_parts(*args):
    vmem = pl.BlockSpec(memory_space=pltpu.VMEM)
    return pl.pallas_call(
        weight_parts_kernel,
        grid=(1,),
        in_specs=[vmem] * 8,
        out_specs=[
            pl.BlockSpec((64, 2, 8, D), lambda i: (0, 0, 0, 0)),
            pl.BlockSpec((64, 2 * D), lambda i: (0, 0)),
        ],
        out_shape=[
            jax.ShapeDtypeStruct((64, 3, 8, D), BF16),
            jax.ShapeDtypeStruct((64, 2 * D), F32),
        ],
        name="weight_parts",
    )(*args)


def image_sums_kernel(core_ref, got_ref, g_ref, mine_ref, theirs_ref, tok_ref, scr):
    def add(s, sums):
        terms = got_ref[s].astype(F32)
        first = terms[:, 36:37, :] == 0.0
        zero = jnp.zeros_like(terms)
        return sums[0] + jnp.where(first, terms, zero), sums[1] + jnp.where(first, zero, terms)

    zero = jnp.zeros((2, 40, G), F32)
    sums = lax.fori_loop(0, 32, add, (zero, zero))
    rounded = [x.reshape(80, G).astype(BF16) for x in sums]
    prod = dot(rounded[0], g_ref[:, 0].reshape(G, D), 1, 0)
    prod = prod + dot(rounded[1], g_ref[:, 1].reshape(G, D), 1, 0)
    scr[...] = jnp.concatenate([prod, jnp.zeros((48, D), F32)], axis=0).T
    core = core_ref[0]
    for n in range(2):
        for out, c in ((mine_ref, core), (theirs_ref, 1 - core)):
            start = pl.multiple_of(n * 576 + c * 288, 32)
            out[n * 288 : n * 288 + 288] = scr[pl.ds(start, 288), :]
    both = jnp.concatenate([x.astype(F32) for x in rounded] + [jnp.zeros((96, G), F32)], axis=0)
    tok_ref[...] = both.T


def image_sums(core, got, whole):
    vmem = pl.BlockSpec(memory_space=pltpu.VMEM)
    return pl.pallas_call(
        image_sums_kernel,
        in_specs=[pl.BlockSpec(memory_space=pltpu.SMEM), vmem, vmem],
        out_specs=[vmem] * 3,
        out_shape=[
            jax.ShapeDtypeStruct((ROWS, 128), F32),
            jax.ShapeDtypeStruct((ROWS, 128), F32),
            jax.ShapeDtypeStruct((G, 256), F32),
        ],
        scratch_shapes=[pltpu.VMEM((D, 128), F32)],
        name="image_sums",
    )(core, got, whole)


SLOTS = [(row, lane) for lane in range(512, D, 128) for row in range(8)]


def fill_rest_kernel(send_ref, mine_ref, got_ref, tok_ref, ninth_ref, gain_ref, out_ref, scr):
    scr[:, :, 384:512] = jnp.zeros((64, 8, 128), F32)
    total = mine_ref[...] + got_ref[...]
    high = total.astype(BF16)
    low = (total - high.astype(F32)).astype(BF16)
    want = eight_and_one(lax.broadcasted_iota(jnp.int32, (ROWS, ROWS), 0))
    order = (want == lax.broadcasted_iota(jnp.int32, (ROWS, ROWS), 1)).astype(BF16)
    moved = [dot(order, x, 1, 0) for x in (high, low)]
    tok = tok_ref[...].reshape(32, 16, 256)
    for n in range(2):
        scr[:, :, 80 * n : 80 * n + 80] = moved[n][:512].reshape(64, 8, 128)[:, :, :80]
        for half in range(2):
            lanes = slice(160 * half + 160, 160 * half + 320)
            scr[32 * n : 32 * n + 32, :, lanes] = tok[:, 8 * half : 8 * half + 8, :160]
    gain = gain_ref[...]
    gain_high = gain.astype(BF16).astype(F32)
    gains = jnp.concatenate([gain_high, gain - gain_high], axis=1)
    for b, (row, lane) in enumerate(SLOTS):
        if b < 18:
            block = ninth_ref[:, 128 * b : 128 * b + 128]
        elif b < 20:
            block = moved[b - 18][512:]
        elif b < 38:
            block = jnp.broadcast_to(gains[:, 128 * (b - 20) : 128 * (b - 20) + 128], (64, 128))
        else:
            block = jnp.zeros((64, 128), F32)
        scr[:, row, lane : lane + 128] = block
    out_ref[:, 0] = scr[...].astype(BF16)


def fill_rest(send, mine, got, tok, ninth, gain):
    vmem = pl.BlockSpec(memory_space=pltpu.VMEM)
    return pl.pallas_call(
        fill_rest_kernel,
        grid=(1,),
        in_specs=[pl.BlockSpec(memory_space=pl.ANY)] + [vmem] * 5,
        out_specs=pl.BlockSpec((64, 1, 8, D), lambda i: (0, 2, 0, 0)),
        out_shape=jax.ShapeDtypeStruct((64, 3, 8, D), BF16),
        scratch_shapes=[pltpu.VMEM((64, 8, D), F32)],
        input_output_aliases={0: 0},
        name="fill_rest",
    )(send, mine, got, tok, ninth, gain)


def finish_kernel(yl_ref, recv_ref, wk_hbm, wv_hbm, gw_ref, gg_ref, gain_ref, scr, wk, wv, sems):
    copies = [
        pltpu.make_async_copy(wk_hbm, wk, sems.at[0]),
        pltpu.make_async_copy(wv_hbm, wv, sems.at[1]),
    ]
    for copy in copies:
        copy.start()

    def add(j, sums):
        return tuple(s + recv_ref[j, n].astype(F32) for n, s in enumerate(sums))

    sums = lax.fori_loop(0, 64, add, tuple(jnp.zeros((8, D), F32) for _ in range(3)))
    gw_ref[:8, 0] = sums[0]
    gw_ref[:8, 3] = sums[1]

    def slot(b):
        row, lane = SLOTS[b]
        return sums[2][row : row + 1, lane : lane + 128]

    for b in range(18):
        at = 128 * (b % 9)
        gw_ref[8:9, 3 * (b // 9), at : at + 128] = slot(b)
    for b in range(9):
        gain_ref[b : b + 1] = slot(20 + b) + slot(29 + b)
    base = yl_ref[0] * 32
    nines = [SLOTS[18], SLOTS[19]]
    for t in range(32):
        cols = slice(36 * t, 36 * t + 36)
        x = recv_ref[t, 2, :, :256].astype(F32) + recv_ref[32 + t, 2, :, :256].astype(F32)
        eight = x[:, :80] + x[:, 80:160]
        one = jnp.zeros((1, 128), F32)
        for row, lane in nines:
            for j in (t, 32 + t):
                one = one + recv_ref[j, 2, :, lane : lane + 128].astype(F32)[row : row + 1]
        for n in range(2):
            gw_ref[:8, 1 + n, cols] = eight[:, 40 * n : 40 * n + 36]
            gw_ref[8:9, 1 + n, cols] = one[:, 40 * n : 40 * n + 36]
        near = recv_ref[base + t, 2, :, 128:512].astype(F32)
        for half in range(2):
            for m in range(2):
                for n in range(2):
                    lane = 32 + 160 * half + 80 * m + 40 * n
                    row = 16 * m + 8 * half
                    scr[n, row : row + 8, cols] = near[:, lane : lane + 36]
    for copy in copies:
        copy.wait()
    grad = dot(scr[0].astype(BF16), wk[...], 1, 1) + dot(scr[1].astype(BF16), wv[...], 1, 1)
    gg_ref[...] = grad.astype(BF16)


def finish(yl, recv, w_key, w_value):
    vmem = pl.BlockSpec(memory_space=pltpu.VMEM)
    hbm = pl.BlockSpec(memory_space=pl.ANY)
    return pl.pallas_call(
        finish_kernel,
        in_specs=[pl.BlockSpec(memory_space=pltpu.SMEM), vmem, hbm, hbm],
        out_specs=[vmem] * 3,
        out_shape=[
            jax.ShapeDtypeStruct((9, 4, D), F32),
            jax.ShapeDtypeStruct((32, D), BF16),
            jax.ShapeDtypeStruct((9, 128), F32),
        ],
        scratch_shapes=[
            pltpu.VMEM((2, 32, D), F32),
            pltpu.VMEM((D, D), BF16),
            pltpu.VMEM((D, D), BF16),
            pltpu.SemaphoreType.DMA((2,)),
        ],
        name="finish",
    )(yl, recv, w_key, w_value)


def on_device(tiles, tile_image, guide, gain, w_query, w_key, w_value, w_out, grad_out):
    core = lax.axis_index("c")
    yl = lax.axis_index("yl")
    pos = jnp.stack([lax.axis_index(name) for name in ("x", "yh", "z")])
    zero_blocks, one_blocks = gather_guide(guide)
    blocks = zero_blocks + one_blocks
    xf = tiles.astype(F32)
    rstd = lax.rsqrt(jnp.mean(xf * xf, axis=-1, keepdims=True) + 1e-06)
    normed = xf * rstd
    hidden = (normed * gain).astype(BF16)
    query = dot(hidden, w_query, 1, 0).astype(BF16)
    dout = dot(grad_out, w_out, 1, 1).astype(BF16)
    want = wanted_rows(core)
    hid_both = jnp.concatenate([hidden, lax.ppermute(hidden, "c", SWAP)], axis=0)
    hid_rows = dot(one_hot(want, D), hid_both, 1, 1).astype(BF16)
    grad_got = lax.ppermute(grad_out, "c", SWAP)
    query, hid_rows = lax.optimization_barrier((query, hid_rows))

    pay, outv, dq = attention(tile_image, pos, blocks, w_key, w_value, query, dout)
    got = lax.all_to_all(pay, TILE_AXES, 0, 0, tiled=True)

    dq_got = lax.ppermute(dq, "c", SWAP)
    out_got = lax.ppermute(outv, "c", SWAP)
    send, ninth = weight_parts(want, hid_rows, outv, out_got, dq, dq_got, grad_out, grad_got)
    dh = dot(dq, w_query, 1, 1)
    gain_part = jnp.sum(dh * normed, axis=0, keepdims=True)
    gain_part = gain_part + lax.ppermute(gain_part, "c", SWAP)
    dn = dh * gain
    grad_tiles = (rstd * (dn - normed * jnp.mean(dn * normed, axis=-1, keepdims=True))).astype(BF16)

    whole = whole_guide(pos, blocks)
    got, ninth, gain_part, whole = lax.optimization_barrier((got, ninth, gain_part, whole))
    mine, theirs, tok = image_sums(core[None], got, whole)
    send = fill_rest(send, mine, lax.ppermute(theirs, "c", SWAP), tok, ninth, gain_part)
    recv = lax.all_to_all(send, CHIP_AXES, 0, 0, tiled=True)
    grad_weights, grad_guide, grad_gain = finish(yl[None], recv, w_key, w_value)
    grad_weights = grad_weights.transpose(1, 0, 2)
    return (grad_tiles, grad_guide.reshape(guide.shape), grad_weights, grad_gain.reshape(D))


def solution(mesh):
    fine = Mesh(mesh.devices.reshape(2, 2, 4, 2, 4), ("yl", "c", "x", "yh", "z"))
    every = ("yl", "c", "x", "yh", "z")
    return jax.shard_map(
        on_device,
        mesh=fine,
        in_specs=(
            P(every, None),
            P(every),
            P(("yl", "c"), TILE_AXES, None),
            P(),
            P(),
            P(),
            P(),
            P(),
            P(every, None),
        ),
        out_specs=(
            P(every, None),
            P(("yl", "c"), TILE_AXES, None),
            P(None, every, None),
            P(),
        ),
        check_vma=False,
    )
```

```python
import jax
import jax.numpy as jnp
from jax import lax
from jax.experimental import pallas as pl
from jax.experimental.pallas import tpu as pltpu
from jax.sharding import Mesh, PartitionSpec as P

HEADS = 16
HD = 72
D = 1152
G = 512
F32 = jnp.float32
BF16 = jnp.bfloat16
TILE_AXES = ("x", "yh", "z")
CHIP_AXES = ("yl", "x", "yh", "z")
SWAP = [(0, 1), (1, 0)]


def dot(a, b, ca, cb):
    return lax.dot_general(a, b, (((ca,), (cb,)), ((), ())), preferred_element_type=F32)


def copies_kernel(g_ref, out, sems):
    copies = [pltpu.make_async_copy(g_ref, out.at[i], sems.at[i]) for i in range(32)]
    for copy in copies:
        copy.start()
    for copy in copies:
        copy.wait()


def copies_of(guide):
    return pl.pallas_call(
        copies_kernel,
        in_specs=[pl.BlockSpec(memory_space=pltpu.VMEM)],
        out_specs=pl.BlockSpec(memory_space=pl.ANY),
        out_shape=jax.ShapeDtypeStruct((32, *guide.shape), guide.dtype),
        scratch_shapes=[pltpu.SemaphoreType.DMA((32,))],
        name="copies_of_guide",
    )(guide)


def attention_kernel(
    img_ref, g_hbm, wk_hbm, wv_hbm, q_ref, d_ref, pay_hbm, o_ref, dq_ref,
    guide, wk, wv, k_scr, v_scr, pay, sems, out_sems,
):
    loads = [
        pltpu.make_async_copy(g_hbm.at[:, img_ref[0]], guide, sems.at[0]),
        pltpu.make_async_copy(wk_hbm, wk, sems.at[1]),
        pltpu.make_async_copy(wv_hbm, wv, sems.at[2]),
    ]
    for copy in loads:
        copy.start()
    loads[0].wait()
    tokens = guide[...].reshape(G, D)
    loads[1].wait()
    k_scr[...] = dot(tokens, wk[...], 1, 0).astype(BF16)
    loads[2].wait()
    v_scr[...] = dot(tokens, wv[...], 1, 0).astype(BF16)
    scale = HD ** (-0.5)
    flag = jnp.full((4, G), img_ref[0], jnp.int32).astype(F32)
    stores = []
    for h in range(HEADS):
        cols = slice(h * HD, (h + 1) * HD)
        q, d, k, v = q_ref[:, cols], d_ref[:, cols], k_scr[:, cols], v_scr[:, cols]
        scores = dot(q, k, 1, 1) * scale
        dprob = dot(d, v, 1, 1)
        top = jnp.max(scores, axis=-1, keepdims=True)
        expo = jnp.exp(scores - top)
        probs = expo * (1.0 / jnp.sum(expo, axis=-1, keepdims=True))
        pb = probs.astype(BF16)
        weighted = probs * dprob
        delta = jnp.sum(weighted, axis=-1, keepdims=True)
        ds = ((weighted - probs * delta) * scale).astype(BF16)
        o_ref[:, cols] = dot(pb, v, 1, 0).astype(BF16)
        dq_ref[:, cols] = dot(ds, k, 1, 0).astype(BF16)
        for j, part in enumerate((dot(q, ds, 0, 0), dot(d, pb, 0, 0))):
            for i in range(2):
                rows = jnp.concatenate([part[36 * i : 36 * i + 36], flag], axis=0)
                pay[2 * h + i, j] = rows.astype(BF16)
        two = pl.ds(2 * h, 2)
        stores.append(pltpu.make_async_copy(pay.at[two], pay_hbm.at[two], out_sems.at[h]))
        stores[-1].start()
    for copy in stores:
        copy.wait()


def attention(img, whole, w_key, w_value, q, d):
    t = q.shape[0]
    vmem = pl.BlockSpec(memory_space=pltpu.VMEM)
    hbm = pl.BlockSpec(memory_space=pl.ANY)
    return pl.pallas_call(
        attention_kernel,
        in_specs=[pl.BlockSpec(memory_space=pltpu.SMEM), hbm, hbm, hbm, vmem, vmem],
        out_specs=[hbm, vmem, vmem],
        out_shape=[
            jax.ShapeDtypeStruct((32, 2, 40, G), BF16),
            jax.ShapeDtypeStruct((t, D), BF16),
            jax.ShapeDtypeStruct((t, D), BF16),
        ],
        scratch_shapes=[
            pltpu.VMEM((32, 16, D), BF16),
            pltpu.VMEM((D, D), BF16),
            pltpu.VMEM((D, D), BF16),
            pltpu.VMEM((G, D), BF16),
            pltpu.VMEM((G, D), BF16),
            pltpu.VMEM((32, 2, 40, G), BF16),
            pltpu.SemaphoreType.DMA((3,)),
            pltpu.SemaphoreType.DMA((HEADS,)),
        ],
        name="attention",
    )(img, whole, w_key, w_value, q, d)


ROWS = 576


def eight_and_one(rows):
    return jnp.where(rows < 512, rows // 8 * 9 + rows % 8, (rows - 512) * 9 + 8)


def wanted_rows(core):
    row = eight_and_one(jnp.arange(ROWS, dtype=jnp.int32))
    return (row // 288 * 576 + core * 288 + row % 288)[:, None]


def one_hot(want, width):
    return (want == lax.broadcasted_iota(jnp.int32, (want.shape[0], width), 1)).astype(BF16)


EARLY = 640
SLOTS = [(row, lane) for lane in range(EARLY, D, 128) for row in range(8)]
GAINS = SLOTS[18:] + [(row, 512) for row in range(1, 5)]


def weight_parts_kernel(
    want_ref, hid_ref, o_ref, o2_ref, dq_ref, dq2_ref, g_ref, g2_ref, gain_ref, send_ref, scr
):
    o = jnp.concatenate([o_ref[...], o2_ref[...]], axis=0)
    dq = jnp.concatenate([dq_ref[...], dq2_ref[...]], axis=0)
    g = jnp.concatenate([g_ref[...], g2_ref[...]], axis=0)
    o_rows = dot(one_hot(want_ref[...], D), o, 1, 1).astype(BF16)
    parts = (dot(hid_ref[...], dq, 1, 0), dot(o_rows, g, 1, 0))
    for m, part in enumerate(parts):
        send_ref[:, m] = part[:512].reshape(64, 8, D).astype(BF16)
        for b in range(9):
            row, lane = SLOTS[9 * m + b]
            at = lane - EARLY
            scr[:, row, at : at + 128] = part[512:, 128 * b : 128 * b + 128]
    for b in range(14):
        row, lane = GAINS[b]
        at = lane - EARLY
        block = gain_ref[:, 128 * b : 128 * b + 128]
        scr[:, row, at : at + 128] = jnp.broadcast_to(block, (64, 128))
    send_ref[:, 2, :, EARLY:] = scr[...].astype(BF16)


def weight_parts(*args):
    vmem = pl.BlockSpec(memory_space=pltpu.VMEM)
    return pl.pallas_call(
        weight_parts_kernel,
        in_specs=[vmem] * 9,
        out_specs=vmem,
        out_shape=jax.ShapeDtypeStruct((64, 3, 8, D), BF16),
        scratch_shapes=[pltpu.VMEM((64, 8, D - EARLY), F32)],
        name="weight_parts",
    )(*args)


def image_sums_kernel(core_ref, got_hbm, g_hbm, mine_ref, theirs_ref, tok_ref, scr, got, guide, sems):
    loads = []
    for n in range(2):
        for part in range(2):
            some = pl.ds(16 * part, 16)
            sem = sems.at[2 * n + part]
            loads.append(pltpu.make_async_copy(got_hbm.at[some, n], got.at[n, some], sem))
    last = pltpu.make_async_copy(g_hbm, guide, sems.at[4])
    for copy in loads + [last]:
        copy.start()
    zero = jnp.zeros((40, G), F32)
    sums = [None, None]
    for n in range(2):

        def add(s, pair, n=n):
            terms = got[n, s].astype(F32)
            first = terms[36:37, :] == 0.0
            return pair[0] + jnp.where(first, terms, zero), pair[1] + jnp.where(first, zero, terms)

        pair = (zero, zero)
        for part in range(2):
            loads[2 * n + part].wait()
            pair = lax.fori_loop(16 * part, 16 * part + 16, add, pair)
        sums[n] = pair
    rounded = [jnp.concatenate([sums[0][m], sums[1][m]], axis=0).astype(BF16) for m in range(2)]
    last.wait()
    prod = dot(rounded[0], guide[:, 0].reshape(G, D), 1, 0)
    prod = prod + dot(rounded[1], guide[:, 1].reshape(G, D), 1, 0)
    scr[...] = jnp.concatenate([prod, jnp.zeros((48, D), F32)], axis=0).T
    core = core_ref[0]
    for n in range(2):
        for out, c in ((mine_ref, core), (theirs_ref, 1 - core)):
            start = pl.multiple_of(n * 576 + c * 288, 32)
            out[n * 288 : n * 288 + 288] = scr[pl.ds(start, 288), :]
    both = jnp.concatenate([x.astype(F32) for x in rounded] + [jnp.zeros((96, G), F32)], axis=0)
    tok_ref[...] = both.T


def image_sums(core, got, whole):
    vmem = pl.BlockSpec(memory_space=pltpu.VMEM)
    hbm = pl.BlockSpec(memory_space=pl.ANY)
    return pl.pallas_call(
        image_sums_kernel,
        in_specs=[pl.BlockSpec(memory_space=pltpu.SMEM), hbm, hbm],
        out_specs=[vmem] * 3,
        out_shape=[
            jax.ShapeDtypeStruct((ROWS, 128), F32),
            jax.ShapeDtypeStruct((ROWS, 128), F32),
            jax.ShapeDtypeStruct((G, 256), F32),
        ],
        scratch_shapes=[
            pltpu.VMEM((D, 128), F32),
            pltpu.VMEM((2, 32, 40, G), BF16),
            pltpu.VMEM((32, 2, 16, D), BF16),
            pltpu.SemaphoreType.DMA((5,)),
        ],
        name="image_sums",
    )(core, got, whole)


def fill_rest_kernel(send_ref, mine_ref, got_ref, tok_ref, gain_ref, out_ref, scr):
    scr[:, :, 512:EARLY] = jnp.zeros((64, 8, EARLY - 512), F32)
    total = mine_ref[...] + got_ref[...]
    high = total.astype(BF16)
    low = (total - high.astype(F32)).astype(BF16)
    want = eight_and_one(lax.broadcasted_iota(jnp.int32, (ROWS, ROWS), 0))
    order = (want == lax.broadcasted_iota(jnp.int32, (ROWS, ROWS), 1)).astype(BF16)
    moved = dot(order, jnp.concatenate([high, low], axis=1), 1, 0)
    tok = tok_ref[...].reshape(32, 16, 256)
    for half in range(2):
        lanes = slice(160 * half + 160, 160 * half + 320)
        for n in range(2):
            scr[32 * n : 32 * n + 32, :, lanes] = tok[:, 8 * half : 8 * half + 8, :160]
    for n in range(2):
        piece = moved[:, 128 * n : 128 * n + 80]
        scr[:, :, 80 * n : 80 * n + 80] = piece[:512].reshape(64, 8, 80)
        scr[:, 0, 480 + 80 * n : 560 + 80 * n] = piece[512:]
    for b in range(14, 18):
        row, lane = GAINS[b]
        block = gain_ref[:, 128 * b : 128 * b + 128]
        scr[:, row, lane : lane + 128] = jnp.broadcast_to(block, (64, 128))
    out_ref[:, 0] = scr[...].astype(BF16)


def fill_rest(send, mine, got, tok, gain):
    vmem = pl.BlockSpec(memory_space=pltpu.VMEM)
    return pl.pallas_call(
        fill_rest_kernel,
        grid=(1,),
        in_specs=[pl.BlockSpec(memory_space=pl.ANY)] + [vmem] * 4,
        out_specs=pl.BlockSpec((64, 1, 8, EARLY), lambda i: (0, 2, 0, 0)),
        out_shape=jax.ShapeDtypeStruct((64, 3, 8, D), BF16),
        scratch_shapes=[pltpu.VMEM((64, 8, EARLY), F32)],
        input_output_aliases={0: 0},
        name="fill_rest",
    )(send, mine, got, tok, gain)


def finish_kernel(
    yl_ref, recv_hbm, wk_hbm, wv_hbm, gw_ref, gg_ref, gain_ref, tok, kv, recv, wk, wv, sems
):
    loads = []
    for part in range(4):
        some = pl.ds(16 * part, 16)
        loads.append(pltpu.make_async_copy(recv_hbm.at[some], recv.at[some], sems.at[part]))
    late = [
        pltpu.make_async_copy(wk_hbm, wk, sems.at[4]),
        pltpu.make_async_copy(wv_hbm, wv, sems.at[5]),
    ]
    for copy in loads + late:
        copy.start()

    def add(j, sums):
        return tuple(s + recv[j, n].astype(F32) for n, s in enumerate(sums))

    sums = tuple(jnp.zeros((8, D), F32) for _ in range(3))
    for part in range(4):
        loads[part].wait()
        sums = lax.fori_loop(16 * part, 16 * part + 16, add, sums)
    gw_ref[:8, 0] = sums[0]
    gw_ref[:8, 3] = sums[1]

    def slot(place):
        row, lane = place
        return sums[2][row : row + 1, lane : lane + 128]

    for b in range(18):
        at = 128 * (b % 9)
        gw_ref[8:9, 3 * (b // 9), at : at + 128] = slot(SLOTS[b])
    for b in range(9):
        gain_ref[b : b + 1] = slot(GAINS[b]) + slot(GAINS[9 + b])
    base = yl_ref[0] * 32
    for t in range(32):
        cols = slice(36 * t, 36 * t + 36)
        x = recv[t, 2, :, :EARLY].astype(F32) + recv[32 + t, 2, :, :EARLY].astype(F32)
        eight = x[:, :80] + x[:, 80:160]
        one = x[:1, 480:560] + x[:1, 560:640]
        near = recv[base + t, 2, :, 128:512].astype(F32)
        for n in range(2):
            kv[n, :8, cols] = eight[:, 40 * n : 40 * n + 36]
            kv[n, 8:9, cols] = one[:, 40 * n : 40 * n + 36]
            for half in range(2):
                for m in range(2):
                    lane = 32 + 160 * half + 80 * m + 40 * n
                    row = 16 * m + 8 * half
                    tok[n, row : row + 8, cols] = near[:, lane : lane + 36]
    for n in range(2):
        gw_ref[:8, 1 + n] = kv[n, :8]
        gw_ref[8:9, 1 + n] = kv[n, 8:9]
    for copy in late:
        copy.wait()
    grad = dot(tok[0].astype(BF16), wk[...], 1, 1) + dot(tok[1].astype(BF16), wv[...], 1, 1)
    gg_ref[...] = grad.astype(BF16)


def finish(yl, recv, w_key, w_value):
    vmem = pl.BlockSpec(memory_space=pltpu.VMEM)
    hbm = pl.BlockSpec(memory_space=pl.ANY)
    return pl.pallas_call(
        finish_kernel,
        in_specs=[pl.BlockSpec(memory_space=pltpu.SMEM), hbm, hbm, hbm],
        out_specs=[vmem] * 3,
        out_shape=[
            jax.ShapeDtypeStruct((9, 4, D), F32),
            jax.ShapeDtypeStruct((32, D), BF16),
            jax.ShapeDtypeStruct((9, 128), F32),
        ],
        scratch_shapes=[
            pltpu.VMEM((2, 32, D), F32),
            pltpu.VMEM((2, 16, D), F32),
            pltpu.VMEM((64, 3, 8, D), BF16),
            pltpu.VMEM((D, D), BF16),
            pltpu.VMEM((D, D), BF16),
            pltpu.SemaphoreType.DMA((6,)),
        ],
        name="finish",
    )(yl, recv, w_key, w_value)


def on_device(tiles, tile_image, guide, gain, w_query, w_key, w_value, w_out, grad_out):
    core = lax.axis_index("c")
    yl = lax.axis_index("yl")
    whole = lax.all_to_all(copies_of(guide), TILE_AXES, 0, 0, tiled=True)
    xf = tiles.astype(F32)
    rstd = lax.rsqrt(jnp.mean(xf * xf, axis=-1, keepdims=True) + 1e-06)
    normed = xf * rstd
    hidden = (normed * gain).astype(BF16)
    query = dot(hidden, w_query, 1, 0).astype(BF16)
    dout = dot(grad_out, w_out, 1, 1).astype(BF16)
    want = wanted_rows(core)
    hid_both = jnp.concatenate([hidden, lax.ppermute(hidden, "c", SWAP)], axis=0)
    hid_rows = dot(one_hot(want, D), hid_both, 1, 1).astype(BF16)
    grad_got = lax.ppermute(grad_out, "c", SWAP)
    query, hid_rows = lax.optimization_barrier((query, hid_rows))

    pay, outv, dq = attention(tile_image, whole, w_key, w_value, query, dout)
    got = lax.all_to_all(pay, TILE_AXES, 0, 0, tiled=True)

    dq_got = lax.ppermute(dq, "c", SWAP)
    out_got = lax.ppermute(outv, "c", SWAP)
    dh = dot(dq, w_query, 1, 1)
    gain_part = jnp.sum(dh * normed, axis=0, keepdims=True)
    gain_part = gain_part + lax.ppermute(gain_part, "c", SWAP)
    gain_high = lax.reduce_precision(gain_part, 8, 7)
    gains = jnp.concatenate([gain_high, gain_part - gain_high], axis=1)
    send = weight_parts(
        want, hid_rows, outv, out_got, dq, dq_got, grad_out, grad_got, gains
    )
    dn = dh * gain
    grad_tiles = (rstd * (dn - normed * jnp.mean(dn * normed, axis=-1, keepdims=True))).astype(BF16)

    got, send = lax.optimization_barrier((got, send))
    mine, theirs, tok = image_sums(core[None], got, whole)
    send = fill_rest(send, mine, lax.ppermute(theirs, "c", SWAP), tok, gains)
    recv = lax.all_to_all(send, CHIP_AXES, 0, 0, tiled=True)
    grad_weights, grad_guide, grad_gain = finish(yl[None], recv, w_key, w_value)
    grad_weights = grad_weights.transpose(1, 0, 2)
    return (grad_tiles, grad_guide.reshape(guide.shape), grad_weights, grad_gain.reshape(D))


def solution(mesh):
    fine = Mesh(mesh.devices.reshape(2, 2, 4, 2, 4), ("yl", "c", "x", "yh", "z"))
    every = ("yl", "c", "x", "yh", "z")
    return jax.shard_map(
        on_device,
        mesh=fine,
        in_specs=(
            P(every, None),
            P(every),
            P(("yl", "c"), TILE_AXES, None),
            P(),
            P(),
            P(),
            P(),
            P(),
            P(every, None),
        ),
        out_specs=(
            P(every, None),
            P(("yl", "c"), TILE_AXES, None),
            P(None, every, None),
            P(),
        ),
        check_vma=False,
    )
```

```python
import jax
import jax.numpy as jnp
from jax import lax
from jax.experimental import pallas as pl
from jax.experimental.pallas import tpu as pltpu
from jax.sharding import Mesh, PartitionSpec as P

HEADS = 16
HD = 72
D = 1152
G = 512
F32 = jnp.float32
BF16 = jnp.bfloat16
TILE_AXES = ("x", "yh", "z")
CHIP_AXES = ("yl", "x", "yh", "z")
SWAP = [(0, 1), (1, 0)]


def dot(a, b, ca, cb):
    return lax.dot_general(a, b, (((ca,), (cb,)), ((), ())), preferred_element_type=F32)


def copies_kernel(g_ref, out):
    for i in range(32):
        out[i] = g_ref[...]


def copies_of(guide):
    vmem = pl.BlockSpec(memory_space=pltpu.VMEM)
    return pl.pallas_call(
        copies_kernel,
        in_specs=[vmem],
        out_specs=vmem,
        out_shape=pltpu.VMEM((32, *guide.shape), guide.dtype),
        name="copies_of_guide",
    )(guide)


def attention_kernel(
    img_ref, g_hbm, wk_hbm, wv_hbm, q_ref, d_ref, pay_hbm, o_ref, dq_ref,
    guide, wk, wv, k_scr, v_scr, pay, sems, out_sems,
):
    loads = [
        pltpu.make_async_copy(g_hbm.at[:, img_ref[0]], guide, sems.at[0]),
        pltpu.make_async_copy(wk_hbm, wk, sems.at[1]),
        pltpu.make_async_copy(wv_hbm, wv, sems.at[2]),
    ]
    for copy in loads:
        copy.start()
    loads[0].wait()
    tokens = guide[...].reshape(G, D)
    loads[1].wait()
    k_scr[...] = dot(tokens, wk[...], 1, 0).astype(BF16)
    loads[2].wait()
    v_scr[...] = dot(tokens, wv[...], 1, 0).astype(BF16)
    scale = HD ** (-0.5)
    flag = jnp.full((4, G), img_ref[0], jnp.int32).astype(F32)
    stores = []
    t = q_ref.shape[0]
    lane = lax.broadcasted_iota(jnp.int32, (t, 2 * HD), 1)
    none = jnp.zeros((t, 2 * HD), BF16)
    for h in range(0, HEADS, 2):
        cols = slice(h * HD, (h + 2) * HD)
        k, v = k_scr[:, cols], v_scr[:, cols]

        def both(x):
            return jnp.concatenate([jnp.where(lane < HD, x, none), jnp.where(lane < HD, none, x)], axis=0)

        def own(x):
            return jnp.where(lane < HD, x[:t], x[t:]).astype(BF16)

        q, d = both(q_ref[:, cols]), both(d_ref[:, cols])
        scores = dot(q, k, 1, 1) * scale
        dprob = dot(d, v, 1, 1)
        top = jnp.max(scores, axis=-1, keepdims=True)
        expo = jnp.exp(scores - top)
        probs = expo * (1.0 / jnp.sum(expo, axis=-1, keepdims=True))
        pb = probs.astype(BF16)
        weighted = probs * dprob
        delta = jnp.sum(weighted, axis=-1, keepdims=True)
        ds = ((weighted - probs * delta) * scale).astype(BF16)
        o_ref[:, cols] = own(dot(pb, v, 1, 0))
        dq_ref[:, cols] = own(dot(ds, k, 1, 0))
        for j, part in enumerate((dot(q, ds, 0, 0), dot(d, pb, 0, 0))):
            for i in range(4):
                rows = jnp.concatenate([part[36 * i : 36 * i + 36], flag], axis=0)
                pay[2 * h + i, j] = rows.astype(BF16)
        some = pl.ds(2 * h, 4)
        stores.append(pltpu.make_async_copy(pay.at[some], pay_hbm.at[some], out_sems.at[h // 2]))
        stores[-1].start()
    for copy in stores:
        copy.wait()


def attention(img, whole, w_key, w_value, q, d):
    t = q.shape[0]
    vmem = pl.BlockSpec(memory_space=pltpu.VMEM)
    hbm = pl.BlockSpec(memory_space=pl.ANY)
    return pl.pallas_call(
        attention_kernel,
        in_specs=[pl.BlockSpec(memory_space=pltpu.SMEM), hbm, hbm, hbm, vmem, vmem],
        out_specs=[hbm, vmem, vmem],
        out_shape=[
            jax.ShapeDtypeStruct((32, 2, 40, G), BF16),
            jax.ShapeDtypeStruct((t, D), BF16),
            jax.ShapeDtypeStruct((t, D), BF16),
        ],
        scratch_shapes=[
            pltpu.VMEM((32, 16, D), BF16),
            pltpu.VMEM((D, D), BF16),
            pltpu.VMEM((D, D), BF16),
            pltpu.VMEM((G, D), BF16),
            pltpu.VMEM((G, D), BF16),
            pltpu.VMEM((32, 2, 40, G), BF16),
            pltpu.SemaphoreType.DMA((3,)),
            pltpu.SemaphoreType.DMA((HEADS // 2,)),
        ],
        name="attention",
    )(img, whole, w_key, w_value, q, d)


ROWS = 576


def eight_and_one(rows):
    return jnp.where(rows < 512, rows // 8 * 9 + rows % 8, (rows - 512) * 9 + 8)


def wanted_rows(core):
    row = eight_and_one(jnp.arange(ROWS, dtype=jnp.int32))
    return (row // 288 * 576 + core * 288 + row % 288)[:, None]


def one_hot(want, width):
    return (want == lax.broadcasted_iota(jnp.int32, (want.shape[0], width), 1)).astype(BF16)


EARLY = 640
SLOTS = [(row, lane) for lane in range(EARLY, D, 128) for row in range(8)]
GAINS = SLOTS[18:] + [(row, 512) for row in range(1, 5)]


def weight_parts_kernel(
    want_ref, hid_ref, o_ref, o2_ref, dq_ref, dq2_ref, g_ref, g2_ref, gain_ref, send_ref, scr
):
    o = jnp.concatenate([o_ref[...], o2_ref[...]], axis=0)
    dq = jnp.concatenate([dq_ref[...], dq2_ref[...]], axis=0)
    g = jnp.concatenate([g_ref[...], g2_ref[...]], axis=0)
    o_rows = dot(one_hot(want_ref[...], D), o, 1, 1).astype(BF16)
    parts = (dot(hid_ref[...], dq, 1, 0), dot(o_rows, g, 1, 0))
    for m, part in enumerate(parts):
        send_ref[:, m] = part[:512].reshape(64, 8, D).astype(BF16)
        for b in range(9):
            row, lane = SLOTS[9 * m + b]
            at = lane - EARLY
            scr[:, row, at : at + 128] = part[512:, 128 * b : 128 * b + 128]
    for b in range(14):
        row, lane = GAINS[b]
        at = lane - EARLY
        block = gain_ref[:, 128 * b : 128 * b + 128]
        scr[:, row, at : at + 128] = jnp.broadcast_to(block, (64, 128))
    send_ref[:, 2, :, EARLY:] = scr[...].astype(BF16)


def weight_parts(*args):
    vmem = pl.BlockSpec(memory_space=pltpu.VMEM)
    return pl.pallas_call(
        weight_parts_kernel,
        in_specs=[vmem] * 9,
        out_specs=vmem,
        out_shape=jax.ShapeDtypeStruct((64, 3, 8, D), BF16),
        scratch_shapes=[pltpu.VMEM((64, 8, D - EARLY), F32)],
        name="weight_parts",
    )(*args)


def image_sums_kernel(core_ref, got_hbm, g_hbm, mine_ref, theirs_ref, tok_ref, scr, got, guide, sems):
    loads = []
    for n in range(2):
        for part in range(2):
            some = pl.ds(16 * part, 16)
            sem = sems.at[2 * n + part]
            loads.append(pltpu.make_async_copy(got_hbm.at[some, n], got.at[n, some], sem))
    last = pltpu.make_async_copy(g_hbm, guide, sems.at[4])
    for copy in loads + [last]:
        copy.start()
    zero = jnp.zeros((40, G), F32)
    sums = [None, None]
    for n in range(2):

        def add(s, pair, n=n):
            terms = got[n, s].astype(F32)
            first = terms[36:37, :] == 0.0
            return pair[0] + jnp.where(first, terms, zero), pair[1] + jnp.where(first, zero, terms)

        pair = (zero, zero)
        for part in range(2):
            loads[2 * n + part].wait()
            pair = lax.fori_loop(16 * part, 16 * part + 16, add, pair)
        sums[n] = pair
    rounded = [jnp.concatenate([sums[0][m], sums[1][m]], axis=0).astype(BF16) for m in range(2)]
    last.wait()
    prod = dot(rounded[0], guide[:, 0].reshape(G, D), 1, 0)
    prod = prod + dot(rounded[1], guide[:, 1].reshape(G, D), 1, 0)
    scr[...] = jnp.concatenate([prod, jnp.zeros((48, D), F32)], axis=0).T
    core = core_ref[0]
    for n in range(2):
        for out, c in ((mine_ref, core), (theirs_ref, 1 - core)):
            start = pl.multiple_of(n * 576 + c * 288, 32)
            out[n * 288 : n * 288 + 288] = scr[pl.ds(start, 288), :]
    both = jnp.concatenate([x.astype(F32) for x in rounded] + [jnp.zeros((96, G), F32)], axis=0)
    tok_ref[...] = both.T


def image_sums(core, got, whole):
    vmem = pl.BlockSpec(memory_space=pltpu.VMEM)
    hbm = pl.BlockSpec(memory_space=pl.ANY)
    return pl.pallas_call(
        image_sums_kernel,
        in_specs=[pl.BlockSpec(memory_space=pltpu.SMEM), hbm, hbm],
        out_specs=[vmem] * 3,
        out_shape=[
            jax.ShapeDtypeStruct((ROWS, 128), F32),
            jax.ShapeDtypeStruct((ROWS, 128), F32),
            jax.ShapeDtypeStruct((G, 256), F32),
        ],
        scratch_shapes=[
            pltpu.VMEM((D, 128), F32),
            pltpu.VMEM((2, 32, 40, G), BF16),
            pltpu.VMEM((32, 2, 16, D), BF16),
            pltpu.SemaphoreType.DMA((5,)),
        ],
        name="image_sums",
    )(core, got, whole)


def fill_rest_kernel(send_ref, mine_ref, got_ref, tok_ref, gain_ref, out_ref, scr):
    scr[:, :, 512:EARLY] = jnp.zeros((64, 8, EARLY - 512), F32)
    total = mine_ref[...] + got_ref[...]
    high = total.astype(BF16)
    low = (total - high.astype(F32)).astype(BF16)
    want = eight_and_one(lax.broadcasted_iota(jnp.int32, (ROWS, ROWS), 0))
    order = (want == lax.broadcasted_iota(jnp.int32, (ROWS, ROWS), 1)).astype(BF16)
    moved = dot(order, jnp.concatenate([high, low], axis=1), 1, 0)
    tok = tok_ref[...].reshape(32, 16, 256)
    for half in range(2):
        lanes = slice(160 * half + 160, 160 * half + 320)
        for n in range(2):
            scr[32 * n : 32 * n + 32, :, lanes] = tok[:, 8 * half : 8 * half + 8, :160]
    for n in range(2):
        piece = moved[:, 128 * n : 128 * n + 80]
        scr[:, :, 80 * n : 80 * n + 80] = piece[:512].reshape(64, 8, 80)
        scr[:, 0, 480 + 80 * n : 560 + 80 * n] = piece[512:]
    for b in range(14, 18):
        row, lane = GAINS[b]
        block = gain_ref[:, 128 * b : 128 * b + 128]
        scr[:, row, lane : lane + 128] = jnp.broadcast_to(block, (64, 128))
    out_ref[:, 0] = scr[...].astype(BF16)


def fill_rest(send, mine, got, tok, gain):
    vmem = pl.BlockSpec(memory_space=pltpu.VMEM)
    return pl.pallas_call(
        fill_rest_kernel,
        grid=(1,),
        in_specs=[pl.BlockSpec(memory_space=pl.ANY)] + [vmem] * 4,
        out_specs=pl.BlockSpec((64, 1, 8, EARLY), lambda i: (0, 2, 0, 0)),
        out_shape=jax.ShapeDtypeStruct((64, 3, 8, D), BF16),
        scratch_shapes=[pltpu.VMEM((64, 8, EARLY), F32)],
        input_output_aliases={0: 0},
        name="fill_rest",
    )(send, mine, got, tok, gain)


def finish_kernel(
    yl_ref, recv_hbm, wk_hbm, wv_hbm, gw_ref, gg_ref, gain_ref, tok, kv, recv, wk, wv, sems
):
    loads = []
    for part in range(4):
        some = pl.ds(16 * part, 16)
        loads.append(pltpu.make_async_copy(recv_hbm.at[some], recv.at[some], sems.at[part]))
    late = [
        pltpu.make_async_copy(wk_hbm, wk, sems.at[4]),
        pltpu.make_async_copy(wv_hbm, wv, sems.at[5]),
    ]
    for copy in loads + late:
        copy.start()

    def add(j, sums):
        return tuple(s + recv[j, n].astype(F32) for n, s in enumerate(sums))

    sums = tuple(jnp.zeros((8, D), F32) for _ in range(3))
    for part in range(4):
        loads[part].wait()
        sums = lax.fori_loop(16 * part, 16 * part + 16, add, sums)
    gw_ref[:8, 0] = sums[0]
    gw_ref[:8, 3] = sums[1]

    def slot(place):
        row, lane = place
        return sums[2][row : row + 1, lane : lane + 128]

    for b in range(18):
        at = 128 * (b % 9)
        gw_ref[8:9, 3 * (b // 9), at : at + 128] = slot(SLOTS[b])
    for b in range(9):
        gain_ref[b : b + 1] = slot(GAINS[b]) + slot(GAINS[9 + b])
    base = yl_ref[0] * 32
    for t in range(32):
        cols = slice(36 * t, 36 * t + 36)
        x = recv[t, 2, :, :EARLY].astype(F32) + recv[32 + t, 2, :, :EARLY].astype(F32)
        eight = x[:, :80] + x[:, 80:160]
        one = x[:1, 480:560] + x[:1, 560:640]
        near = recv[base + t, 2, :, 128:512].astype(F32)
        for n in range(2):
            kv[n, :8, cols] = eight[:, 40 * n : 40 * n + 36]
            kv[n, 8:9, cols] = one[:, 40 * n : 40 * n + 36]
            for half in range(2):
                for m in range(2):
                    lane = 32 + 160 * half + 80 * m + 40 * n
                    row = 16 * m + 8 * half
                    tok[n, row : row + 8, cols] = near[:, lane : lane + 36]
    for n in range(2):
        gw_ref[:8, 1 + n] = kv[n, :8]
        gw_ref[8:9, 1 + n] = kv[n, 8:9]
    for copy in late:
        copy.wait()
    grad = dot(tok[0].astype(BF16), wk[...], 1, 1) + dot(tok[1].astype(BF16), wv[...], 1, 1)
    gg_ref[...] = grad.astype(BF16)


def finish(yl, recv, w_key, w_value):
    vmem = pl.BlockSpec(memory_space=pltpu.VMEM)
    hbm = pl.BlockSpec(memory_space=pl.ANY)
    return pl.pallas_call(
        finish_kernel,
        in_specs=[pl.BlockSpec(memory_space=pltpu.SMEM), hbm, hbm, hbm],
        out_specs=[vmem] * 3,
        out_shape=[
            jax.ShapeDtypeStruct((9, 4, D), F32),
            jax.ShapeDtypeStruct((32, D), BF16),
            jax.ShapeDtypeStruct((9, 128), F32),
        ],
        scratch_shapes=[
            pltpu.VMEM((2, 32, D), F32),
            pltpu.VMEM((2, 16, D), F32),
            pltpu.VMEM((64, 3, 8, D), BF16),
            pltpu.VMEM((D, D), BF16),
            pltpu.VMEM((D, D), BF16),
            pltpu.SemaphoreType.DMA((6,)),
        ],
        name="finish",
    )(yl, recv, w_key, w_value)


def on_device(tiles, tile_image, guide, gain, w_query, w_key, w_value, w_out, grad_out):
    core = lax.axis_index("c")
    yl = lax.axis_index("yl")
    whole = lax.all_to_all(copies_of(guide), TILE_AXES, 0, 0, tiled=True)
    xf = tiles.astype(F32)
    rstd = lax.rsqrt(jnp.mean(xf * xf, axis=-1, keepdims=True) + 1e-06)
    normed = xf * rstd
    hidden = (normed * gain).astype(BF16)
    query = dot(hidden, w_query, 1, 0).astype(BF16)
    dout = dot(grad_out, w_out, 1, 1).astype(BF16)
    want = wanted_rows(core)
    hid_both = jnp.concatenate([hidden, lax.ppermute(hidden, "c", SWAP)], axis=0)
    hid_rows = dot(one_hot(want, D), hid_both, 1, 1).astype(BF16)
    grad_got = lax.ppermute(grad_out, "c", SWAP)
    query, hid_rows = lax.optimization_barrier((query, hid_rows))

    pay, outv, dq = attention(tile_image, whole, w_key, w_value, query, dout)
    got = lax.all_to_all(pay, TILE_AXES, 0, 0, tiled=True)

    dq_got = lax.ppermute(dq, "c", SWAP)
    out_got = lax.ppermute(outv, "c", SWAP)
    dh = dot(dq, w_query, 1, 1)
    gain_part = jnp.sum(dh * normed, axis=0, keepdims=True)
    gain_part = gain_part + lax.ppermute(gain_part, "c", SWAP)
    gain_high = lax.reduce_precision(gain_part, 8, 7)
    gains = jnp.concatenate([gain_high, gain_part - gain_high], axis=1)
    send = weight_parts(
        want, hid_rows, outv, out_got, dq, dq_got, grad_out, grad_got, gains
    )
    dn = dh * gain
    grad_tiles = (rstd * (dn - normed * jnp.mean(dn * normed, axis=-1, keepdims=True))).astype(BF16)

    got, send = lax.optimization_barrier((got, send))
    mine, theirs, tok = image_sums(core[None], got, whole)
    send = fill_rest(send, mine, lax.ppermute(theirs, "c", SWAP), tok, gains)
    recv = lax.all_to_all(send, CHIP_AXES, 0, 0, tiled=True)
    grad_weights, grad_guide, grad_gain = finish(yl[None], recv, w_key, w_value)
    grad_weights = grad_weights.transpose(1, 0, 2)
    return (grad_tiles, grad_guide.reshape(guide.shape), grad_weights, grad_gain.reshape(D))


def solution(mesh):
    fine = Mesh(mesh.devices.reshape(2, 2, 4, 2, 4), ("yl", "c", "x", "yh", "z"))
    every = ("yl", "c", "x", "yh", "z")
    return jax.shard_map(
        on_device,
        mesh=fine,
        in_specs=(
            P(every, None),
            P(every),
            P(("yl", "c"), TILE_AXES, None),
            P(),
            P(),
            P(),
            P(),
            P(),
            P(every, None),
        ),
        out_specs=(
            P(every, None),
            P(("yl", "c"), TILE_AXES, None),
            P(None, every, None),
            P(),
        ),
        check_vma=False,
    )
```

```python
import jax
import jax.numpy as jnp
from jax import lax
from jax.experimental import pallas as pl
from jax.experimental.pallas import tpu as pltpu
from jax.sharding import Mesh, PartitionSpec as P

HEADS = 16
HD = 72
D = 1152
G = 512
F32 = jnp.float32
BF16 = jnp.bfloat16
TILE_AXES = ("x", "yh", "z")
CHIP_AXES = ("yl", "x", "yh", "z")
SWAP = [(0, 1), (1, 0)]


def dot(a, b, ca, cb):
    return lax.dot_general(a, b, (((ca,), (cb,)), ((), ())), preferred_element_type=F32)


def copies_kernel(g_ref, out, sems):
    copies = [pltpu.make_async_copy(g_ref, out.at[i], sems.at[i]) for i in range(32)]
    for copy in copies:
        copy.start()
    for copy in copies:
        copy.wait()


def copies_of(guide):
    return pl.pallas_call(
        copies_kernel,
        in_specs=[pl.BlockSpec(memory_space=pltpu.VMEM)],
        out_specs=pl.BlockSpec(memory_space=pl.ANY),
        out_shape=jax.ShapeDtypeStruct((32, *guide.shape), guide.dtype),
        scratch_shapes=[pltpu.SemaphoreType.DMA((32,))],
        name="copies_of_guide",
    )(guide)


def attention_kernel(
    img_ref, g_hbm, wk_hbm, wv_hbm, q_ref, d_ref, pay_hbm, o_ref, dq_ref,
    guide, wk, wv, k_scr, v_scr, pay, sems, out_sems,
):
    loads = [
        pltpu.make_async_copy(g_hbm.at[:, img_ref[0]], guide, sems.at[0]),
        pltpu.make_async_copy(wk_hbm, wk, sems.at[1]),
        pltpu.make_async_copy(wv_hbm, wv, sems.at[2]),
    ]
    for copy in loads:
        copy.start()
    loads[0].wait()
    tokens = guide[...].reshape(G, D)
    loads[1].wait()
    k_scr[...] = dot(tokens, wk[...], 1, 0).astype(BF16)
    loads[2].wait()
    v_scr[...] = dot(tokens, wv[...], 1, 0).astype(BF16)
    scale = HD ** (-0.5)
    flag = jnp.full((4, G), img_ref[0], jnp.int32).astype(F32)
    stores = []
    t = q_ref.shape[0]
    lane = lax.broadcasted_iota(jnp.int32, (t, 2 * HD), 1)
    none = jnp.zeros((t, 2 * HD), BF16)
    for h in range(0, HEADS, 2):
        cols = slice(h * HD, (h + 2) * HD)
        k, v = k_scr[:, cols], v_scr[:, cols]

        def both(x):
            return jnp.concatenate([jnp.where(lane < HD, x, none), jnp.where(lane < HD, none, x)], axis=0)

        def own(x):
            return jnp.where(lane < HD, x[:t], x[t:]).astype(BF16)

        q, d = both(q_ref[:, cols]), both(d_ref[:, cols])
        scores = dot(q, k, 1, 1) * scale
        dprob = dot(d, v, 1, 1)
        top = jnp.max(scores, axis=-1, keepdims=True)
        expo = jnp.exp(scores - top)
        probs = expo * (1.0 / jnp.sum(expo, axis=-1, keepdims=True))
        pb = probs.astype(BF16)
        weighted = probs * dprob
        delta = jnp.sum(weighted, axis=-1, keepdims=True)
        ds = ((weighted - probs * delta) * scale).astype(BF16)
        o_ref[:, cols] = own(dot(pb, v, 1, 0))
        dq_ref[:, cols] = own(dot(ds, k, 1, 0))
        for j, part in enumerate((dot(q, ds, 0, 0), dot(d, pb, 0, 0))):
            for i in range(4):
                rows = jnp.concatenate([part[36 * i : 36 * i + 36], flag], axis=0)
                pay[2 * h + i, j] = rows.astype(BF16)
        some = pl.ds(2 * h, 4)
        stores.append(pltpu.make_async_copy(pay.at[some], pay_hbm.at[some], out_sems.at[h // 2]))
        stores[-1].start()
    for copy in stores:
        copy.wait()


def attention(img, whole, w_key, w_value, q, d):
    t = q.shape[0]
    vmem = pl.BlockSpec(memory_space=pltpu.VMEM)
    hbm = pl.BlockSpec(memory_space=pl.ANY)
    return pl.pallas_call(
        attention_kernel,
        in_specs=[pl.BlockSpec(memory_space=pltpu.SMEM), hbm, hbm, hbm, vmem, vmem],
        out_specs=[hbm, vmem, vmem],
        out_shape=[
            jax.ShapeDtypeStruct((32, 2, 40, G), BF16),
            jax.ShapeDtypeStruct((t, D), BF16),
            jax.ShapeDtypeStruct((t, D), BF16),
        ],
        scratch_shapes=[
            pltpu.VMEM((32, 16, D), BF16),
            pltpu.VMEM((D, D), BF16),
            pltpu.VMEM((D, D), BF16),
            pltpu.VMEM((G, D), BF16),
            pltpu.VMEM((G, D), BF16),
            pltpu.VMEM((32, 2, 40, G), BF16),
            pltpu.SemaphoreType.DMA((3,)),
            pltpu.SemaphoreType.DMA((HEADS // 2,)),
        ],
        name="attention",
    )(img, whole, w_key, w_value, q, d)


ROWS = 576


def eight_and_one(rows):
    return jnp.where(rows < 512, rows // 8 * 9 + rows % 8, (rows - 512) * 9 + 8)


def wanted_rows(core):
    row = eight_and_one(jnp.arange(ROWS, dtype=jnp.int32))
    return (row // 288 * 576 + core * 288 + row % 288)[:, None]


def one_hot(want, width):
    return (want == lax.broadcasted_iota(jnp.int32, (want.shape[0], width), 1)).astype(BF16)


EARLY = 640
SLOTS = [(row, lane) for lane in range(EARLY, D, 128) for row in range(8)]
GAINS = SLOTS[18:] + [(row, 512) for row in range(1, 5)]


def weight_parts_kernel(
    want_ref, hid_ref, o_ref, o2_ref, dq_ref, dq2_ref, g_ref, g2_ref, gain_ref, send_ref, scr
):
    o = jnp.concatenate([o_ref[...], o2_ref[...]], axis=0)
    dq = jnp.concatenate([dq_ref[...], dq2_ref[...]], axis=0)
    g = jnp.concatenate([g_ref[...], g2_ref[...]], axis=0)
    o_rows = dot(one_hot(want_ref[...], D), o, 1, 1).astype(BF16)
    parts = (dot(hid_ref[...], dq, 1, 0), dot(o_rows, g, 1, 0))
    for m, part in enumerate(parts):
        send_ref[:, m] = part[:512].reshape(64, 8, D).astype(BF16)
        for b in range(9):
            row, lane = SLOTS[9 * m + b]
            at = lane - EARLY
            scr[:, row, at : at + 128] = part[512:, 128 * b : 128 * b + 128]
    for b in range(14):
        row, lane = GAINS[b]
        at = lane - EARLY
        block = gain_ref[:, 128 * b : 128 * b + 128]
        scr[:, row, at : at + 128] = jnp.broadcast_to(block, (64, 128))
    send_ref[:, 2, :, EARLY:] = scr[...].astype(BF16)


def weight_parts(*args):
    vmem = pl.BlockSpec(memory_space=pltpu.VMEM)
    return pl.pallas_call(
        weight_parts_kernel,
        in_specs=[vmem] * 9,
        out_specs=vmem,
        out_shape=jax.ShapeDtypeStruct((64, 3, 8, D), BF16),
        scratch_shapes=[pltpu.VMEM((64, 8, D - EARLY), F32)],
        name="weight_parts",
    )(*args)


def image_sums_kernel(core_ref, got_hbm, g_hbm, mine_ref, theirs_ref, tok_ref, scr, got, guide, sems):
    loads = []
    for n in range(2):
        for part in range(2):
            some = pl.ds(16 * part, 16)
            sem = sems.at[2 * n + part]
            loads.append(pltpu.make_async_copy(got_hbm.at[some, n], got.at[n, some], sem))
    last = pltpu.make_async_copy(g_hbm, guide, sems.at[4])
    for copy in loads + [last]:
        copy.start()
    zero = jnp.zeros((40, G), F32)
    sums = [None, None]
    for n in range(2):

        def add(s, pair, n=n):
            terms = got[n, s].astype(F32)
            first = terms[36:37, :] == 0.0
            return pair[0] + jnp.where(first, terms, zero), pair[1] + jnp.where(first, zero, terms)

        pair = (zero, zero)
        for part in range(2):
            loads[2 * n + part].wait()
            pair = lax.fori_loop(16 * part, 16 * part + 16, add, pair)
        sums[n] = pair
    rounded = [jnp.concatenate([sums[0][m], sums[1][m]], axis=0).astype(BF16) for m in range(2)]
    last.wait()
    prod = dot(rounded[0], guide[:, 0].reshape(G, D), 1, 0)
    prod = prod + dot(rounded[1], guide[:, 1].reshape(G, D), 1, 0)
    scr[...] = jnp.concatenate([prod, jnp.zeros((48, D), F32)], axis=0).T
    core = core_ref[0]
    for n in range(2):
        for out, c in ((mine_ref, core), (theirs_ref, 1 - core)):
            start = pl.multiple_of(n * 576 + c * 288, 32)
            out[n * 288 : n * 288 + 288] = scr[pl.ds(start, 288), :]
    tok_ref[:80] = rounded[0]
    tok_ref[80:] = rounded[1]


def image_sums(core, got, whole):
    vmem = pl.BlockSpec(memory_space=pltpu.VMEM)
    hbm = pl.BlockSpec(memory_space=pl.ANY)
    return pl.pallas_call(
        image_sums_kernel,
        in_specs=[pl.BlockSpec(memory_space=pltpu.SMEM), hbm, hbm],
        out_specs=[vmem] * 3,
        out_shape=[
            jax.ShapeDtypeStruct((ROWS, 128), F32),
            jax.ShapeDtypeStruct((ROWS, 128), F32),
            jax.ShapeDtypeStruct((160, G), BF16),
        ],
        scratch_shapes=[
            pltpu.VMEM((D, 128), F32),
            pltpu.VMEM((2, 32, 40, G), BF16),
            pltpu.VMEM((32, 2, 16, D), BF16),
            pltpu.SemaphoreType.DMA((5,)),
        ],
        name="image_sums",
    )(core, got, whole)


def fill_tokens_kernel(tok_ref, gain_ref, out_ref):
    out_ref[:, :, 512:EARLY] = jnp.zeros((64, 8, EARLY - 512), F32)
    rows = jnp.concatenate([tok_ref[...].astype(F32), jnp.zeros((96, G), F32)], axis=0)
    tok = rows.T.reshape(32, 16, 256)
    for half in range(2):
        lanes = slice(160 * half + 160, 160 * half + 320)
        for n in range(2):
            out_ref[32 * n : 32 * n + 32, :, lanes] = tok[:, 8 * half : 8 * half + 8, :160]
    for b in range(14, 18):
        row, lane = GAINS[b]
        block = gain_ref[:, 128 * b : 128 * b + 128]
        out_ref[:, row, lane : lane + 128] = jnp.broadcast_to(block, (64, 128))


def fill_tokens(tok, gain):
    vmem = pl.BlockSpec(memory_space=pltpu.VMEM)
    return pl.pallas_call(
        fill_tokens_kernel,
        in_specs=[vmem] * 2,
        out_specs=vmem,
        out_shape=jax.ShapeDtypeStruct((64, 8, EARLY), F32),
        name="fill_tokens",
    )(tok, gain)


def fill_rest_kernel(send_ref, mine_ref, got_ref, part_ref, out_ref, scr):
    total = mine_ref[...] + got_ref[...]
    high = total.astype(BF16)
    low = (total - high.astype(F32)).astype(BF16)
    want = eight_and_one(lax.broadcasted_iota(jnp.int32, (ROWS, ROWS), 0))
    order = (want == lax.broadcasted_iota(jnp.int32, (ROWS, ROWS), 1)).astype(BF16)
    moved = dot(order, jnp.concatenate([high, low], axis=1), 1, 0)
    scr[...] = part_ref[...]
    for n in range(2):
        piece = moved[:, 128 * n : 128 * n + 80]
        scr[:, :, 80 * n : 80 * n + 80] = piece[:512].reshape(64, 8, 80)
        scr[:, 0, 480 + 80 * n : 560 + 80 * n] = piece[512:]
    out_ref[:, 0] = scr[...].astype(BF16)


def fill_rest(send, mine, got, part):
    vmem = pl.BlockSpec(memory_space=pltpu.VMEM)
    return pl.pallas_call(
        fill_rest_kernel,
        grid=(1,),
        in_specs=[pl.BlockSpec(memory_space=pl.ANY)] + [vmem] * 3,
        out_specs=pl.BlockSpec((64, 1, 8, EARLY), lambda i: (0, 2, 0, 0)),
        out_shape=jax.ShapeDtypeStruct((64, 3, 8, D), BF16),
        scratch_shapes=[pltpu.VMEM((64, 8, EARLY), F32)],
        input_output_aliases={0: 0},
        name="fill_rest",
    )(send, mine, got, part)


def finish_kernel(
    yl_ref, recv_hbm, wk_hbm, wv_hbm, gw_ref, gg_ref, gain_ref, tok, kv, recv, wk, wv, sems
):
    loads = []
    for part in range(4):
        some = pl.ds(16 * part, 16)
        loads.append(pltpu.make_async_copy(recv_hbm.at[some], recv.at[some], sems.at[part]))
    late = [
        pltpu.make_async_copy(wk_hbm, wk, sems.at[4]),
        pltpu.make_async_copy(wv_hbm, wv, sems.at[5]),
    ]
    for copy in loads + late:
        copy.start()

    def add(j, sums):
        return tuple(s + recv[j, n].astype(F32) for n, s in enumerate(sums))

    sums = tuple(jnp.zeros((8, D), F32) for _ in range(3))
    for part in range(4):
        loads[part].wait()
        sums = lax.fori_loop(16 * part, 16 * part + 16, add, sums)
    gw_ref[:8, 0] = sums[0]
    gw_ref[:8, 3] = sums[1]

    def slot(place):
        row, lane = place
        return sums[2][row : row + 1, lane : lane + 128]

    for b in range(18):
        at = 128 * (b % 9)
        gw_ref[8:9, 3 * (b // 9), at : at + 128] = slot(SLOTS[b])
    for b in range(9):
        gain_ref[b : b + 1] = slot(GAINS[b]) + slot(GAINS[9 + b])
    base = yl_ref[0] * 32
    for t in range(32):
        cols = slice(36 * t, 36 * t + 36)
        x = recv[t, 2, :, :EARLY].astype(F32) + recv[32 + t, 2, :, :EARLY].astype(F32)
        eight = x[:, :80] + x[:, 80:160]
        one = x[:1, 480:560] + x[:1, 560:640]
        near = recv[base + t, 2, :, 128:512].astype(F32)
        for n in range(2):
            kv[n, :8, cols] = eight[:, 40 * n : 40 * n + 36]
            kv[n, 8:9, cols] = one[:, 40 * n : 40 * n + 36]
            for half in range(2):
                for m in range(2):
                    lane = 32 + 160 * half + 80 * m + 40 * n
                    row = 16 * m + 8 * half
                    tok[n, row : row + 8, cols] = near[:, lane : lane + 36]
    for n in range(2):
        gw_ref[:8, 1 + n] = kv[n, :8]
        gw_ref[8:9, 1 + n] = kv[n, 8:9]
    for copy in late:
        copy.wait()
    grad = dot(wk[...], tok[0].astype(BF16), 1, 1) + dot(wv[...], tok[1].astype(BF16), 1, 1)
    gg_ref[...] = grad.T.astype(BF16)


def finish(yl, recv, w_key, w_value):
    vmem = pl.BlockSpec(memory_space=pltpu.VMEM)
    hbm = pl.BlockSpec(memory_space=pl.ANY)
    return pl.pallas_call(
        finish_kernel,
        in_specs=[pl.BlockSpec(memory_space=pltpu.SMEM), hbm, hbm, hbm],
        out_specs=[vmem] * 3,
        out_shape=[
            jax.ShapeDtypeStruct((9, 4, D), F32),
            jax.ShapeDtypeStruct((32, D), BF16),
            jax.ShapeDtypeStruct((9, 128), F32),
        ],
        scratch_shapes=[
            pltpu.VMEM((2, 32, D), F32),
            pltpu.VMEM((2, 16, D), F32),
            pltpu.VMEM((64, 3, 8, D), BF16),
            pltpu.VMEM((D, D), BF16),
            pltpu.VMEM((D, D), BF16),
            pltpu.SemaphoreType.DMA((6,)),
        ],
        name="finish",
    )(yl, recv, w_key, w_value)


def on_device(tiles, tile_image, guide, gain, w_query, w_key, w_value, w_out, grad_out):
    core = lax.axis_index("c")
    yl = lax.axis_index("yl")
    whole = lax.all_to_all(copies_of(guide), TILE_AXES, 0, 0, tiled=True)
    xf = tiles.astype(F32)
    rstd = lax.rsqrt(jnp.mean(xf * xf, axis=-1, keepdims=True) + 1e-06)
    normed = xf * rstd
    hidden = (normed * gain).astype(BF16)
    query = dot(hidden, w_query, 1, 0).astype(BF16)
    dout = dot(grad_out, w_out, 1, 1).astype(BF16)
    want = wanted_rows(core)
    hid_both = jnp.concatenate([hidden, lax.ppermute(hidden, "c", SWAP)], axis=0)
    hid_rows = dot(one_hot(want, D), hid_both, 1, 1).astype(BF16)
    grad_got = lax.ppermute(grad_out, "c", SWAP)
    query, hid_rows = lax.optimization_barrier((query, hid_rows))

    pay, outv, dq = attention(tile_image, whole, w_key, w_value, query, dout)
    got = lax.all_to_all(pay, TILE_AXES, 0, 0, tiled=True)

    dq_got = lax.ppermute(dq, "c", SWAP)
    out_got = lax.ppermute(outv, "c", SWAP)
    dh = dot(dq, w_query, 1, 1)
    gain_part = jnp.sum(dh * normed, axis=0, keepdims=True)
    gain_part = gain_part + lax.ppermute(gain_part, "c", SWAP)
    gain_high = lax.reduce_precision(gain_part, 8, 7)
    gains = jnp.concatenate([gain_high, gain_part - gain_high], axis=1)
    send = weight_parts(
        want, hid_rows, outv, out_got, dq, dq_got, grad_out, grad_got, gains
    )
    dn = dh * gain
    grad_tiles = (rstd * (dn - normed * jnp.mean(dn * normed, axis=-1, keepdims=True))).astype(BF16)

    got, send = lax.optimization_barrier((got, send))
    mine, theirs, tok = image_sums(core[None], got, whole)
    send = fill_rest(send, mine, lax.ppermute(theirs, "c", SWAP), fill_tokens(tok, gains))
    recv = lax.all_to_all(send, CHIP_AXES, 0, 0, tiled=True)
    grad_weights, grad_guide, grad_gain = finish(yl[None], recv, w_key, w_value)
    grad_weights = grad_weights.transpose(1, 0, 2)
    return (grad_tiles, grad_guide.reshape(guide.shape), grad_weights, grad_gain.reshape(D))


def solution(mesh):
    fine = Mesh(mesh.devices.reshape(2, 2, 4, 2, 4), ("yl", "c", "x", "yh", "z"))
    every = ("yl", "c", "x", "yh", "z")
    return jax.shard_map(
        on_device,
        mesh=fine,
        in_specs=(
            P(every, None),
            P(every),
            P(("yl", "c"), TILE_AXES, None),
            P(),
            P(),
            P(),
            P(),
            P(),
            P(every, None),
        ),
        out_specs=(
            P(every, None),
            P(("yl", "c"), TILE_AXES, None),
            P(None, every, None),
            P(),
        ),
        check_vma=False,
    )
```

```python
import jax
import jax.numpy as jnp
from jax import lax
from jax.experimental import pallas as pl
from jax.experimental.pallas import tpu as pltpu
from jax.sharding import Mesh, PartitionSpec as P

HEADS = 16
HD = 72
D = 1152
G = 512
F32 = jnp.float32
BF16 = jnp.bfloat16
TILE_AXES = ("x", "yh", "z")
SWAP = [(0, 1), (1, 0)]


def dot(a, b, ca, cb):
    return lax.dot_general(a, b, (((ca,), (cb,)), ((), ())), preferred_element_type=F32)


def copies_kernel(g_ref, out, sems):
    copies = [pltpu.make_async_copy(g_ref, out.at[i], sems.at[i]) for i in range(32)]
    for copy in copies:
        copy.start()
    for copy in copies:
        copy.wait()


def copies_of(guide):
    return pl.pallas_call(
        copies_kernel,
        in_specs=[pl.BlockSpec(memory_space=pltpu.VMEM)],
        out_specs=pl.BlockSpec(memory_space=pl.ANY),
        out_shape=jax.ShapeDtypeStruct((32, *guide.shape), guide.dtype),
        scratch_shapes=[pltpu.SemaphoreType.DMA((32,))],
        name="copies_of_guide",
    )(guide)


def attention_kernel(
    img_ref, g_hbm, wk_hbm, wv_hbm, q_ref, d_ref, pay_hbm, o_ref, dq_ref,
    guide, wk, wv, k_scr, v_scr, pay, sems, out_sems,
):
    loads = [
        pltpu.make_async_copy(g_hbm.at[:, img_ref[0]], guide, sems.at[0]),
        pltpu.make_async_copy(wk_hbm, wk, sems.at[1]),
        pltpu.make_async_copy(wv_hbm, wv, sems.at[2]),
    ]
    for copy in loads:
        copy.start()
    loads[0].wait()
    tokens = guide[...].reshape(G, D)
    loads[1].wait()
    k_scr[...] = dot(tokens, wk[...], 1, 0).astype(BF16)
    loads[2].wait()
    v_scr[...] = dot(tokens, wv[...], 1, 0).astype(BF16)
    scale = HD ** (-0.5)
    flag = jnp.full((4, G), img_ref[0], jnp.int32).astype(F32)
    stores = []
    t = q_ref.shape[0]
    lane = lax.broadcasted_iota(jnp.int32, (t, 2 * HD), 1)
    none = jnp.zeros((t, 2 * HD), BF16)
    for h in range(0, HEADS, 2):
        cols = slice(h * HD, (h + 2) * HD)
        k, v = k_scr[:, cols], v_scr[:, cols]

        def both(x):
            return jnp.concatenate([jnp.where(lane < HD, x, none), jnp.where(lane < HD, none, x)], axis=0)

        def own(x):
            return jnp.where(lane < HD, x[:t], x[t:]).astype(BF16)

        q, d = both(q_ref[:, cols]), both(d_ref[:, cols])
        scores = dot(q, k, 1, 1) * scale
        dprob = dot(d, v, 1, 1)
        top = jnp.max(scores, axis=-1, keepdims=True)
        expo = jnp.exp(scores - top)
        probs = expo * (1.0 / jnp.sum(expo, axis=-1, keepdims=True))
        pb = probs.astype(BF16)
        weighted = probs * dprob
        delta = jnp.sum(weighted, axis=-1, keepdims=True)
        ds = ((weighted - probs * delta) * scale).astype(BF16)
        o_ref[:, cols] = own(dot(pb, v, 1, 0))
        dq_ref[:, cols] = own(dot(ds, k, 1, 0))
        for j, part in enumerate((dot(q, ds, 0, 0), dot(d, pb, 0, 0))):
            for i in range(4):
                rows = jnp.concatenate([part[36 * i : 36 * i + 36], flag], axis=0)
                pay[2 * h + i, j] = rows.astype(BF16)
        some = pl.ds(2 * h, 4)
        stores.append(pltpu.make_async_copy(pay.at[some], pay_hbm.at[some], out_sems.at[h // 2]))
        stores[-1].start()
    for copy in stores:
        copy.wait()


def attention(img, whole, w_key, w_value, q, d):
    t = q.shape[0]
    vmem = pl.BlockSpec(memory_space=pltpu.VMEM)
    hbm = pl.BlockSpec(memory_space=pl.ANY)
    return pl.pallas_call(
        attention_kernel,
        in_specs=[pl.BlockSpec(memory_space=pltpu.SMEM), hbm, hbm, hbm, vmem, vmem],
        out_specs=[hbm, vmem, vmem],
        out_shape=[
            jax.ShapeDtypeStruct((32, 2, 40, G), BF16),
            jax.ShapeDtypeStruct((t, D), BF16),
            jax.ShapeDtypeStruct((t, D), BF16),
        ],
        scratch_shapes=[
            pltpu.VMEM((32, 16, D), BF16),
            pltpu.VMEM((D, D), BF16),
            pltpu.VMEM((D, D), BF16),
            pltpu.VMEM((G, D), BF16),
            pltpu.VMEM((G, D), BF16),
            pltpu.VMEM((32, 2, 40, G), BF16),
            pltpu.SemaphoreType.DMA((3,)),
            pltpu.SemaphoreType.DMA((HEADS // 2,)),
        ],
        name="attention",
    )(img, whole, w_key, w_value, q, d)


ROWS = 576


def eight_and_one(rows):
    return jnp.where(rows < 512, rows // 8 * 9 + rows % 8, (rows - 512) * 9 + 8)


def wanted_rows(core):
    row = eight_and_one(jnp.arange(ROWS, dtype=jnp.int32))
    return (row // 288 * 576 + core * 288 + row % 288)[:, None]


def one_hot(want, width):
    return (want == lax.broadcasted_iota(jnp.int32, (want.shape[0], width), 1)).astype(BF16)


MISC = 4 * D
LATE = 896
WIDE = MISC + LATE + 768
SLOTS = [(row, lane) for lane in range(LATE, LATE + 768, 128) for row in range(8)]
GAINS = SLOTS[36:] + [(row, 640) for row in range(2, 8)]


def weight_parts_kernel(
    want_ref, hid_ref, o_ref, o2_ref, dq_ref, dq2_ref, g_ref, g2_ref, gain_ref, send_ref, scr
):
    o = jnp.concatenate([o_ref[...], o2_ref[...]], axis=0)
    dq = jnp.concatenate([dq_ref[...], dq2_ref[...]], axis=0)
    g = jnp.concatenate([g_ref[...], g2_ref[...]], axis=0)
    o_rows = dot(one_hot(want_ref[...], D), o, 1, 1).astype(BF16)
    parts = (dot(hid_ref[...], dq, 1, 0), dot(o_rows, g, 1, 0))
    for m, part in enumerate(parts):
        for y in range(2):
            at = (2 * y + m) * D
            eight = part[256 * y : 256 * y + 256].reshape(32, 8, D)
            send_ref[:, :, at : at + D] = eight.astype(BF16)
            for b in range(9):
                row, lane = SLOTS[9 * (2 * y + m) + b]
                ninth = part[512 + 32 * y : 544 + 32 * y, 128 * b : 128 * b + 128]
                scr[:, row, lane - LATE : lane - LATE + 128] = ninth
    for b in range(12):
        row, lane = GAINS[b]
        block = gain_ref[:, 128 * b : 128 * b + 128]
        scr[:, row, lane - LATE : lane - LATE + 128] = jnp.broadcast_to(block, (32, 128))
    send_ref[:, :, MISC + LATE :] = scr[...].astype(BF16)


def weight_parts(*args):
    vmem = pl.BlockSpec(memory_space=pltpu.VMEM)
    return pl.pallas_call(
        weight_parts_kernel,
        in_specs=[vmem] * 9,
        out_specs=vmem,
        out_shape=jax.ShapeDtypeStruct((32, 8, WIDE), BF16),
        scratch_shapes=[pltpu.VMEM((32, 8, 768), F32)],
        name="weight_parts",
    )(*args)


def image_sums_kernel(core_ref, got_hbm, g_hbm, mine_ref, theirs_ref, tok_ref, scr, got, guide, sems):
    loads = []
    for n in range(2):
        for part in range(2):
            some = pl.ds(16 * part, 16)
            sem = sems.at[2 * n + part]
            loads.append(pltpu.make_async_copy(got_hbm.at[some, n], got.at[n, some], sem))
    last = pltpu.make_async_copy(g_hbm, guide, sems.at[4])
    for copy in loads + [last]:
        copy.start()
    zero = jnp.zeros((40, G), F32)
    sums = [None, None]
    for n in range(2):

        def add(s, pair, n=n):
            terms = got[n, s].astype(F32)
            first = terms[36:37, :] == 0.0
            return pair[0] + jnp.where(first, terms, zero), pair[1] + jnp.where(first, zero, terms)

        pair = (zero, zero)
        for part in range(2):
            loads[2 * n + part].wait()
            pair = lax.fori_loop(16 * part, 16 * part + 16, add, pair)
        sums[n] = pair
    rounded = [jnp.concatenate([sums[0][m], sums[1][m]], axis=0).astype(BF16) for m in range(2)]
    last.wait()
    prod = dot(rounded[0], guide[:, 0].reshape(G, D), 1, 0)
    prod = prod + dot(rounded[1], guide[:, 1].reshape(G, D), 1, 0)
    scr[...] = jnp.concatenate([prod, jnp.zeros((48, D), F32)], axis=0).T
    core = core_ref[0]
    for n in range(2):
        for out, c in ((mine_ref, core), (theirs_ref, 1 - core)):
            start = pl.multiple_of(n * 576 + c * 288, 32)
            out[n * 288 : n * 288 + 288] = scr[pl.ds(start, 288), :]
    tok_ref[:80] = rounded[0]
    tok_ref[80:] = rounded[1]


def image_sums(core, got, whole):
    vmem = pl.BlockSpec(memory_space=pltpu.VMEM)
    hbm = pl.BlockSpec(memory_space=pl.ANY)
    return pl.pallas_call(
        image_sums_kernel,
        in_specs=[pl.BlockSpec(memory_space=pltpu.SMEM), hbm, hbm],
        out_specs=[vmem] * 3,
        out_shape=[
            jax.ShapeDtypeStruct((ROWS, 128), F32),
            jax.ShapeDtypeStruct((ROWS, 128), F32),
            jax.ShapeDtypeStruct((160, G), BF16),
        ],
        scratch_shapes=[
            pltpu.VMEM((D, 128), F32),
            pltpu.VMEM((2, 32, 40, G), BF16),
            pltpu.VMEM((32, 2, 16, D), BF16),
            pltpu.SemaphoreType.DMA((5,)),
        ],
        name="image_sums",
    )(core, got, whole)


def fill_rest_kernel(send_hbm, mine_ref, got_ref, tok_ref, gain_ref, out_hbm, scr, late, sem):
    total = mine_ref[...] + got_ref[...]
    high = total.astype(BF16)
    low = (total - high.astype(F32)).astype(BF16)
    want = eight_and_one(lax.broadcasted_iota(jnp.int32, (ROWS, ROWS), 0))
    order = (want == lax.broadcasted_iota(jnp.int32, (ROWS, ROWS), 1)).astype(BF16)
    moved = dot(order, jnp.concatenate([high, low], axis=1), 1, 0)
    scr[:, :, 640:] = jnp.zeros((32, 8, LATE - 640), F32)
    rows = jnp.concatenate([tok_ref[...].astype(F32), jnp.zeros((96, G), F32)], axis=0)
    tok = rows.T.reshape(32, 16, 256)
    for half in range(2):
        scr[:, :, 160 * half : 160 * half + 160] = tok[:, 8 * half : 8 * half + 8, :160]
    for y in range(2):
        for n in range(2):
            piece = moved[:, 128 * n : 128 * n + 80]
            at = 320 + 160 * y + 80 * n
            scr[:, :, at : at + 80] = piece[256 * y : 256 * y + 256].reshape(32, 8, 80)
            scr[:, y, 640 + 80 * n : 720 + 80 * n] = piece[512 + 32 * y : 544 + 32 * y]
    for b in range(12, 18):
        row, lane = GAINS[b]
        block = gain_ref[:, 128 * b : 128 * b + 128]
        scr[:, row, lane : lane + 128] = jnp.broadcast_to(block, (32, 128))
    late[...] = scr[...].astype(BF16)
    copy = pltpu.make_async_copy(late, out_hbm.at[:, :, pl.ds(MISC, LATE)], sem)
    copy.start()
    copy.wait()


def fill_rest(send, mine, got, tok, gain):
    vmem = pl.BlockSpec(memory_space=pltpu.VMEM)
    hbm = pl.BlockSpec(memory_space=pl.ANY)
    return pl.pallas_call(
        fill_rest_kernel,
        in_specs=[hbm] + [vmem] * 4,
        out_specs=hbm,
        out_shape=jax.ShapeDtypeStruct((32, 8, WIDE), BF16),
        scratch_shapes=[
            pltpu.VMEM((32, 8, LATE), F32),
            pltpu.VMEM((32, 8, LATE), BF16),
            pltpu.SemaphoreType.DMA,
        ],
        input_output_aliases={0: 0},
        name="fill_rest",
    )(send, mine, got, tok, gain)


def group_sums_kernel(yl_ref, recv_hbm, keep_ref, give_ref, both, recv, sems):
    loads = []
    for part in range(4):
        some = pl.ds(8 * part, 8)
        loads.append(pltpu.make_async_copy(recv_hbm.at[some], recv.at[some], sems.at[part]))
    for copy in loads:
        copy.start()
    sums = [None] * 4
    for part in range(4):
        loads[part].wait()
    for n in range(4):

        def add(t, total, n=n):
            return total + recv[t, :, n * D : n * D + D].astype(F32)

        sums[n] = lax.fori_loop(0, 32, add, jnp.zeros((8, D), F32))

    def add_rest(t, total):
        return total + recv[t, :, MISC + 640 :].astype(F32)

    rest = lax.fori_loop(0, 32, add_rest, jnp.zeros((8, WIDE - MISC - 640), F32))

    def slot(place):
        row, lane = place
        return rest[row : row + 1, lane - 640 : lane - 512]

    for y in range(2):
        for m in range(2):
            both[y, 3 * m, :8] = sums[2 * y + m]
            for b in range(9):
                at = 128 * b
                both[y, 3 * m, 8:9, at : at + 128] = slot(SLOTS[9 * (2 * y + m) + b])
        for b in range(9):
            at = 128 * b
            both[y, 0, 9:10, at : at + 128] = slot(GAINS[b]) + slot(GAINS[9 + b])
    for t in range(32):
        cols = slice(36 * t, 36 * t + 36)
        x = recv[t, :, MISC + 256 : MISC + LATE].astype(F32)
        for y in range(2):
            at = 64 + 160 * y
            eight = x[:, at : at + 80] + x[:, at + 80 : at + 160]
            one = x[y : y + 1, 384:464] + x[y : y + 1, 464:544]
            for n in range(2):
                both[y, 1 + n, :8, cols] = eight[:, 40 * n : 40 * n + 36]
                both[y, 1 + n, 8:9, cols] = one[:, 40 * n : 40 * n + 36]
    for out, y in ((keep_ref, yl_ref[0]), (give_ref, 1 - yl_ref[0])):
        for m in range(4):
            out[:, m] = both[y, m, :10]


def group_sums(yl, recv):
    vmem = pl.BlockSpec(memory_space=pltpu.VMEM)
    return pl.pallas_call(
        group_sums_kernel,
        in_specs=[pl.BlockSpec(memory_space=pltpu.SMEM), pl.BlockSpec(memory_space=pl.ANY)],
        out_specs=[vmem] * 2,
        out_shape=[jax.ShapeDtypeStruct((10, 4, D), F32)] * 2,
        scratch_shapes=[
            pltpu.VMEM((2, 4, 16, D), F32),
            pltpu.VMEM((32, 8, WIDE), BF16),
            pltpu.SemaphoreType.DMA((4,)),
        ],
        name="group_sums",
    )(yl, recv)


def both_sums_kernel(keep_ref, got_ref, gw_ref, gain_ref):
    gw_ref[...] = keep_ref[:9] + got_ref[:9]
    gain = keep_ref[9, :1] + got_ref[9, :1]
    for b in range(9):
        gain_ref[b : b + 1] = gain[:, 128 * b : 128 * b + 128]


def both_sums(keep, got):
    vmem = pl.BlockSpec(memory_space=pltpu.VMEM)
    return pl.pallas_call(
        both_sums_kernel,
        in_specs=[vmem] * 2,
        out_specs=[vmem] * 2,
        out_shape=[jax.ShapeDtypeStruct((9, 4, D), F32), jax.ShapeDtypeStruct((9, 128), F32)],
        name="both_sums",
    )(keep, got)


def guide_grad_kernel(recv_hbm, wk_hbm, wv_hbm, gg_ref, tok, recv, wk, wv, sems):
    copies = [
        pltpu.make_async_copy(recv_hbm.at[:, :, pl.ds(MISC, 384)], recv, sems.at[0]),
        pltpu.make_async_copy(wk_hbm, wk, sems.at[1]),
        pltpu.make_async_copy(wv_hbm, wv, sems.at[2]),
    ]
    for copy in copies:
        copy.start()
    copies[0].wait()
    for t in range(32):
        near = recv[t].astype(F32)
        for n in range(2):
            for half in range(2):
                for m in range(2):
                    lane = 160 * half + 80 * m + 40 * n
                    row = 16 * m + 8 * half
                    tok[n, row : row + 8, 36 * t : 36 * t + 36] = near[:, lane : lane + 36]
    copies[1].wait()
    grad = dot(wk[...], tok[0].astype(BF16), 1, 1)
    copies[2].wait()
    grad = grad + dot(wv[...], tok[1].astype(BF16), 1, 1)
    gg_ref[...] = grad.T.astype(BF16)


def guide_grad(recv, w_key, w_value):
    hbm = pl.BlockSpec(memory_space=pl.ANY)
    return pl.pallas_call(
        guide_grad_kernel,
        in_specs=[hbm] * 3,
        out_specs=pl.BlockSpec(memory_space=pltpu.VMEM),
        out_shape=jax.ShapeDtypeStruct((32, D), BF16),
        scratch_shapes=[
            pltpu.VMEM((2, 32, D), F32),
            pltpu.VMEM((32, 8, 384), BF16),
            pltpu.VMEM((D, D), BF16),
            pltpu.VMEM((D, D), BF16),
            pltpu.SemaphoreType.DMA((3,)),
        ],
        name="guide_grad",
    )(recv, w_key, w_value)


def on_device(tiles, tile_image, guide, gain, w_query, w_key, w_value, w_out, grad_out):
    core = lax.axis_index("c")
    yl = lax.axis_index("yl")
    whole = lax.all_to_all(copies_of(guide), TILE_AXES, 0, 0, tiled=True)
    xf = tiles.astype(F32)
    rstd = lax.rsqrt(jnp.mean(xf * xf, axis=-1, keepdims=True) + 1e-06)
    normed = xf * rstd
    hidden = (normed * gain).astype(BF16)
    query = dot(hidden, w_query, 1, 0).astype(BF16)
    dout = dot(grad_out, w_out, 1, 1).astype(BF16)
    want = wanted_rows(core)
    hid_both = jnp.concatenate([hidden, lax.ppermute(hidden, "c", SWAP)], axis=0)
    hid_rows = dot(one_hot(want, D), hid_both, 1, 1).astype(BF16)
    grad_got = lax.ppermute(grad_out, "c", SWAP)
    query, hid_rows = lax.optimization_barrier((query, hid_rows))

    pay, outv, dq = attention(tile_image, whole, w_key, w_value, query, dout)
    got = lax.all_to_all(pay, TILE_AXES, 0, 0, tiled=True)

    dq_got = lax.ppermute(dq, "c", SWAP)
    out_got = lax.ppermute(outv, "c", SWAP)
    dh = dot(dq, w_query, 1, 1)
    gain_part = jnp.sum(dh * normed, axis=0, keepdims=True)
    gain_part = gain_part + lax.ppermute(gain_part, "c", SWAP)
    gain_high = lax.reduce_precision(gain_part, 8, 7)
    gains = jnp.concatenate([gain_high, gain_part - gain_high], axis=1)
    send = weight_parts(
        want, hid_rows, outv, out_got, dq, dq_got, grad_out, grad_got, gains
    )
    dn = dh * gain
    grad_tiles = (rstd * (dn - normed * jnp.mean(dn * normed, axis=-1, keepdims=True))).astype(BF16)

    got, send = lax.optimization_barrier((got, send))
    mine, theirs, tok = image_sums(core[None], got, whole)
    send = fill_rest(send, mine, lax.ppermute(theirs, "c", SWAP), tok, gains)
    recv = lax.all_to_all(send, TILE_AXES, 0, 0, tiled=True)
    keep, give = group_sums(yl[None], recv)
    grad_weights, grad_gain = both_sums(keep, lax.ppermute(give, "yl", SWAP))
    grad_guide = guide_grad(recv, w_key, w_value).reshape(guide.shape)
    return (grad_tiles, grad_guide, grad_weights.transpose(1, 0, 2), grad_gain.reshape(D))


def solution(mesh):
    fine = Mesh(mesh.devices.reshape(2, 2, 4, 2, 4), ("yl", "c", "x", "yh", "z"))
    every = ("yl", "c", "x", "yh", "z")
    return jax.shard_map(
        on_device,
        mesh=fine,
        in_specs=(
            P(every, None),
            P(every),
            P(("yl", "c"), TILE_AXES, None),
            P(),
            P(),
            P(),
            P(),
            P(),
            P(every, None),
        ),
        out_specs=(
            P(every, None),
            P(("yl", "c"), TILE_AXES, None),
            P(None, every, None),
            P(),
        ),
        check_vma=False,
    )
```

```python
import jax
import jax.numpy as jnp
from jax import lax
from jax.experimental import pallas as pl
from jax.experimental.pallas import tpu as pltpu
from jax.sharding import Mesh, PartitionSpec as P

HEADS = 16
HD = 72
D = 1152
G = 512
F32 = jnp.float32
BF16 = jnp.bfloat16
TILE_AXES = ("x", "yh", "z")
SWAP = [(0, 1), (1, 0)]


def dot(a, b, ca, cb):
    return lax.dot_general(a, b, (((ca,), (cb,)), ((), ())), preferred_element_type=F32)


def copies_kernel(g_ref, out, sems):
    copies = [pltpu.make_async_copy(g_ref, out.at[i], sems.at[i]) for i in range(32)]
    for copy in copies:
        copy.start()
    for copy in copies:
        copy.wait()


def copies_of(guide):
    return pl.pallas_call(
        copies_kernel,
        in_specs=[pl.BlockSpec(memory_space=pltpu.VMEM)],
        out_specs=pl.BlockSpec(memory_space=pl.ANY),
        out_shape=jax.ShapeDtypeStruct((32, *guide.shape), guide.dtype),
        scratch_shapes=[pltpu.SemaphoreType.DMA((32,))],
        name="copies_of_guide",
    )(guide)


def attention_kernel(
    img_ref, g_hbm, wk_hbm, wv_hbm, q_ref, d_ref, pay_hbm, o_ref, dq_ref,
    guide, wk, wv, k_scr, v_scr, pay, sems, out_sems,
):
    loads = [
        pltpu.make_async_copy(g_hbm.at[:, img_ref[0]], guide, sems.at[0]),
        pltpu.make_async_copy(wk_hbm, wk, sems.at[1]),
        pltpu.make_async_copy(wv_hbm, wv, sems.at[2]),
    ]
    for copy in loads:
        copy.start()
    loads[0].wait()
    tokens = guide[...].reshape(G, D)
    loads[1].wait()
    k_scr[...] = dot(tokens, wk[...], 1, 0).astype(BF16)
    loads[2].wait()
    v_scr[...] = dot(tokens, wv[...], 1, 0).astype(BF16)
    scale = HD ** (-0.5)
    flag = jnp.full((4, G), img_ref[0], jnp.int32).astype(F32)
    stores = []
    t = q_ref.shape[0]
    lane = lax.broadcasted_iota(jnp.int32, (t, 2 * HD), 1)
    none = jnp.zeros((t, 2 * HD), BF16)
    for h in range(0, HEADS, 2):
        cols = slice(h * HD, (h + 2) * HD)
        k, v = k_scr[:, cols], v_scr[:, cols]

        def both(x):
            return jnp.concatenate([jnp.where(lane < HD, x, none), jnp.where(lane < HD, none, x)], axis=0)

        def own(x):
            return jnp.where(lane < HD, x[:t], x[t:]).astype(BF16)

        q, d = both(q_ref[:, cols]), both(d_ref[:, cols])
        scores = dot(q, k, 1, 1) * scale
        dprob = dot(d, v, 1, 1)
        top = jnp.max(scores, axis=-1, keepdims=True)
        expo = jnp.exp(scores - top)
        probs = expo * (1.0 / jnp.sum(expo, axis=-1, keepdims=True))
        pb = probs.astype(BF16)
        weighted = probs * dprob
        delta = jnp.sum(weighted, axis=-1, keepdims=True)
        ds = ((weighted - probs * delta) * scale).astype(BF16)
        o_ref[:, cols] = own(dot(pb, v, 1, 0))
        dq_ref[:, cols] = own(dot(ds, k, 1, 0))
        for j, part in enumerate((dot(q, ds, 0, 0), dot(d, pb, 0, 0))):
            for i in range(4):
                rows = jnp.concatenate([part[36 * i : 36 * i + 36], flag], axis=0)
                pay[2 * h + i, j] = rows.astype(BF16)
        some = pl.ds(2 * h, 4)
        stores.append(pltpu.make_async_copy(pay.at[some], pay_hbm.at[some], out_sems.at[h // 2]))
        stores[-1].start()
    for copy in stores:
        copy.wait()


def attention(img, whole, w_key, w_value, q, d):
    t = q.shape[0]
    vmem = pl.BlockSpec(memory_space=pltpu.VMEM)
    hbm = pl.BlockSpec(memory_space=pl.ANY)
    return pl.pallas_call(
        attention_kernel,
        in_specs=[pl.BlockSpec(memory_space=pltpu.SMEM), hbm, hbm, hbm, vmem, vmem],
        out_specs=[hbm, vmem, vmem],
        out_shape=[
            jax.ShapeDtypeStruct((32, 2, 40, G), BF16),
            jax.ShapeDtypeStruct((t, D), BF16),
            jax.ShapeDtypeStruct((t, D), BF16),
        ],
        scratch_shapes=[
            pltpu.VMEM((32, 16, D), BF16),
            pltpu.VMEM((D, D), BF16),
            pltpu.VMEM((D, D), BF16),
            pltpu.VMEM((G, D), BF16),
            pltpu.VMEM((G, D), BF16),
            pltpu.VMEM((32, 2, 40, G), BF16),
            pltpu.SemaphoreType.DMA((3,)),
            pltpu.SemaphoreType.DMA((HEADS // 2,)),
        ],
        name="attention",
    )(img, whole, w_key, w_value, q, d)


ROWS = 576


def eight_and_one(rows):
    return jnp.where(rows < 512, rows // 8 * 9 + rows % 8, (rows - 512) * 9 + 8)


def wanted_rows(core):
    row = eight_and_one(jnp.arange(ROWS, dtype=jnp.int32))
    return (row // 288 * 576 + core * 288 + row % 288)[:, None]


def one_hot(want, width):
    return (want == lax.broadcasted_iota(jnp.int32, (want.shape[0], width), 1)).astype(BF16)


MISC = 4 * D
LATE = 896
WIDE = MISC + LATE + 768
SLOTS = [(row, lane) for lane in range(LATE, LATE + 768, 128) for row in range(8)]
GAINS = SLOTS[36:] + [(row, 640) for row in range(2, 8)]


def weight_parts_kernel(
    want_ref, hid_ref, o_ref, o2_ref, dq_ref, dq2_ref, g_ref, g2_ref, gain_ref, send_ref, scr
):
    o = jnp.concatenate([o_ref[...], o2_ref[...]], axis=0)
    dq = jnp.concatenate([dq_ref[...], dq2_ref[...]], axis=0)
    g = jnp.concatenate([g_ref[...], g2_ref[...]], axis=0)
    o_rows = dot(one_hot(want_ref[...], D), o, 1, 1).astype(BF16)
    parts = (dot(hid_ref[...], dq, 1, 0), dot(o_rows, g, 1, 0))
    for m, part in enumerate(parts):
        for y in range(2):
            at = (2 * y + m) * D
            eight = part[256 * y : 256 * y + 256].reshape(32, 8, D)
            send_ref[:, :, at : at + D] = eight.astype(BF16)
            for b in range(9):
                row, lane = SLOTS[9 * (2 * y + m) + b]
                ninth = part[512 + 32 * y : 544 + 32 * y, 128 * b : 128 * b + 128]
                scr[:, row, lane - LATE : lane - LATE + 128] = ninth
    for b in range(12):
        row, lane = GAINS[b]
        block = gain_ref[:, 128 * b : 128 * b + 128]
        scr[:, row, lane - LATE : lane - LATE + 128] = jnp.broadcast_to(block, (32, 128))
    send_ref[:, :, MISC + LATE :] = scr[...].astype(BF16)


def weight_parts(*args):
    vmem = pl.BlockSpec(memory_space=pltpu.VMEM)
    return pl.pallas_call(
        weight_parts_kernel,
        in_specs=[vmem] * 9,
        out_specs=vmem,
        out_shape=jax.ShapeDtypeStruct((32, 8, WIDE), BF16),
        scratch_shapes=[pltpu.VMEM((32, 8, 768), F32)],
        name="weight_parts",
    )(*args)


def image_sums_kernel(core_ref, got_hbm, g_hbm, mine_ref, theirs_ref, tok_ref, scr, got, guide, sems):
    loads = []
    for n in range(2):
        for part in range(2):
            some = pl.ds(16 * part, 16)
            sem = sems.at[2 * n + part]
            loads.append(pltpu.make_async_copy(got_hbm.at[some, n], got.at[n, some], sem))
    last = pltpu.make_async_copy(g_hbm, guide, sems.at[4])
    for copy in loads + [last]:
        copy.start()
    zero = jnp.zeros((40, G), F32)
    sums = [None, None]
    for n in range(2):

        def add(s, pair, n=n):
            terms = got[n, s].astype(F32)
            first = terms[36:37, :] == 0.0
            return pair[0] + jnp.where(first, terms, zero), pair[1] + jnp.where(first, zero, terms)

        pair = (zero, zero)
        for part in range(2):
            loads[2 * n + part].wait()
            pair = lax.fori_loop(16 * part, 16 * part + 16, add, pair)
        sums[n] = pair
    rounded = [jnp.concatenate([sums[0][m], sums[1][m]], axis=0).astype(BF16) for m in range(2)]
    last.wait()
    prod = dot(rounded[0], guide[:, 0].reshape(G, D), 1, 0)
    prod = prod + dot(rounded[1], guide[:, 1].reshape(G, D), 1, 0)
    scr[...] = jnp.concatenate([prod, jnp.zeros((48, D), F32)], axis=0).T
    core = core_ref[0]
    for n in range(2):
        for out, c in ((mine_ref, core), (theirs_ref, 1 - core)):
            start = pl.multiple_of(n * 576 + c * 288, 32)
            out[n * 288 : n * 288 + 288] = scr[pl.ds(start, 288), :]
    tok_ref[:80] = rounded[0]
    tok_ref[80:] = rounded[1]


def image_sums(core, got, whole):
    vmem = pl.BlockSpec(memory_space=pltpu.VMEM)
    hbm = pl.BlockSpec(memory_space=pl.ANY)
    return pl.pallas_call(
        image_sums_kernel,
        in_specs=[pl.BlockSpec(memory_space=pltpu.SMEM), hbm, hbm],
        out_specs=[vmem] * 3,
        out_shape=[
            jax.ShapeDtypeStruct((ROWS, 128), F32),
            jax.ShapeDtypeStruct((ROWS, 128), F32),
            jax.ShapeDtypeStruct((160, G), BF16),
        ],
        scratch_shapes=[
            pltpu.VMEM((D, 128), F32),
            pltpu.VMEM((2, 32, 40, G), BF16),
            pltpu.VMEM((32, 2, 16, D), BF16),
            pltpu.SemaphoreType.DMA((5,)),
        ],
        name="image_sums",
    )(core, got, whole)


def fill_rest_kernel(send_hbm, mine_ref, got_ref, tok_ref, gain_ref, out_hbm, scr, late, sem):
    total = mine_ref[...] + got_ref[...]
    high = total.astype(BF16)
    low = (total - high.astype(F32)).astype(BF16)
    want = eight_and_one(lax.broadcasted_iota(jnp.int32, (ROWS, ROWS), 0))
    order = (want == lax.broadcasted_iota(jnp.int32, (ROWS, ROWS), 1)).astype(BF16)
    moved = dot(order, jnp.concatenate([high, low], axis=1), 1, 0)
    scr[:, :, 640:] = jnp.zeros((32, 8, LATE - 640), F32)
    rows = jnp.concatenate([tok_ref[...].astype(F32), jnp.zeros((96, G), F32)], axis=0)
    tok = rows.T.reshape(32, 16, 256)
    for half in range(2):
        scr[:, :, 160 * half : 160 * half + 160] = tok[:, 8 * half : 8 * half + 8, :160]
    for y in range(2):
        for n in range(2):
            piece = moved[:, 128 * n : 128 * n + 80]
            at = 320 + 160 * y + 80 * n
            scr[:, :, at : at + 80] = piece[256 * y : 256 * y + 256].reshape(32, 8, 80)
            scr[:, y, 640 + 80 * n : 720 + 80 * n] = piece[512 + 32 * y : 544 + 32 * y]
    for b in range(12, 18):
        row, lane = GAINS[b]
        block = gain_ref[:, 128 * b : 128 * b + 128]
        scr[:, row, lane : lane + 128] = jnp.broadcast_to(block, (32, 128))
    late[...] = scr[...].astype(BF16)
    copy = pltpu.make_async_copy(late, out_hbm.at[:, :, pl.ds(MISC, LATE)], sem)
    copy.start()
    copy.wait()


def fill_rest(send, mine, got, tok, gain):
    vmem = pl.BlockSpec(memory_space=pltpu.VMEM)
    hbm = pl.BlockSpec(memory_space=pl.ANY)
    return pl.pallas_call(
        fill_rest_kernel,
        in_specs=[hbm] + [vmem] * 4,
        out_specs=hbm,
        out_shape=jax.ShapeDtypeStruct((32, 8, WIDE), BF16),
        scratch_shapes=[
            pltpu.VMEM((32, 8, LATE), F32),
            pltpu.VMEM((32, 8, LATE), BF16),
            pltpu.SemaphoreType.DMA,
        ],
        input_output_aliases={0: 0},
        name="fill_rest",
    )(send, mine, got, tok, gain)


def group_sums_kernel(yl_ref, recv_hbm, keep_ref, give_ref, both, recv, sems):
    loads = []
    for part in range(4):
        some = pl.ds(8 * part, 8)
        loads.append(pltpu.make_async_copy(recv_hbm.at[some], recv.at[some], sems.at[part]))
    for copy in loads:
        copy.start()
    def add(t, totals):
        sums = [x + recv[t, :, n * D : n * D + D].astype(F32) for n, x in enumerate(totals[:4])]
        return (*sums, totals[4] + recv[t, :, MISC + 640 :].astype(F32))

    def place_columns(t):
        cols = slice(36 * t, 36 * t + 36)
        x = recv[t, :, MISC + 256 : MISC + LATE].astype(F32)
        for y in range(2):
            at = 64 + 160 * y
            eight = x[:, at : at + 80] + x[:, at + 80 : at + 160]
            one = x[y : y + 1, 384:464] + x[y : y + 1, 464:544]
            for n in range(2):
                both[y, 1 + n, :8, cols] = eight[:, 40 * n : 40 * n + 36]
                both[y, 1 + n, 8:9, cols] = one[:, 40 * n : 40 * n + 36]

    sums = tuple(jnp.zeros((8, D), F32) for _ in range(4))
    sums = (*sums, jnp.zeros((8, WIDE - MISC - 640), F32))
    for part in range(4):
        loads[part].wait()
        sums = lax.fori_loop(8 * part, 8 * part + 8, add, sums)
        for t in range(8 * part, 8 * part + 8):
            place_columns(t)
    rest = sums[4]

    def slot(place):
        row, lane = place
        return rest[row : row + 1, lane - 640 : lane - 512]

    for y in range(2):
        for m in range(2):
            both[y, 3 * m, :8] = sums[2 * y + m]
            for b in range(9):
                at = 128 * b
                both[y, 3 * m, 8:9, at : at + 128] = slot(SLOTS[9 * (2 * y + m) + b])
        for b in range(9):
            at = 128 * b
            both[y, 0, 9:10, at : at + 128] = slot(GAINS[b]) + slot(GAINS[9 + b])
    for out, y in ((keep_ref, yl_ref[0]), (give_ref, 1 - yl_ref[0])):
        for m in range(4):
            out[:, m] = both[y, m, :10]


def group_sums(yl, recv):
    vmem = pl.BlockSpec(memory_space=pltpu.VMEM)
    return pl.pallas_call(
        group_sums_kernel,
        in_specs=[pl.BlockSpec(memory_space=pltpu.SMEM), pl.BlockSpec(memory_space=pl.ANY)],
        out_specs=[vmem] * 2,
        out_shape=[jax.ShapeDtypeStruct((10, 4, D), F32)] * 2,
        scratch_shapes=[
            pltpu.VMEM((2, 4, 16, D), F32),
            pltpu.VMEM((32, 8, WIDE), BF16),
            pltpu.SemaphoreType.DMA((4,)),
        ],
        name="group_sums",
    )(yl, recv)


def both_sums_kernel(keep_ref, got_ref, gw_ref, gain_ref):
    gw_ref[...] = keep_ref[:9] + got_ref[:9]
    gain = keep_ref[9, :1] + got_ref[9, :1]
    for b in range(9):
        gain_ref[b : b + 1] = gain[:, 128 * b : 128 * b + 128]


def both_sums(keep, got):
    vmem = pl.BlockSpec(memory_space=pltpu.VMEM)
    return pl.pallas_call(
        both_sums_kernel,
        in_specs=[vmem] * 2,
        out_specs=[vmem] * 2,
        out_shape=[jax.ShapeDtypeStruct((9, 4, D), F32), jax.ShapeDtypeStruct((9, 128), F32)],
        name="both_sums",
    )(keep, got)


def guide_grad_kernel(recv_hbm, wk_hbm, wv_hbm, gg_ref, tok, recv, wk, wv, sems):
    copies = [
        pltpu.make_async_copy(recv_hbm.at[:, :, pl.ds(MISC, 384)], recv, sems.at[0]),
        pltpu.make_async_copy(wk_hbm, wk, sems.at[1]),
        pltpu.make_async_copy(wv_hbm, wv, sems.at[2]),
    ]
    for copy in copies:
        copy.start()
    copies[0].wait()
    for t in range(32):
        near = recv[t].astype(F32)
        for n in range(2):
            for half in range(2):
                for m in range(2):
                    lane = 160 * half + 80 * m + 40 * n
                    row = 16 * m + 8 * half
                    tok[n, row : row + 8, 36 * t : 36 * t + 36] = near[:, lane : lane + 36]
    copies[1].wait()
    grad = dot(wk[...], tok[0].astype(BF16), 1, 1)
    copies[2].wait()
    grad = grad + dot(wv[...], tok[1].astype(BF16), 1, 1)
    gg_ref[...] = grad.T.astype(BF16)


def guide_grad(recv, w_key, w_value):
    hbm = pl.BlockSpec(memory_space=pl.ANY)
    return pl.pallas_call(
        guide_grad_kernel,
        in_specs=[hbm] * 3,
        out_specs=pl.BlockSpec(memory_space=pltpu.VMEM),
        out_shape=jax.ShapeDtypeStruct((32, D), BF16),
        scratch_shapes=[
            pltpu.VMEM((2, 32, D), F32),
            pltpu.VMEM((32, 8, 384), BF16),
            pltpu.VMEM((D, D), BF16),
            pltpu.VMEM((D, D), BF16),
            pltpu.SemaphoreType.DMA((3,)),
        ],
        name="guide_grad",
    )(recv, w_key, w_value)


def on_device(tiles, tile_image, guide, gain, w_query, w_key, w_value, w_out, grad_out):
    core = lax.axis_index("c")
    yl = lax.axis_index("yl")
    whole = lax.all_to_all(copies_of(guide), TILE_AXES, 0, 0, tiled=True)
    xf = tiles.astype(F32)
    rstd = lax.rsqrt(jnp.mean(xf * xf, axis=-1, keepdims=True) + 1e-06)
    normed = xf * rstd
    hidden = (normed * gain).astype(BF16)
    query = dot(hidden, w_query, 1, 0).astype(BF16)
    dout = dot(grad_out, w_out, 1, 1).astype(BF16)
    want = wanted_rows(core)
    hid_both = jnp.concatenate([hidden, lax.ppermute(hidden, "c", SWAP)], axis=0)
    hid_rows = dot(one_hot(want, D), hid_both, 1, 1).astype(BF16)
    grad_got = lax.ppermute(grad_out, "c", SWAP)
    query, hid_rows = lax.optimization_barrier((query, hid_rows))

    pay, outv, dq = attention(tile_image, whole, w_key, w_value, query, dout)
    got = lax.all_to_all(pay, TILE_AXES, 0, 0, tiled=True)

    dq_got = lax.ppermute(dq, "c", SWAP)
    out_got = lax.ppermute(outv, "c", SWAP)
    dh = dot(dq, w_query, 1, 1)
    gain_part = jnp.sum(dh * normed, axis=0, keepdims=True)
    gain_part = gain_part + lax.ppermute(gain_part, "c", SWAP)
    gain_high = lax.reduce_precision(gain_part, 8, 7)
    gains = jnp.concatenate([gain_high, gain_part - gain_high], axis=1)
    send = weight_parts(
        want, hid_rows, outv, out_got, dq, dq_got, grad_out, grad_got, gains
    )
    dn = dh * gain
    grad_tiles = (rstd * (dn - normed * jnp.mean(dn * normed, axis=-1, keepdims=True))).astype(BF16)

    got, send = lax.optimization_barrier((got, send))
    mine, theirs, tok = image_sums(core[None], got, whole)
    send = fill_rest(send, mine, lax.ppermute(theirs, "c", SWAP), tok, gains)
    recv = lax.all_to_all(send, TILE_AXES, 0, 0, tiled=True)
    recv, grad_tiles = lax.optimization_barrier((recv, grad_tiles))
    keep, give = group_sums(yl[None], recv)
    grad_weights, grad_gain = both_sums(keep, lax.ppermute(give, "yl", SWAP))
    grad_guide = guide_grad(recv, w_key, w_value).reshape(guide.shape)
    return (grad_tiles, grad_guide, grad_weights.transpose(1, 0, 2), grad_gain.reshape(D))


def solution(mesh):
    fine = Mesh(mesh.devices.reshape(2, 2, 4, 2, 4), ("yl", "c", "x", "yh", "z"))
    every = ("yl", "c", "x", "yh", "z")
    return jax.shard_map(
        on_device,
        mesh=fine,
        in_specs=(
            P(every, None),
            P(every),
            P(("yl", "c"), TILE_AXES, None),
            P(),
            P(),
            P(),
            P(),
            P(),
            P(every, None),
        ),
        out_specs=(
            P(every, None),
            P(("yl", "c"), TILE_AXES, None),
            P(None, every, None),
            P(),
        ),
        check_vma=False,
    )
```

```python
import jax
import jax.numpy as jnp
from jax import lax
from jax.experimental import pallas as pl
from jax.experimental.pallas import tpu as pltpu
from jax.sharding import Mesh, PartitionSpec as P

HEADS = 16
HD = 72
D = 1152
G = 512
F32 = jnp.float32
BF16 = jnp.bfloat16
TILE_AXES = ("x", "yh", "z")
SWAP = [(0, 1), (1, 0)]


def dot(a, b, ca, cb):
    return lax.dot_general(a, b, (((ca,), (cb,)), ((), ())), preferred_element_type=F32)


def copies_kernel(g_ref, out, sems):
    copies = [pltpu.make_async_copy(g_ref, out.at[i], sems.at[i]) for i in range(32)]
    for copy in copies:
        copy.start()
    for copy in copies:
        copy.wait()


def copies_of(guide):
    return pl.pallas_call(
        copies_kernel,
        in_specs=[pl.BlockSpec(memory_space=pltpu.VMEM)],
        out_specs=pl.BlockSpec(memory_space=pl.ANY),
        out_shape=jax.ShapeDtypeStruct((32, *guide.shape), guide.dtype),
        scratch_shapes=[pltpu.SemaphoreType.DMA((32,))],
        name="copies_of_guide",
    )(guide)


def attention_kernel(
    img_ref, g_hbm, wk_hbm, wv_hbm, q_ref, d_ref, pay_hbm, o_ref, dq_ref,
    guide, wk, wv, k_scr, v_scr, pay, sems, out_sems,
):
    loads = [
        pltpu.make_async_copy(g_hbm.at[:, img_ref[0]], guide, sems.at[0]),
        pltpu.make_async_copy(wk_hbm.at[:, pl.ds(0, 512)], wk.at[:, pl.ds(0, 512)], sems.at[1]),
        pltpu.make_async_copy(wk_hbm.at[:, pl.ds(512, 640)], wk.at[:, pl.ds(512, 640)], sems.at[2]),
        pltpu.make_async_copy(wv_hbm, wv, sems.at[3]),
    ]
    for copy in loads:
        copy.start()
    loads[0].wait()
    tokens = guide[...].reshape(G, D)
    loads[1].wait()
    k_scr[:, :512] = dot(tokens, wk[:, :512], 1, 0).astype(BF16)
    loads[2].wait()
    k_scr[:, 512:] = dot(tokens, wk[:, 512:], 1, 0).astype(BF16)
    loads[3].wait()
    v_scr[...] = dot(tokens, wv[...], 1, 0).astype(BF16)
    scale = HD ** (-0.5)
    flag = jnp.full((4, G), img_ref[0], jnp.int32).astype(F32)
    stores = []
    t = q_ref.shape[0]
    lane = lax.broadcasted_iota(jnp.int32, (t, 2 * HD), 1)
    none = jnp.zeros((t, 2 * HD), BF16)
    for h in range(0, HEADS, 2):
        cols = slice(h * HD, (h + 2) * HD)
        k, v = k_scr[:, cols], v_scr[:, cols]

        def both(x):
            return jnp.concatenate([jnp.where(lane < HD, x, none), jnp.where(lane < HD, none, x)], axis=0)

        def own(x):
            return jnp.where(lane < HD, x[:t], x[t:]).astype(BF16)

        q, d = both(q_ref[:, cols]), both(d_ref[:, cols])
        scores = dot(q, k, 1, 1) * scale
        dprob = dot(d, v, 1, 1)
        top = jnp.max(scores, axis=-1, keepdims=True)
        expo = jnp.exp(scores - top)
        probs = expo * (1.0 / jnp.sum(expo, axis=-1, keepdims=True))
        pb = probs.astype(BF16)
        weighted = probs * dprob
        delta = jnp.sum(weighted, axis=-1, keepdims=True)
        ds = ((weighted - probs * delta) * scale).astype(BF16)
        o_ref[:, cols] = own(dot(pb, v, 1, 0))
        dq_ref[:, cols] = own(dot(ds, k, 1, 0))
        for j, part in enumerate((dot(q, ds, 0, 0), dot(d, pb, 0, 0))):
            for i in range(4):
                rows = jnp.concatenate([part[36 * i : 36 * i + 36], flag], axis=0)
                pay[2 * h + i, j] = rows.astype(BF16)
        some = pl.ds(2 * h, 4)
        stores.append(pltpu.make_async_copy(pay.at[some], pay_hbm.at[some], out_sems.at[h // 2]))
        stores[-1].start()
    for copy in stores:
        copy.wait()


def attention(img, whole, w_key, w_value, q, d):
    t = q.shape[0]
    vmem = pl.BlockSpec(memory_space=pltpu.VMEM)
    hbm = pl.BlockSpec(memory_space=pl.ANY)
    return pl.pallas_call(
        attention_kernel,
        in_specs=[pl.BlockSpec(memory_space=pltpu.SMEM), hbm, hbm, hbm, vmem, vmem],
        out_specs=[hbm, vmem, vmem],
        out_shape=[
            jax.ShapeDtypeStruct((32, 2, 40, G), BF16),
            jax.ShapeDtypeStruct((t, D), BF16),
            jax.ShapeDtypeStruct((t, D), BF16),
        ],
        scratch_shapes=[
            pltpu.VMEM((32, 16, D), BF16),
            pltpu.VMEM((D, D), BF16),
            pltpu.VMEM((D, D), BF16),
            pltpu.VMEM((G, D), BF16),
            pltpu.VMEM((G, D), BF16),
            pltpu.VMEM((32, 2, 40, G), BF16),
            pltpu.SemaphoreType.DMA((4,)),
            pltpu.SemaphoreType.DMA((HEADS // 2,)),
        ],
        name="attention",
    )(img, whole, w_key, w_value, q, d)


ROWS = 576


def eight_and_one(rows):
    return jnp.where(rows < 512, rows // 8 * 9 + rows % 8, (rows - 512) * 9 + 8)


def wanted_rows(core):
    row = eight_and_one(jnp.arange(ROWS, dtype=jnp.int32))
    return (row // 288 * 576 + core * 288 + row % 288)[:, None]


def one_hot(want, width):
    return (want == lax.broadcasted_iota(jnp.int32, (want.shape[0], width), 1)).astype(BF16)


MISC = 4 * D
LATE = 896
WIDE = MISC + LATE + 768
SLOTS = [(row, lane) for lane in range(LATE, LATE + 768, 128) for row in range(8)]
GAINS = SLOTS[36:] + [(row, 640) for row in range(2, 8)]


def weight_parts_kernel(
    want_ref, hid_ref, o_ref, o2_ref, dq_ref, dq2_ref, g_ref, g2_ref, gain_ref, send_ref, scr
):
    o = jnp.concatenate([o_ref[...], o2_ref[...]], axis=0)
    dq = jnp.concatenate([dq_ref[...], dq2_ref[...]], axis=0)
    g = jnp.concatenate([g_ref[...], g2_ref[...]], axis=0)
    o_rows = dot(one_hot(want_ref[...], D), o, 1, 1).astype(BF16)
    parts = (dot(hid_ref[...], dq, 1, 0), dot(o_rows, g, 1, 0))
    for m, part in enumerate(parts):
        for y in range(2):
            at = (2 * y + m) * D
            eight = part[256 * y : 256 * y + 256].reshape(32, 8, D)
            send_ref[:, :, at : at + D] = eight.astype(BF16)
            for b in range(9):
                row, lane = SLOTS[9 * (2 * y + m) + b]
                ninth = part[512 + 32 * y : 544 + 32 * y, 128 * b : 128 * b + 128]
                scr[:, row, lane - LATE : lane - LATE + 128] = ninth
    for b in range(12):
        row, lane = GAINS[b]
        block = gain_ref[:, 128 * b : 128 * b + 128]
        scr[:, row, lane - LATE : lane - LATE + 128] = jnp.broadcast_to(block, (32, 128))
    send_ref[:, :, MISC + LATE :] = scr[...].astype(BF16)


def weight_parts(*args):
    vmem = pl.BlockSpec(memory_space=pltpu.VMEM)
    return pl.pallas_call(
        weight_parts_kernel,
        in_specs=[vmem] * 9,
        out_specs=vmem,
        out_shape=jax.ShapeDtypeStruct((32, 8, WIDE), BF16),
        scratch_shapes=[pltpu.VMEM((32, 8, 768), F32)],
        name="weight_parts",
    )(*args)


def image_sums_kernel(core_ref, got_hbm, g_hbm, mine_ref, theirs_ref, tok_ref, scr, got, guide, sems):
    loads = []
    for n in range(2):
        for part in range(2):
            some = pl.ds(16 * part, 16)
            sem = sems.at[2 * n + part]
            loads.append(pltpu.make_async_copy(got_hbm.at[some, n], got.at[n, some], sem))
    last = pltpu.make_async_copy(g_hbm, guide, sems.at[4])
    for copy in loads + [last]:
        copy.start()
    zero = jnp.zeros((40, G), F32)
    sums = [None, None]
    for n in range(2):

        def add(s, pair, n=n):
            terms = got[n, s].astype(F32)
            first = terms[36:37, :] == 0.0
            return pair[0] + jnp.where(first, terms, zero), pair[1] + jnp.where(first, zero, terms)

        pair = (zero, zero)
        for part in range(2):
            loads[2 * n + part].wait()
            pair = lax.fori_loop(16 * part, 16 * part + 16, add, pair)
        sums[n] = pair
    rounded = [jnp.concatenate([sums[0][m], sums[1][m]], axis=0).astype(BF16) for m in range(2)]
    last.wait()
    prod = dot(rounded[0], guide[:, 0].reshape(G, D), 1, 0)
    prod = prod + dot(rounded[1], guide[:, 1].reshape(G, D), 1, 0)
    scr[...] = jnp.concatenate([prod, jnp.zeros((48, D), F32)], axis=0).T
    core = core_ref[0]
    for n in range(2):
        for out, c in ((mine_ref, core), (theirs_ref, 1 - core)):
            start = pl.multiple_of(n * 576 + c * 288, 32)
            out[n * 288 : n * 288 + 288] = scr[pl.ds(start, 288), :]
    tok_ref[:80] = rounded[0]
    tok_ref[80:] = rounded[1]


def image_sums(core, got, whole):
    vmem = pl.BlockSpec(memory_space=pltpu.VMEM)
    hbm = pl.BlockSpec(memory_space=pl.ANY)
    return pl.pallas_call(
        image_sums_kernel,
        in_specs=[pl.BlockSpec(memory_space=pltpu.SMEM), hbm, hbm],
        out_specs=[vmem] * 3,
        out_shape=[
            jax.ShapeDtypeStruct((ROWS, 128), F32),
            jax.ShapeDtypeStruct((ROWS, 128), F32),
            jax.ShapeDtypeStruct((160, G), BF16),
        ],
        scratch_shapes=[
            pltpu.VMEM((D, 128), F32),
            pltpu.VMEM((2, 32, 40, G), BF16),
            pltpu.VMEM((32, 2, 16, D), BF16),
            pltpu.SemaphoreType.DMA((5,)),
        ],
        name="image_sums",
    )(core, got, whole)


def fill_rest_kernel(send_hbm, mine_ref, got_ref, tok_ref, gain_ref, out_hbm, scr, late, sem):
    total = mine_ref[...] + got_ref[...]
    high = total.astype(BF16)
    low = (total - high.astype(F32)).astype(BF16)
    want = eight_and_one(lax.broadcasted_iota(jnp.int32, (ROWS, ROWS), 0))
    order = (want == lax.broadcasted_iota(jnp.int32, (ROWS, ROWS), 1)).astype(BF16)
    moved = dot(order, jnp.concatenate([high, low], axis=1), 1, 0)
    scr[:, :, 640:] = jnp.zeros((32, 8, LATE - 640), F32)
    rows = jnp.concatenate([tok_ref[...].astype(F32), jnp.zeros((96, G), F32)], axis=0)
    tok = rows.T.reshape(32, 16, 256)
    for half in range(2):
        scr[:, :, 160 * half : 160 * half + 160] = tok[:, 8 * half : 8 * half + 8, :160]
    for y in range(2):
        for n in range(2):
            piece = moved[:, 128 * n : 128 * n + 80]
            at = 320 + 160 * y + 80 * n
            scr[:, :, at : at + 80] = piece[256 * y : 256 * y + 256].reshape(32, 8, 80)
            scr[:, y, 640 + 80 * n : 720 + 80 * n] = piece[512 + 32 * y : 544 + 32 * y]
    for b in range(12, 18):
        row, lane = GAINS[b]
        block = gain_ref[:, 128 * b : 128 * b + 128]
        scr[:, row, lane : lane + 128] = jnp.broadcast_to(block, (32, 128))
    late[...] = scr[...].astype(BF16)
    copy = pltpu.make_async_copy(late, out_hbm.at[:, :, pl.ds(MISC, LATE)], sem)
    copy.start()
    copy.wait()


def fill_rest(send, mine, got, tok, gain):
    vmem = pl.BlockSpec(memory_space=pltpu.VMEM)
    hbm = pl.BlockSpec(memory_space=pl.ANY)
    return pl.pallas_call(
        fill_rest_kernel,
        in_specs=[hbm] + [vmem] * 4,
        out_specs=hbm,
        out_shape=jax.ShapeDtypeStruct((32, 8, WIDE), BF16),
        scratch_shapes=[
            pltpu.VMEM((32, 8, LATE), F32),
            pltpu.VMEM((32, 8, LATE), BF16),
            pltpu.SemaphoreType.DMA,
        ],
        input_output_aliases={0: 0},
        name="fill_rest",
    )(send, mine, got, tok, gain)


def group_sums_kernel(yl_ref, recv_hbm, keep_ref, give_ref, gain_ref, both, recv, sems):
    loads = []
    for part in range(4):
        some = pl.ds(8 * part, 8)
        loads.append(pltpu.make_async_copy(recv_hbm.at[some], recv.at[some], sems.at[part]))
    for copy in loads:
        copy.start()
    def add(t, totals):
        sums = [x + recv[t, :, n * D : n * D + D].astype(F32) for n, x in enumerate(totals[:4])]
        return (*sums, totals[4] + recv[t, :, MISC + 640 :].astype(F32))

    def place_columns(t):
        cols = slice(36 * t, 36 * t + 36)
        x = recv[t, :, MISC + 256 : MISC + LATE].astype(F32)
        for y in range(2):
            at = 64 + 160 * y
            eight = x[:, at : at + 80] + x[:, at + 80 : at + 160]
            one = x[y : y + 1, 384:464] + x[y : y + 1, 464:544]
            for n in range(2):
                both[y, 1 + n, :8, cols] = eight[:, 40 * n : 40 * n + 36]
                both[y, 1 + n, 8:9, cols] = one[:, 40 * n : 40 * n + 36]

    sums = tuple(jnp.zeros((8, D), F32) for _ in range(4))
    sums = (*sums, jnp.zeros((8, WIDE - MISC - 640), F32))
    for part in range(4):
        loads[part].wait()
        sums = lax.fori_loop(8 * part, 8 * part + 8, add, sums)
        for t in range(8 * part, 8 * part + 8):
            place_columns(t)
    rest = sums[4]

    def slot(place):
        row, lane = place
        return rest[row : row + 1, lane - 640 : lane - 512]

    for y in range(2):
        for m in range(2):
            both[y, 3 * m, :8] = sums[2 * y + m]
            for b in range(9):
                at = 128 * b
                both[y, 3 * m, 8:9, at : at + 128] = slot(SLOTS[9 * (2 * y + m) + b])
    for b in range(9):
        gain_ref[b : b + 1] = slot(GAINS[b]) + slot(GAINS[9 + b])
    for out, y in ((keep_ref, yl_ref[0]), (give_ref, 1 - yl_ref[0])):
        for m in range(4):
            out[:, m] = both[y, m, :9]


def group_sums(yl, recv):
    vmem = pl.BlockSpec(memory_space=pltpu.VMEM)
    return pl.pallas_call(
        group_sums_kernel,
        in_specs=[pl.BlockSpec(memory_space=pltpu.SMEM), pl.BlockSpec(memory_space=pl.ANY)],
        out_specs=[vmem] * 3,
        out_shape=[jax.ShapeDtypeStruct((9, 4, D), F32)] * 2 + [jax.ShapeDtypeStruct((9, 128), F32)],
        scratch_shapes=[
            pltpu.VMEM((2, 4, 16, D), F32),
            pltpu.VMEM((32, 8, WIDE), BF16),
            pltpu.SemaphoreType.DMA((4,)),
        ],
        name="group_sums",
    )(yl, recv)


def guide_grad_kernel(recv_hbm, wk_hbm, wv_hbm, gg_ref, tok, recv, wk, wv, sems):
    copies = [
        pltpu.make_async_copy(recv_hbm.at[:, :, pl.ds(MISC, 384)], recv, sems.at[0]),
        pltpu.make_async_copy(wk_hbm, wk, sems.at[1]),
        pltpu.make_async_copy(wv_hbm, wv, sems.at[2]),
    ]
    for copy in copies:
        copy.start()
    copies[0].wait()
    for t in range(32):
        near = recv[t].astype(F32)
        for n in range(2):
            for half in range(2):
                for m in range(2):
                    lane = 160 * half + 80 * m + 40 * n
                    row = 16 * m + 8 * half
                    tok[n, row : row + 8, 36 * t : 36 * t + 36] = near[:, lane : lane + 36]
    copies[1].wait()
    grad = dot(wk[...], tok[0].astype(BF16), 1, 1)
    copies[2].wait()
    grad = grad + dot(wv[...], tok[1].astype(BF16), 1, 1)
    gg_ref[...] = grad.T.astype(BF16)


def guide_grad(recv, w_key, w_value):
    hbm = pl.BlockSpec(memory_space=pl.ANY)
    return pl.pallas_call(
        guide_grad_kernel,
        in_specs=[hbm] * 3,
        out_specs=pl.BlockSpec(memory_space=pltpu.VMEM),
        out_shape=jax.ShapeDtypeStruct((32, D), BF16),
        scratch_shapes=[
            pltpu.VMEM((2, 32, D), F32),
            pltpu.VMEM((32, 8, 384), BF16),
            pltpu.VMEM((D, D), BF16),
            pltpu.VMEM((D, D), BF16),
            pltpu.SemaphoreType.DMA((3,)),
        ],
        name="guide_grad",
    )(recv, w_key, w_value)


def on_device(tiles, tile_image, guide, gain, w_query, w_key, w_value, w_out, grad_out):
    core = lax.axis_index("c")
    yl = lax.axis_index("yl")
    whole = lax.all_to_all(copies_of(guide), TILE_AXES, 0, 0, tiled=True)
    xf = tiles.astype(F32)
    rstd = lax.rsqrt(jnp.mean(xf * xf, axis=-1, keepdims=True) + 1e-06)
    normed = xf * rstd
    hidden = (normed * gain).astype(BF16)
    query = dot(hidden, w_query, 1, 0).astype(BF16)
    dout = dot(grad_out, w_out, 1, 1).astype(BF16)
    want = wanted_rows(core)
    hid_both = jnp.concatenate([hidden, lax.ppermute(hidden, "c", SWAP)], axis=0)
    hid_rows = dot(one_hot(want, D), hid_both, 1, 1).astype(BF16)
    grad_got = lax.ppermute(grad_out, "c", SWAP)
    query, hid_rows = lax.optimization_barrier((query, hid_rows))

    pay, outv, dq = attention(tile_image, whole, w_key, w_value, query, dout)
    got = lax.all_to_all(pay, TILE_AXES, 0, 0, tiled=True)

    dq_got = lax.ppermute(dq, "c", SWAP)
    out_got = lax.ppermute(outv, "c", SWAP)
    dh = dot(dq, w_query, 1, 1)
    gain_part = jnp.sum(dh * normed, axis=0, keepdims=True)
    gain_part = gain_part + lax.ppermute(gain_part, "c", SWAP)
    gain_high = lax.reduce_precision(gain_part, 8, 7)
    gains = jnp.concatenate([gain_high, gain_part - gain_high], axis=1)
    send = weight_parts(
        want, hid_rows, outv, out_got, dq, dq_got, grad_out, grad_got, gains
    )
    dn = dh * gain
    grad_tiles = (rstd * (dn - normed * jnp.mean(dn * normed, axis=-1, keepdims=True))).astype(BF16)

    got, send = lax.optimization_barrier((got, send))
    mine, theirs, tok = image_sums(core[None], got, whole)
    send = fill_rest(send, mine, lax.ppermute(theirs, "c", SWAP), tok, gains)
    recv = lax.all_to_all(send, TILE_AXES, 0, 0, tiled=True)
    recv, grad_tiles = lax.optimization_barrier((recv, grad_tiles))
    keep, give, grad_gain = group_sums(yl[None], recv)
    grad_weights = keep + lax.ppermute(give, "yl", SWAP)
    grad_gain = grad_gain + lax.ppermute(grad_gain, "yl", SWAP)
    grad_guide = guide_grad(recv, w_key, w_value).reshape(guide.shape)
    return (grad_tiles, grad_guide, grad_weights.transpose(1, 0, 2), grad_gain.reshape(D))


def solution(mesh):
    fine = Mesh(mesh.devices.reshape(2, 2, 4, 2, 4), ("yl", "c", "x", "yh", "z"))
    every = ("yl", "c", "x", "yh", "z")
    return jax.shard_map(
        on_device,
        mesh=fine,
        in_specs=(
            P(every, None),
            P(every),
            P(("yl", "c"), TILE_AXES, None),
            P(),
            P(),
            P(),
            P(),
            P(),
            P(every, None),
        ),
        out_specs=(
            P(every, None),
            P(("yl", "c"), TILE_AXES, None),
            P(None, every, None),
            P(),
        ),
        check_vma=False,
    )
```

```python
import jax
import jax.numpy as jnp
from jax import lax
from jax.experimental import pallas as pl
from jax.experimental.pallas import tpu as pltpu
from jax.sharding import Mesh, PartitionSpec as P


HEADS = 16
HD = 72
D = 1152
G = 512
F32 = jnp.float32
BF16 = jnp.bfloat16
TILE_AXES = ("x", "yh", "z")
SWAP = [(0, 1), (1, 0)]


def dot(a, b, ca, cb):
    return lax.dot_general(a, b, (((ca,), (cb,)), ((), ())), preferred_element_type=F32)


def copies_kernel(g_ref, out, sems):
    copies = [pltpu.make_async_copy(g_ref, out.at[i], sems.at[i]) for i in range(32)]
    for copy in copies:
        copy.start()
    for copy in copies:
        copy.wait()


def copies_of(guide):
    return pl.pallas_call(
        copies_kernel,
        in_specs=[pl.BlockSpec(memory_space=pltpu.VMEM)],
        out_specs=pl.BlockSpec(memory_space=pl.ANY),
        out_shape=jax.ShapeDtypeStruct((32, *guide.shape), guide.dtype),
        scratch_shapes=[pltpu.SemaphoreType.DMA((32,))],
        name="copies_of_guide",
    )(guide)


def attention_kernel(
    img_ref, g_hbm, wk_hbm, wv_hbm, q_ref, d_ref, pay_hbm, o_ref, dq_ref,
    guide, wk, wv, k_scr, v_scr, pay, sems, out_sems,
):
    loads = [
        pltpu.make_async_copy(g_hbm.at[:, img_ref[0]], guide, sems.at[0]),
        pltpu.make_async_copy(wk_hbm.at[:, pl.ds(0, 512)], wk.at[:, pl.ds(0, 512)], sems.at[1]),
        pltpu.make_async_copy(wk_hbm.at[:, pl.ds(512, 640)], wk.at[:, pl.ds(512, 640)], sems.at[2]),
        pltpu.make_async_copy(wv_hbm, wv, sems.at[3]),
    ]
    for copy in loads:
        copy.start()
    loads[0].wait()
    tokens = guide[...].reshape(G, D)
    loads[1].wait()
    k_scr[:, :512] = dot(tokens, wk[:, :512], 1, 0).astype(BF16)
    loads[2].wait()
    k_scr[:, 512:] = dot(tokens, wk[:, 512:], 1, 0).astype(BF16)
    loads[3].wait()
    v_scr[...] = dot(tokens, wv[...], 1, 0).astype(BF16)
    scale = HD ** (-0.5)
    flag = jnp.full((4, G), img_ref[0], jnp.int32).astype(F32)
    stores = []
    t = q_ref.shape[0]
    lane = lax.broadcasted_iota(jnp.int32, (t, 2 * HD), 1)
    none = jnp.zeros((t, 2 * HD), BF16)
    for h in range(0, HEADS, 2):
        cols = slice(h * HD, (h + 2) * HD)
        k, v = k_scr[:, cols], v_scr[:, cols]

        def both(x):
            return jnp.concatenate([jnp.where(lane < HD, x, none), jnp.where(lane < HD, none, x)], axis=0)

        def own(x):
            return jnp.where(lane < HD, x[:t], x[t:]).astype(BF16)

        q, d = both(q_ref[:, cols]), both(d_ref[:, cols])
        scores = dot(q, k, 1, 1) * scale
        dprob = dot(d, v, 1, 1)
        top = jnp.max(scores, axis=-1, keepdims=True)
        expo = jnp.exp(scores - top)
        probs = expo * (1.0 / jnp.sum(expo, axis=-1, keepdims=True))
        pb = probs.astype(BF16)
        weighted = probs * dprob
        delta = jnp.sum(weighted, axis=-1, keepdims=True)
        ds = ((weighted - probs * delta) * scale).astype(BF16)
        o_ref[:, cols] = own(dot(pb, v, 1, 0))
        dq_ref[:, cols] = own(dot(ds, k, 1, 0))
        for j, part in enumerate((dot(q, ds, 0, 0), dot(d, pb, 0, 0))):
            for i in range(4):
                rows = jnp.concatenate([part[36 * i : 36 * i + 36], flag], axis=0)
                pay[2 * h + i, j] = rows.astype(BF16)
        some = pl.ds(2 * h, 4)
        stores.append(pltpu.make_async_copy(pay.at[some], pay_hbm.at[some], out_sems.at[h // 2]))
        stores[-1].start()
    for copy in stores:
        copy.wait()


def attention(img, whole, w_key, w_value, q, d):
    t = q.shape[0]
    vmem = pl.BlockSpec(memory_space=pltpu.VMEM)
    hbm = pl.BlockSpec(memory_space=pl.ANY)
    return pl.pallas_call(
        attention_kernel,
        in_specs=[pl.BlockSpec(memory_space=pltpu.SMEM), hbm, hbm, hbm, vmem, vmem],
        out_specs=[hbm, vmem, vmem],
        out_shape=[
            jax.ShapeDtypeStruct((32, 2, 40, G), BF16),
            jax.ShapeDtypeStruct((t, D), BF16),
            jax.ShapeDtypeStruct((t, D), BF16),
        ],
        scratch_shapes=[
            pltpu.VMEM((32, 16, D), BF16),
            pltpu.VMEM((D, D), BF16),
            pltpu.VMEM((D, D), BF16),
            pltpu.VMEM((G, D), BF16),
            pltpu.VMEM((G, D), BF16),
            pltpu.VMEM((32, 2, 40, G), BF16),
            pltpu.SemaphoreType.DMA((4,)),
            pltpu.SemaphoreType.DMA((HEADS // 2,)),
        ],
        name="attention",
    )(img, whole, w_key, w_value, q, d)


ROWS = 576


def eight_and_one(rows):
    return jnp.where(rows < 512, rows // 8 * 9 + rows % 8, (rows - 512) * 9 + 8)


def wanted_rows(core):
    row = eight_and_one(jnp.arange(ROWS, dtype=jnp.int32))
    return (row // 288 * 576 + core * 288 + row % 288)[:, None]


def one_hot(want, width):
    return (want == lax.broadcasted_iota(jnp.int32, (want.shape[0], width), 1)).astype(BF16)


MISC = 4 * D
LATE = 896
WIDE = MISC + LATE + 768
SLOTS = [(row, lane) for lane in range(LATE, LATE + 768, 128) for row in range(8)]
GAINS = SLOTS[36:] + [(row, 640) for row in range(2, 8)]


def weight_parts_kernel(
    want_ref, hid_ref, o_ref, o2_ref, dq_ref, dq2_ref, g_ref, g2_ref, gain_ref, send_ref, scr
):
    o = jnp.concatenate([o_ref[...], o2_ref[...]], axis=0)
    dq = jnp.concatenate([dq_ref[...], dq2_ref[...]], axis=0)
    g = jnp.concatenate([g_ref[...], g2_ref[...]], axis=0)
    o_rows = dot(one_hot(want_ref[...], D), o, 1, 1).astype(BF16)
    parts = (dot(hid_ref[...], dq, 1, 0), dot(o_rows, g, 1, 0))
    for m, part in enumerate(parts):
        for y in range(2):
            at = (2 * y + m) * D
            eight = part[256 * y : 256 * y + 256].reshape(32, 8, D)
            send_ref[:, :, at : at + D] = eight.astype(BF16)
            for b in range(9):
                row, lane = SLOTS[9 * (2 * y + m) + b]
                ninth = part[512 + 32 * y : 544 + 32 * y, 128 * b : 128 * b + 128]
                scr[:, row, lane - LATE : lane - LATE + 128] = ninth
    for b in range(12):
        row, lane = GAINS[b]
        block = gain_ref[:, 128 * b : 128 * b + 128]
        scr[:, row, lane - LATE : lane - LATE + 128] = jnp.broadcast_to(block, (32, 128))
    send_ref[:, :, MISC + LATE :] = scr[...].astype(BF16)


def weight_parts(*args):
    vmem = pl.BlockSpec(memory_space=pltpu.VMEM)
    return pl.pallas_call(
        weight_parts_kernel,
        in_specs=[vmem] * 9,
        out_specs=vmem,
        out_shape=jax.ShapeDtypeStruct((32, 8, WIDE), BF16),
        scratch_shapes=[pltpu.VMEM((32, 8, 768), F32)],
        name="weight_parts",
    )(*args)


def image_sums_kernel(core_ref, got_hbm, g_hbm, mine_ref, theirs_ref, tok_ref, scr, got, guide, sems):
    loads = []
    for n in range(2):
        for part in range(2):
            some = pl.ds(16 * part, 16)
            sem = sems.at[2 * n + part]
            loads.append(pltpu.make_async_copy(got_hbm.at[some, n], got.at[n, some], sem))
    last = pltpu.make_async_copy(g_hbm, guide, sems.at[4])
    for copy in loads + [last]:
        copy.start()
    zero = jnp.zeros((40, G), F32)
    sums = [None, None]
    for n in range(2):

        def add(s, pair, n=n):
            terms = got[n, s].astype(F32)
            first = terms[36:37, :] == 0.0
            return pair[0] + jnp.where(first, terms, zero), pair[1] + jnp.where(first, zero, terms)

        pair = (zero, zero)
        for part in range(2):
            loads[2 * n + part].wait()
            pair = lax.fori_loop(16 * part, 16 * part + 16, add, pair)
        sums[n] = pair
    rounded = [jnp.concatenate([sums[0][m], sums[1][m]], axis=0).astype(BF16) for m in range(2)]
    last.wait()
    prod = dot(rounded[0], guide[:, 0].reshape(G, D), 1, 0)
    prod = prod + dot(rounded[1], guide[:, 1].reshape(G, D), 1, 0)
    scr[...] = jnp.concatenate([prod, jnp.zeros((48, D), F32)], axis=0).T
    core = core_ref[0]
    for n in range(2):
        for out, c in ((mine_ref, core), (theirs_ref, 1 - core)):
            start = pl.multiple_of(n * 576 + c * 288, 32)
            out[n * 288 : n * 288 + 288] = scr[pl.ds(start, 288), :]
    tok_ref[:80] = rounded[0]
    tok_ref[80:] = rounded[1]


def image_sums(core, got, whole):
    vmem = pl.BlockSpec(memory_space=pltpu.VMEM)
    hbm = pl.BlockSpec(memory_space=pl.ANY)
    return pl.pallas_call(
        image_sums_kernel,
        in_specs=[pl.BlockSpec(memory_space=pltpu.SMEM), hbm, hbm],
        out_specs=[vmem] * 3,
        out_shape=[
            jax.ShapeDtypeStruct((ROWS, 128), F32),
            jax.ShapeDtypeStruct((ROWS, 128), F32),
            jax.ShapeDtypeStruct((160, G), BF16),
        ],
        scratch_shapes=[
            pltpu.VMEM((D, 128), F32),
            pltpu.VMEM((2, 32, 40, G), BF16),
            pltpu.VMEM((32, 2, 16, D), BF16),
            pltpu.SemaphoreType.DMA((5,)),
        ],
        name="image_sums",
    )(core, got, whole)


def fill_rest_kernel(send_hbm, mine_ref, got_ref, tok_ref, gain_ref, out_hbm, scr, late, sem):
    total = mine_ref[...] + got_ref[...]
    high = total.astype(BF16)
    low = (total - high.astype(F32)).astype(BF16)
    want = eight_and_one(lax.broadcasted_iota(jnp.int32, (ROWS, ROWS), 0))
    order = (want == lax.broadcasted_iota(jnp.int32, (ROWS, ROWS), 1)).astype(BF16)
    moved = dot(order, jnp.concatenate([high, low], axis=1), 1, 0)
    scr[:, :, 640:] = jnp.zeros((32, 8, LATE - 640), F32)
    rows = jnp.concatenate([tok_ref[...].astype(F32), jnp.zeros((96, G), F32)], axis=0)
    tok = rows.T.reshape(32, 16, 256)
    for half in range(2):
        scr[:, :, 160 * half : 160 * half + 160] = tok[:, 8 * half : 8 * half + 8, :160]
    for y in range(2):
        for n in range(2):
            piece = moved[:, 128 * n : 128 * n + 80]
            at = 320 + 160 * y + 80 * n
            scr[:, :, at : at + 80] = piece[256 * y : 256 * y + 256].reshape(32, 8, 80)
            scr[:, y, 640 + 80 * n : 720 + 80 * n] = piece[512 + 32 * y : 544 + 32 * y]
    for b in range(12, 18):
        row, lane = GAINS[b]
        block = gain_ref[:, 128 * b : 128 * b + 128]
        scr[:, row, lane : lane + 128] = jnp.broadcast_to(block, (32, 128))
    late[...] = scr[...].astype(BF16)
    copy = pltpu.make_async_copy(late, out_hbm.at[:, :, pl.ds(MISC, LATE)], sem)
    copy.start()
    copy.wait()


def fill_rest(send, mine, got, tok, gain):
    vmem = pl.BlockSpec(memory_space=pltpu.VMEM)
    hbm = pl.BlockSpec(memory_space=pl.ANY)
    return pl.pallas_call(
        fill_rest_kernel,
        in_specs=[hbm] + [vmem] * 4,
        out_specs=hbm,
        out_shape=jax.ShapeDtypeStruct((32, 8, WIDE), BF16),
        scratch_shapes=[
            pltpu.VMEM((32, 8, LATE), F32),
            pltpu.VMEM((32, 8, LATE), BF16),
            pltpu.SemaphoreType.DMA,
        ],
        input_output_aliases={0: 0},
        name="fill_rest",
    )(send, mine, got, tok, gain)


def group_sums_kernel(yl_ref, recv_hbm, keep_ref, give_ref, gain_ref, both, recv, sems):
    loads = []
    for part in range(4):
        some = pl.ds(8 * part, 8)
        loads.append(pltpu.make_async_copy(recv_hbm.at[some], recv.at[some], sems.at[part]))
    for copy in loads:
        copy.start()

    def add(t, totals):
        sums = [x + recv[t, :, n * D : n * D + D].astype(F32) for n, x in enumerate(totals[:4])]
        return (*sums, totals[4] + recv[t, :, MISC + 640 :].astype(F32))

    def place_columns(t):
        cols = slice(36 * t, 36 * t + 36)
        x = recv[t, :, MISC + 256 : MISC + LATE].astype(F32)
        for y in range(2):
            at = 64 + 160 * y
            eight = x[:, at : at + 80] + x[:, at + 80 : at + 160]
            one = x[y : y + 1, 384:464] + x[y : y + 1, 464:544]
            for n in range(2):
                both[y, 1 + n, :8, cols] = eight[:, 40 * n : 40 * n + 36]
                both[y, 1 + n, 8:9, cols] = one[:, 40 * n : 40 * n + 36]

    sums = tuple(jnp.zeros((8, D), F32) for _ in range(4))
    sums = (*sums, jnp.zeros((8, WIDE - MISC - 640), F32))
    for part in range(4):
        loads[part].wait()
        sums = lax.fori_loop(8 * part, 8 * part + 8, add, sums)
        for t in range(8 * part, 8 * part + 8):
            place_columns(t)
    rest = sums[4]

    def slot(place):
        row, lane = place
        return rest[row : row + 1, lane - 640 : lane - 512]

    for y in range(2):
        for m in range(2):
            both[y, 3 * m, :8] = sums[2 * y + m]
            for b in range(9):
                at = 128 * b
                both[y, 3 * m, 8:9, at : at + 128] = slot(SLOTS[9 * (2 * y + m) + b])
    for b in range(9):
        gain_ref[b : b + 1] = slot(GAINS[b]) + slot(GAINS[9 + b])
    for out, y in ((keep_ref, yl_ref[0]), (give_ref, 1 - yl_ref[0])):
        for m in range(4):
            out[:, m] = both[y, m, :9]


def group_sums(yl, recv):
    vmem = pl.BlockSpec(memory_space=pltpu.VMEM)
    return pl.pallas_call(
        group_sums_kernel,
        in_specs=[pl.BlockSpec(memory_space=pltpu.SMEM), pl.BlockSpec(memory_space=pl.ANY)],
        out_specs=[vmem] * 3,
        out_shape=[jax.ShapeDtypeStruct((9, 4, D), F32)] * 2 + [jax.ShapeDtypeStruct((9, 128), F32)],
        scratch_shapes=[
            pltpu.VMEM((2, 4, 16, D), F32),
            pltpu.VMEM((32, 8, WIDE), BF16),
            pltpu.SemaphoreType.DMA((4,)),
        ],
        name="group_sums",
    )(yl, recv)


def guide_grad_kernel(recv_hbm, wk_hbm, wv_hbm, gg_ref, tok, recv, wk, wv, sems):
    copies = [
        pltpu.make_async_copy(recv_hbm.at[:, :, pl.ds(MISC, 384)], recv, sems.at[0]),
        pltpu.make_async_copy(wk_hbm, wk, sems.at[1]),
        pltpu.make_async_copy(wv_hbm, wv, sems.at[2]),
    ]
    for copy in copies:
        copy.start()
    copies[0].wait()
    for t in range(32):
        near = recv[t].astype(F32)
        for n in range(2):
            for half in range(2):
                for m in range(2):
                    lane = 160 * half + 80 * m + 40 * n
                    row = 16 * m + 8 * half
                    tok[n, row : row + 8, 36 * t : 36 * t + 36] = near[:, lane : lane + 36]
    copies[1].wait()
    grad = dot(wk[...], tok[0].astype(BF16), 1, 1)
    copies[2].wait()
    grad = grad + dot(wv[...], tok[1].astype(BF16), 1, 1)
    gg_ref[...] = grad.T.astype(BF16)


def guide_grad(recv, w_key, w_value):
    hbm = pl.BlockSpec(memory_space=pl.ANY)
    return pl.pallas_call(
        guide_grad_kernel,
        in_specs=[hbm] * 3,
        out_specs=pl.BlockSpec(memory_space=pltpu.VMEM),
        out_shape=jax.ShapeDtypeStruct((32, D), BF16),
        scratch_shapes=[
            pltpu.VMEM((2, 32, D), F32),
            pltpu.VMEM((32, 8, 384), BF16),
            pltpu.VMEM((D, D), BF16),
            pltpu.VMEM((D, D), BF16),
            pltpu.SemaphoreType.DMA((3,)),
        ],
        name="guide_grad",
    )(recv, w_key, w_value)


def on_device(tiles, tile_image, guide, gain, w_query, w_key, w_value, w_out, grad_out):
    core = lax.axis_index("c")
    yl = lax.axis_index("yl")
    whole = lax.all_to_all(copies_of(guide), TILE_AXES, 0, 0, tiled=True)
    xf = tiles.astype(F32)
    rstd = lax.rsqrt(jnp.mean(xf * xf, axis=-1, keepdims=True) + 1e-06)
    normed = xf * rstd
    hidden = (normed * gain).astype(BF16)
    query = dot(hidden, w_query, 1, 0).astype(BF16)
    dout = dot(grad_out, w_out, 1, 1).astype(BF16)
    want = wanted_rows(core)
    hid_both = jnp.concatenate([hidden, lax.ppermute(hidden, "c", SWAP)], axis=0)
    hid_rows = dot(one_hot(want, D), hid_both, 1, 1).astype(BF16)
    grad_got = lax.ppermute(grad_out, "c", SWAP)
    query, hid_rows = lax.optimization_barrier((query, hid_rows))

    pay, outv, dq = attention(tile_image, whole, w_key, w_value, query, dout)
    got = lax.all_to_all(pay, TILE_AXES, 0, 0, tiled=True)

    dq_got = lax.ppermute(dq, "c", SWAP)
    out_got = lax.ppermute(outv, "c", SWAP)
    dh = dot(dq, w_query, 1, 1)
    gain_part = jnp.sum(dh * normed, axis=0, keepdims=True)
    gain_part = gain_part + lax.ppermute(gain_part, "c", SWAP)
    gain_part = gain_part + lax.ppermute(gain_part, "yl", SWAP)
    gain_high = lax.reduce_precision(gain_part, 8, 7)
    gains = jnp.concatenate([gain_high, gain_part - gain_high], axis=1)
    send = weight_parts(
        want, hid_rows, outv, out_got, dq, dq_got, grad_out, grad_got, gains
    )
    dn = dh * gain
    grad_tiles = (rstd * (dn - normed * jnp.mean(dn * normed, axis=-1, keepdims=True))).astype(BF16)

    got, send = lax.optimization_barrier((got, send))
    mine, theirs, tok = image_sums(core[None], got, whole)
    send = fill_rest(send, mine, lax.ppermute(theirs, "c", SWAP), tok, gains)
    recv = lax.all_to_all(send, TILE_AXES, 0, 0, tiled=True)
    recv, grad_tiles = lax.optimization_barrier((recv, grad_tiles))
    keep, give, grad_gain = group_sums(yl[None], recv)
    got = lax.ppermute(give, "yl", SWAP)
    grad_guide = guide_grad(recv, w_key, w_value).reshape(guide.shape)
    grad_weights = keep + got
    return (grad_tiles, grad_guide, grad_weights.transpose(1, 0, 2), grad_gain.reshape(D))


def solution(mesh):
    fine = Mesh(mesh.devices.reshape(2, 2, 4, 2, 4), ("yl", "c", "x", "yh", "z"))
    every = ("yl", "c", "x", "yh", "z")
    return jax.shard_map(
        on_device,
        mesh=fine,
        in_specs=(
            P(every, None),
            P(every),
            P(("yl", "c"), TILE_AXES, None),
            P(),
            P(),
            P(),
            P(),
            P(),
            P(every, None),
        ),
        out_specs=(
            P(every, None),
            P(("yl", "c"), TILE_AXES, None),
            P(None, every, None),
            P(),
        ),
        check_vma=False,
    )
```
